32 devices in a mesh: gx: 2 (over y), gy: 4 (over x, core), gz: 4 (over z).
Axes of the slice: x: 2, y: 2, z: 4, core: 2. Of those that a mesh axis runs over, the one named last changes fastest.
Arguments:
- final_adjoint: float32 [19, 16, 32, 512], P(None, 'gx', 'gy', 'gz'), may hold values from -16 to 16
- stored_states: float32 [2, 19, 16, 32, 512], P(None, None, 'gx', 'gy', 'gz'), may hold values from 0.01 to 0.1
- porosity: float32 [16, 32, 512], P('gx', 'gy', 'gz'), may hold values from 0.2 to 1
- solid_labels: int32 [16, 32, 512], P('gx', 'gy', 'gz'), may hold values 0 or 1
- boundary_mask: int32 [16, 32, 512], P('gx', 'gy', 'gz'), may hold values 0 or 1
Outputs:
- initial_adjoint: float32 [19, 16, 32, 512], P(None, 'gx', 'gy', 'gz')
- descent_direction: float32 [16, 32, 512], P('gx', 'gy', 'gz')
- grad_norms: float32 [2], replicated
The draws below stay inside these ranges and needn't reach their ends.
All inputs are finite; a program needn't handle non-finite values. No bound on the sum of `solid_labels` or of `boundary_mask` on one device may be relied on, other than what follows from the above.
Results may differ from the reference program's by a relative error of at most 0.0003.
Values sent between devices are 32-bit elements; how exact they have to be, the bound alone decides.
No kernel may reach another device: no remote copies, remote signals or barrier semaphores. Data moves between devices by JAX's collectives and lax.ppermute only.
A program may use at most 64 MiB of HBM per device.

```python
import jax
import jax.numpy as jnp
from jax import lax

NX = 16
NY = 32
NZ = 512


def draw_final_adjoint(key, part):
    ramp = 1.0 + 2.0 * jnp.arange(NX, dtype=jnp.float32) / (NX - 1)
    base = jnp.clip(jax.random.normal(key, (19, NX, NY, NZ), jnp.float32), -4.0, 4.0)
    return base * ramp[None, :, None, None]


def touch_ends(values, rng, least, top_value):
    dims = values.shape
    place = [jax.random.randint(jax.random.fold_in(rng, axis), (), 0, dims[axis]) for axis in range(len(dims))]
    values = values.at[tuple(place)].set(least)
    longest = dims.index(max(dims))
    place[longest] = (place[longest] + 1) % dims[longest]
    return values.at[tuple(place)].set(top_value)


def steps_of(key, dims, cuts, least, top_value):
    level, own = 1.0, jax.random.fold_in(key, 6)
    for dim, parts in cuts:
        steps = jnp.exp(jax.random.uniform(jax.random.fold_in(own, dim), (parts,), jnp.float32, least / len(cuts), top_value / len(cuts)))
        level = level * jnp.repeat(steps, dims[dim] // parts).reshape([-1 if axis == dim else 1 for axis in range(len(dims))])
    return level


def setup_inputs(seed: int = 0) -> dict:
    key_of = jax.random.split(jax.random.key(seed), 6)
    final_adjoint = draw_final_adjoint(jax.random.fold_in(key_of[5], 71), 0)
    stored_states = jnp.clip(0.01 + 0.09 * jax.random.uniform(key_of[1], (2, 19, NX, NY, NZ), jnp.float32) ** steps_of(key_of[1], (2, 19, NX, NY, NZ), ((2, 2), (3, 4), (4, 4)), -0.2, 0.2), 0.01, 0.1)
    porosity = jnp.clip(0.2 + 0.8 * jax.random.uniform(key_of[2], (NX, NY, NZ), jnp.float32) ** steps_of(key_of[2], (NX, NY, NZ), ((0, 2), (1, 4), (2, 4)), -0.2, 0.2), 0.2, 1.0)
    solid_labels = touch_ends((jax.random.randint(key_of[3], (NX, NY, NZ), 0, 5) < 1).astype(jnp.int32), jax.random.fold_in(key_of[3], 1), 0, 1)
    boundary_mask = touch_ends((jax.random.randint(key_of[4], (NX, NY, NZ), 0, 10) < 1).astype(jnp.int32), jax.random.fold_in(key_of[4], 1), 0, 1)
    return dict(final_adjoint=final_adjoint, stored_states=stored_states, porosity=porosity, solid_labels=solid_labels, boundary_mask=boundary_mask)


lattice = ((0, 0, 0), (1, 0, 0), (-1, 0, 0), (0, 1, 0), (0, -1, 0), (0, 0, 1), (0, 0, -1), (1, 1, 0), (-1, -1, 0), (1, -1, 0), (-1, 1, 0), (1, 0, 1), (-1, 0, -1), (1, 0, -1), (-1, 0, 1), (0, 1, 1), (0, -1, -1), (0, 1, -1), (0, -1, 1))
opposite = (0, 2, 1, 4, 3, 6, 5, 8, 7, 10, 9, 12, 11, 14, 13, 16, 15, 18, 17)

def moment_row(order, vector):
    xval, yval, zval = (float(vector[0]), float(vector[1]), float(vector[2]))
    entries = (1.0, xval, yval, zval, xval * yval, xval * zval, yval * zval, xval * xval, yval * yval, zval * zval, xval * xval * yval, xval * xval * zval, xval * yval * yval, yval * yval * zval, xval * zval * zval, yval * zval * zval, xval * xval * yval * yval, xval * xval * zval * zval, yval * yval * zval * zval)
    return entries[order]

def invert_small(matrix):
    count = len(matrix)
    work = [list(matrix[row]) + [1.0 if row == col else 0.0 for col in range(count)] for row in range(count)]
    for column in range(count):
        pivot = column
        for row in range(column + 1, count):
            if abs(work[row][column]) > abs(work[pivot][column]):
                pivot = row
        work[column], work[pivot] = (work[pivot], work[column])
        scale = 1.0 / work[column][column]
        work[column] = [value * scale for value in work[column]]
        for row in range(count):
            if row != column:
                factor = work[row][column]
                if factor != 0.0:
                    work[row] = [value - factor * other for value, other in zip(work[row], work[column])]
    return [row[count:] for row in work]

def tables():
    moments = [[moment_row(order, vector) for vector in lattice] for order in range(19)]
    rates = [0.0] * 4 + [1.2] * 6 + [1.4] * 6 + [1.6] * 3
    inverse = invert_small(moments)
    relax = [[sum((inverse[row][mid] * rates[mid] * moments[mid][col] for mid in range(19))) for col in range(19)] for row in range(19)]
    weights = [1.0 / 3.0] + [1.0 / 18.0] * 6 + [1.0 / 36.0] * 12
    vectors = [[float(entry) for entry in vector] for vector in lattice]
    return (vectors, weights, relax)

def collide(stored, gamma, solid):
    vectors, weights, relax = tables()
    highest = lax.Precision.HIGHEST
    lattice_f = jnp.asarray(vectors, jnp.float32)
    weights_col = jnp.asarray(weights, jnp.float32)[:, None]
    relax_f = jnp.asarray(relax, jnp.float32)
    density = lax.optimization_barrier(jnp.sum(stored, axis=0))
    momentum = jnp.dot(lattice_f.T, stored, precision=highest)
    damping = 0.5 * (1.0 - gamma)
    velocity = momentum / (density * (1.0 + 0.5 * damping))
    force = -damping * density * velocity
    project = jnp.dot(lattice_f, velocity, precision=highest)
    speed_sq = lax.optimization_barrier(jnp.sum(velocity * velocity, axis=0))
    equil = weights_col * density * (1.0 + 3.0 * project + 4.5 * project * project - 1.5 * speed_sq)
    post = stored - jnp.dot(relax_f, stored - equil, precision=highest)
    post = post + 3.0 * weights_col * jnp.dot(lattice_f, force, precision=highest)
    bounced = jnp.stack([stored[member] for member in opposite])
    return jnp.where(solid[None, :] > 0, bounced, post)

def plane_adjoint(pieces):
    stored, pulled, gamma, solid = pieces
    layout = stored.shape

    def collision(values, porous):
        return collide(values, porous, solid.reshape(-1))
    _, pullback = jax.vjp(collision, stored.reshape(19, -1), gamma.reshape(-1))
    adjoint, gradient = pullback(pulled.reshape(19, -1))
    return (adjoint.reshape(layout), gradient.reshape(layout[1:]))

def reverse_step(adjoint, stored, porosity, solid_labels, boundary_mask):
    masked = adjoint * (1 - boundary_mask).astype(jnp.float32)[None]
    pulled = jnp.stack([jnp.roll(masked[member], (-lattice[member][0], -lattice[member][1], -lattice[member][2]), axis=(0, 1, 2)) for member in range(19)])
    adjoint_new, gradient = lax.map(plane_adjoint, (jnp.moveaxis(stored, 1, 0), jnp.moveaxis(pulled, 1, 0), porosity, solid_labels))
    return (jnp.moveaxis(adjoint_new, 0, 1), gradient)

def reference(final_adjoint, stored_states, porosity, solid_labels, boundary_mask):
    adjoint_one, gradient_one = reverse_step(final_adjoint, stored_states[1], porosity, solid_labels, boundary_mask)
    initial_adjoint, gradient_zero = reverse_step(adjoint_one, stored_states[0], porosity, solid_labels, boundary_mask)
    overall = gradient_one + gradient_zero
    first_norm = jnp.sqrt(jnp.mean(gradient_one * gradient_one) + 1e-06)
    second_norm = jnp.sqrt(jnp.mean(overall * overall) + 1e-06)
    return (initial_adjoint, overall / second_norm, jnp.stack([first_norm, second_norm]))
```

```python
import jax
import jax.numpy as jnp
from jax import lax
from jax.sharding import PartitionSpec as P

lattice = (
    (0, 0, 0),
    (1, 0, 0),
    (-1, 0, 0),
    (0, 1, 0),
    (0, -1, 0),
    (0, 0, 1),
    (0, 0, -1),
    (1, 1, 0),
    (-1, -1, 0),
    (1, -1, 0),
    (-1, 1, 0),
    (1, 0, 1),
    (-1, 0, -1),
    (1, 0, -1),
    (-1, 0, 1),
    (0, 1, 1),
    (0, -1, -1),
    (0, 1, -1),
    (0, -1, 1),
)
opposite = (0, 2, 1, 4, 3, 6, 5, 8, 7, 10, 9, 12, 11, 14, 13, 16, 15, 18, 17)
AXES = ("gx", "gy", "gz")
PLANES = ((0, 1, 7), (0, 2, 11), (1, 2, 15))


def flow(stored, porosity):
    density = sum(stored[1:], stored[0])
    momentum = []
    for axis in range(3):
        total = None
        for vector, value in zip(lattice, stored):
            if vector[axis]:
                if total is None:
                    total = value if vector[axis] > 0 else -value
                else:
                    total = total + value if vector[axis] > 0 else total - value
        momentum.append(total)
    damping = 0.5 * (1.0 - porosity)
    beta = 1.0 / (1.0 + 0.5 * damping)
    scale = beta / density
    return density, [value * scale for value in momentum], beta, damping * beta


def transpose_collision(b, velocity, beta, alpha, solid, density=None):
    base = b[0]
    first, second = [], []
    for axis in range(3):
        ahead, behind = b[2 * axis + 1], b[2 * axis + 2]
        first.append(0.5 * (ahead - behind))
        second.append(0.5 * (ahead + behind) - base)
    odd = [None, None, None]
    tee = [None, None, None]
    ring = [None, None, None]
    evens, crosses, parts = [], [], []

    def join(where, axis, value):
        where[axis] = value if where[axis] is None else where[axis] + value

    for one, two, at in PLANES:
        pp, mm, pm, mp = b[at], b[at + 1], b[at + 2], b[at + 3]
        s1, s2, d1, d2 = pp + mm, pm + mp, pp - mm, pm - mp
        both = second[one] + second[two]
        fourth = 0.25 * (s1 + s2) - base - both
        along_one, along_two = 0.25 * (d1 + d2), 0.25 * (d1 - d2)
        even = 1.2 * both + 1.6 * fourth
        cross = 0.3 * (s1 - s2)
        q_one, q_two = 1.4 * (along_one - first[one]), 1.4 * (along_two - first[two])
        join(odd, one, q_one)
        join(odd, two, q_two)
        join(tee, one, along_one)
        join(tee, two, along_two)
        join(ring, one, even)
        join(ring, two, even)
        evens.append(even)
        crosses.append(cross)
        parts.append((q_one, q_two))
    ninth = 1.0 / 9.0
    axial = 2.4 / 18.0
    s0 = axial * (second[0] + second[1] + second[2]) + ninth * (evens[0] + evens[1] + evens[2])
    sone = [ninth * odd[axis] for axis in range(3)]
    stwo = [axial * second[axis] + ninth * ring[axis] for axis in range(3)]
    sxy, sxz, syz = (ninth * value for value in crosses)
    tees = [ninth * (first[axis] + tee[axis]) for axis in range(3)]
    ux, uy, uz = velocity
    wx = stwo[0] * ux + sxy * uy + sxz * uz
    wy = sxy * ux + stwo[1] * uy + syz * uz
    wz = sxz * ux + syz * uy + stwo[2] * uz
    quad = ux * wx + uy * wy + uz * wz
    speed = ux * ux + uy * uy + uz * uz
    scalar = s0 * (1.0 + 1.5 * speed) - 4.5 * quad
    slope = [
        beta * (3.0 * one + 9.0 * two - 3.0 * s0 * three) - 3.0 * alpha * tau
        for one, two, three, tau in zip(sone, (wx, wy, wz), velocity, tees)
    ]
    out = [base + scalar]
    for axis in range(3):
        even = scalar - 1.2 * second[axis]
        out.append(b[2 * axis + 1] + (even + slope[axis]))
        out.append(b[2 * axis + 2] + (even - slope[axis]))
    for (one, two, at), even, cross, (q_one, q_two) in zip(PLANES, evens, crosses, parts):
        same, other = scalar - even - cross, scalar - even + cross
        a_one, a_two = slope[one] - q_one, slope[two] - q_two
        plus, minus = a_one + a_two, a_one - a_two
        out.append(b[at] + (same + plus))
        out.append(b[at + 1] + (same - plus))
        out.append(b[at + 2] + (other + minus))
        out.append(b[at + 3] + (other - minus))
    out = [jnp.where(solid, b[opposite[i]], out[i]) for i in range(19)]
    if density is None:
        return out, None
    gradient = (beta * density) * (
        0.75 * (sone[0] * ux + sone[1] * uy + sone[2] * uz)
        + 2.25 * quad
        - 0.75 * s0 * speed
        + 1.5 * (tees[0] * ux + tees[1] * uy + tees[2] * uz)
    )
    return out, jnp.where(solid, 0.0, gradient)


def extended(cells, axis, dim, width):
    count = lax.axis_size(axis)
    size = cells.shape[dim]
    head = lax.slice_in_dim(cells, 0, width, axis=dim)
    tail = lax.slice_in_dim(cells, size - width, size, axis=dim)
    if count == 2:
        both = lax.ppermute(jnp.concatenate([tail, head], axis=dim), axis, [(0, 1), (1, 0)])
        low = lax.slice_in_dim(both, 0, width, axis=dim)
        high = lax.slice_in_dim(both, width, 2 * width, axis=dim)
    else:
        low = lax.ppermute(tail, axis, [(i, (i + 1) % count) for i in range(count)])
        high = lax.ppermute(head, axis, [((i + 1) % count, i) for i in range(count)])
    return jnp.concatenate([low, cells, high], axis=dim)


def pulled(cells, width):
    sizes = [n - 2 * width for n in cells[0].shape]
    out = []
    for vector, value in zip(lattice, cells):
        window = tuple(slice(width + c, width + c + n) for c, n in zip(vector, sizes))
        out.append(value[window])
    return out


def shards(final_adjoint, stored_states, porosity, solid_labels, boundary_mask):
    counts = [lax.axis_size(axis) for axis in AXES]
    devices = counts[0] * counts[1] * counts[2]
    cell_count = porosity.size * devices
    free = (1 - boundary_mask).astype(jnp.float32)
    density_one, velocity_one, beta, alpha = flow([stored_states[1, i] for i in range(19)], porosity)
    density_zero, velocity_zero, _, _ = flow([stored_states[0, i] for i in range(19)], porosity)
    solid = solid_labels.astype(jnp.float32)
    block = jnp.concatenate(
        [final_adjoint * free[None], jnp.stack([*velocity_one, porosity, solid, free])], axis=0
    )
    for axis, dim in (("gy", 2), ("gx", 1), ("gz", 3)):
        block = extended(block, axis, dim, 2)
    masked = [block[i] for i in range(19)]
    near = block[19:, 1:-1, 1:-1, 1:-1]
    damping = 0.5 * (1.0 - near[3])
    beta_near = 1.0 / (1.0 + 0.5 * damping)
    adjoint_one, _ = transpose_collision(
        pulled(masked, 1), [near[0], near[1], near[2]], beta_near, damping * beta_near, near[4] > 0.0
    )
    masked_one = [value * near[5] for value in adjoint_one]
    inner = [value[1:-1, 1:-1, 1:-1] for value in pulled(masked, 1)]
    wall = solid_labels > 0
    _, gradient_one = transpose_collision(inner, velocity_one, beta, alpha, wall, density_one)
    initial, gradient_zero = transpose_collision(
        pulled(masked_one, 1), velocity_zero, beta, alpha, wall, density_zero
    )
    overall = gradient_one + gradient_zero
    sums = jnp.stack([jnp.sum(gradient_one * gradient_one), jnp.sum(overall * overall)])
    row = jnp.broadcast_to(jnp.pad(sums, (0, 126))[None, None, :], (devices, 1, 128))
    totals = jnp.sum(lax.all_to_all(row, AXES, 0, 0, tiled=True), axis=0)[0, :2]
    norms = jnp.sqrt(totals / cell_count + 1e-06)
    return jnp.stack(initial), overall / norms[1], norms


def solution(mesh):
    in_specs = (
        P(None, "gx", "gy", "gz"),
        P(None, None, "gx", "gy", "gz"),
        P("gx", "gy", "gz"),
        P("gx", "gy", "gz"),
        P("gx", "gy", "gz"),
    )
    out_specs = (P(None, "gx", "gy", "gz"), P("gx", "gy", "gz"), P())
    return jax.shard_map(shards, mesh=mesh, in_specs=in_specs, out_specs=out_specs, check_vma=False)
```

```python
import functools

import jax
import jax.numpy as jnp
from jax import lax
from jax.experimental import pallas as pl
from jax.experimental.pallas import tpu as pltpu
from jax.sharding import PartitionSpec as P

lattice = (
    (0, 0, 0),
    (1, 0, 0),
    (-1, 0, 0),
    (0, 1, 0),
    (0, -1, 0),
    (0, 0, 1),
    (0, 0, -1),
    (1, 1, 0),
    (-1, -1, 0),
    (1, -1, 0),
    (-1, 1, 0),
    (1, 0, 1),
    (-1, 0, -1),
    (1, 0, -1),
    (-1, 0, 1),
    (0, 1, 1),
    (0, -1, -1),
    (0, 1, -1),
    (0, -1, 1),
)
opposite = (0, 2, 1, 4, 3, 6, 5, 8, 7, 10, 9, 12, 11, 14, 13, 16, 15, 18, 17)
AXES = ("gx", "gy", "gz")
PLANES = ((0, 1, 7), (0, 2, 11), (1, 2, 15))


def flow(stored, porosity):
    density = sum(stored[1:], stored[0])
    momentum = []
    for axis in range(3):
        total = None
        for vector, value in zip(lattice, stored):
            if vector[axis]:
                if total is None:
                    total = value if vector[axis] > 0 else -value
                else:
                    total = total + value if vector[axis] > 0 else total - value
        momentum.append(total)
    damping = 0.5 * (1.0 - porosity)
    beta = 1.0 / (1.0 + 0.5 * damping)
    scale = beta / density
    return density, [value * scale for value in momentum], beta, damping * beta


def transpose_collision(b, velocity, beta, alpha, solid, density=None):
    base = b[0]
    first, second = [], []
    for axis in range(3):
        ahead, behind = b[2 * axis + 1], b[2 * axis + 2]
        first.append(0.5 * (ahead - behind))
        second.append(0.5 * (ahead + behind) - base)
    odd = [None, None, None]
    tee = [None, None, None]
    ring = [None, None, None]
    evens, crosses, parts = [], [], []

    def join(where, axis, value):
        where[axis] = value if where[axis] is None else where[axis] + value

    for one, two, at in PLANES:
        pp, mm, pm, mp = b[at], b[at + 1], b[at + 2], b[at + 3]
        s1, s2, d1, d2 = pp + mm, pm + mp, pp - mm, pm - mp
        both = second[one] + second[two]
        fourth = 0.25 * (s1 + s2) - base - both
        along_one, along_two = 0.25 * (d1 + d2), 0.25 * (d1 - d2)
        even = 1.2 * both + 1.6 * fourth
        cross = 0.3 * (s1 - s2)
        q_one, q_two = 1.4 * (along_one - first[one]), 1.4 * (along_two - first[two])
        join(odd, one, q_one)
        join(odd, two, q_two)
        join(tee, one, along_one)
        join(tee, two, along_two)
        join(ring, one, even)
        join(ring, two, even)
        evens.append(even)
        crosses.append(cross)
        parts.append((q_one, q_two))
    ninth = 1.0 / 9.0
    axial = 2.4 / 18.0
    s0 = axial * (second[0] + second[1] + second[2]) + ninth * (evens[0] + evens[1] + evens[2])
    sone = [ninth * odd[axis] for axis in range(3)]
    stwo = [axial * second[axis] + ninth * ring[axis] for axis in range(3)]
    sxy, sxz, syz = (ninth * value for value in crosses)
    tees = [ninth * (first[axis] + tee[axis]) for axis in range(3)]
    ux, uy, uz = velocity
    wx = stwo[0] * ux + sxy * uy + sxz * uz
    wy = sxy * ux + stwo[1] * uy + syz * uz
    wz = sxz * ux + syz * uy + stwo[2] * uz
    quad = ux * wx + uy * wy + uz * wz
    speed = ux * ux + uy * uy + uz * uz
    scalar = s0 * (1.0 + 1.5 * speed) - 4.5 * quad
    slope = [
        beta * (3.0 * one + 9.0 * two - 3.0 * s0 * three) - 3.0 * alpha * tau
        for one, two, three, tau in zip(sone, (wx, wy, wz), velocity, tees)
    ]
    out = [base + scalar]
    for axis in range(3):
        even = scalar - 1.2 * second[axis]
        out.append(b[2 * axis + 1] + (even + slope[axis]))
        out.append(b[2 * axis + 2] + (even - slope[axis]))
    for (one, two, at), even, cross, (q_one, q_two) in zip(PLANES, evens, crosses, parts):
        same, other = scalar - even - cross, scalar - even + cross
        a_one, a_two = slope[one] - q_one, slope[two] - q_two
        plus, minus = a_one + a_two, a_one - a_two
        out.append(b[at] + (same + plus))
        out.append(b[at + 1] + (same - plus))
        out.append(b[at + 2] + (other + minus))
        out.append(b[at + 3] + (other - minus))
    out = [jnp.where(solid, b[opposite[i]], out[i]) for i in range(19)]
    if density is None:
        return out, None
    gradient = (beta * density) * (
        0.75 * (sone[0] * ux + sone[1] * uy + sone[2] * uz)
        + 2.25 * quad
        - 0.75 * s0 * speed
        + 1.5 * (tees[0] * ux + tees[1] * uy + tees[2] * uz)
    )
    return out, jnp.where(solid, 0.0, gradient)


def face_rows(axis, side):
    near = [(k, 1) for k in range(19) if lattice[k][axis] * side >= 0]
    far = [(k, 2) for k in range(19) if lattice[k][axis] * side > 0]
    return near + far


def edge_rows(side_x, side_y):
    rows = []
    for k in range(19):
        across, along = lattice[k][0] * side_x, lattice[k][1] * side_y
        for layer_x in (1, 2):
            for layer_y in (1, 2):
                fits = across >= layer_x - 1 and along >= layer_y - 1
                if fits:
                    rows.append((k, layer_x, layer_y))
    return rows


NEAR = 19
FACE = 25
UP = [k for k in range(19) if lattice[k][2] > 0]
DOWN = [k for k in range(19) if lattice[k][2] < 0]
TALL = 16
WIDE = 12
PLANE = TALL * WIDE
SIDES = (1, -1)
PLACE = {(axis, side): {row: i for i, row in enumerate(face_rows(axis, side))} for axis in range(3) for side in SIDES}
YROWS = FACE * 8 + 16
XROWS = FACE * 8
EROWS = 72


def lanes_of(shape):
    return lax.broadcasted_iota(jnp.int32, shape, len(shape) - 1)


def turn(value, shift):
    count = value.shape[-1]
    shift = shift % count
    return pltpu.roll(value, shift, value.ndim - 1) if shift else value


def pick(flag, one, two):
    return jnp.where(flag, one, two)


def even_of(axis):
    return lax.axis_index(axis) % 2 == 0


def weave_y(own, high, low):
    place = lanes_of(own.shape) % TALL
    return jnp.where(place < 4, turn(low, -8), jnp.where(place < 12, own, turn(high, 8)))


def weave_x(own, high, low):
    lane = lanes_of(own.shape)
    own = turn(own, 32)
    return jnp.where(lane < 32, turn(low, 32), own), jnp.where(lane < 32, own, turn(high, 32))


def pack_kernel(adj, st, por, sol, msk, za, zb, ya, yb, xm, cen, flw, cells, cols, *, nx):
    lane = lanes_of((8, 128))
    cols[...] = jnp.zeros_like(cols)

    def step(x, carry):
        at = pl.ds(pl.multiple_of(x * 8, 8), 8)
        free = 1.0 - msk[at, :].astype(jnp.float32)
        _, velocity, _, _ = flow([st[k, at, :] for k in range(19)], por[at, :])
        tiles = [adj[k, at, :] * free for k in range(19)]
        tiles += [*velocity, por[at, :], sol[at, :].astype(jnp.float32), free]
        for k in range(FACE):
            cells[k, at, :] = tiles[k]
        for i in range(3):
            flw[i, at, :] = velocity[i]
        spread = jnp.zeros((8, 128), jnp.float32)
        for half, side in enumerate(SIDES):
            wanted = face_rows(2, side) + [(NEAR + i, 1) for i in range(6)]
            for i, (k, layer) in enumerate(wanted):
                source = layer - 1 if side > 0 else 128 - layer
                spread = jnp.where(lane == half * 32 + i, turn(tiles[k], half * 32 + i - source), spread)
        cols[x, pl.ds(4, 8), :] = spread
        return carry

    lax.fori_loop(0, 8, step, 0)
    table = jnp.transpose(cols[...].reshape(128, 128))
    low, high = table[0:32], table[32:64]
    even = even_of("gz")
    za[...] = pick(even, high, low)
    zb[...] = pick(even, low, high)
    cols[0] = jnp.zeros((TALL, 128), jnp.float32)
    center = []
    for base, side, pops in ((32, -1, DOWN), (0, 1, UP)):
        for i, k in enumerate(pops):
            row = base + PLACE[2, side][k, 1]
            center.append(((base == 0) * 8 + i, table[row : row + 1]))
    for row, value in center:
        cols[0, row : row + 1, :] = value
    cen[...] = cols[0]
    even = even_of("gy")
    for i in range(FACE):
        pair = []
        for side in SIDES:
            k, layer = (face_rows(1, side) + [(NEAR + j, 1) for j in range(6)])[i]
            y = layer - 1 if side > 0 else 8 - layer
            pair.append(cells[k, pl.ds(y, 8, stride=8), :])
        low, high = pair
        ya[i * 8 : i * 8 + 8, :] = pick(even, high, low)
        yb[i * 8 : i * 8 + 8, :] = pick(even, low, high)
    ya[FACE * 8 :, :] = cols[0]
    yb[FACE * 8 :, :] = cols[0]
    even = even_of("gx")
    for i in range(FACE):
        pair = []
        for side in SIDES:
            k, layer = (face_rows(0, side) + [(NEAR + j, 1) for j in range(6)])[i]
            x = layer - 1 if side > 0 else 8 - layer
            pair.append(cells[k, x * 8 : x * 8 + 8, :])
        low, high = pair
        if nx > 2:
            low, high = pick(even, high, low), pick(even, low, high)
        xm[0, i * 8 : i * 8 + 8, :] = low
        xm[1, i * 8 : i * 8 + 8, :] = high


def edge_kernel(ya, yb, cen, out, full, *, nx):
    even = even_of("gy")
    a, b = ya[...], yb[...]
    high, low = pick(even, a, b), pick(even, b, a)
    center = weave_y(cen[...], high[FACE * 8 :], low[FACE * 8 :])
    full[...] = center
    even = even_of("gx")
    out[...] = jnp.zeros_like(out)
    for i in range(NEAR + 6):
        for where, side_y, source in ((0, 1, high), (FACE, -1, low)):
            pair = []
            for side_x in SIDES:
                rows = edge_rows(side_x, side_y) + [(NEAR + j, 1, 1) for j in range(6)]
                k, layer_x, layer_y = rows[i]
                row = PLACE[1, side_y][k, layer_y] if k < NEAR else k
                x = layer_x - 1 if side_x > 0 else 8 - layer_x
                pair.append(source[row * 8 + x : row * 8 + x + 1])
            one, two = pair
            if nx > 2:
                one, two = pick(even, two, one), pick(even, one, two)
            out[0, where + i : where + i + 1, :] = one
            out[1, where + i : where + i + 1, :] = two
    out[0, 56:, :] = center
    out[1, 56:, :] = center


def ghost_kernel(za, zb, ga, gb, out):
    even = even_of("gy")
    for half, ref in enumerate((za, zb)):
        at = slice(half * 32, half * 32 + 32)
        a, b = ga[at, :], gb[at, :]
        out[at, :] = weave_y(ref[...], pick(even, a, b), pick(even, b, a))


def main_kernel(adj, st, por, sol, msk, flw, ya, yb, xm, edges, full, own, far, init, over, sums,
                m0, aux, m1, ghosts, table, rho, *, nx):
    lane = lanes_of((8, 128))
    even_x, even_y, even_z = even_of("gx"), even_of("gy"), even_of("gz")

    def along_x(ref):
        a, b = ref[0], ref[1]
        if nx == 2:
            return a, b
        return pick(even_x, a, b), pick(even_x, b, a)

    def fill(x, carry):
        at = pl.ds(pl.multiple_of(x * 8, 8), 8)
        free = 1.0 - msk[at, :].astype(jnp.float32)
        for k in range(19):
            m0[k * WIDE + x + 2, pl.ds(4, 8), :] = adj[k, at, :] * free
        extra = [flw[i, at, :] for i in range(3)] + [por[at, :], sol[at, :].astype(jnp.float32), free]
        for i, value in enumerate(extra):
            aux[i * WIDE + x + 2, pl.ds(4, 8), :] = value
        return carry

    lax.fori_loop(0, 8, fill, 0)
    flat0, flat1, flat_aux = (ref.reshape(ref.shape[0] * TALL, 128) for ref in (m0, m1, aux))
    flat_table = table
    for side, tiles in zip(SIDES, along_x(xm)):
        for i, (k, layer) in enumerate(face_rows(0, side)):
            x = 9 + layer if side > 0 else 2 - layer
            m0[k * WIDE + x, pl.ds(4, 8), :] = tiles[i * 8 : i * 8 + 8]
        for i in range(6):
            at = (NEAR + i) * 8
            aux[i * WIDE + (10 if side > 0 else 1), pl.ds(4, 8), :] = tiles[at : at + 8]
    a, b = ya[...], yb[...]
    for side, tiles in ((1, pick(even_y, a, b)), (-1, pick(even_y, b, a))):
        for i, (k, layer) in enumerate(face_rows(1, side)):
            y = 11 + layer if side > 0 else 4 - layer
            flat0[pl.ds(k * PLANE + 2 * TALL + y, 8, stride=TALL), :] = tiles[i * 8 : i * 8 + 8]
        for i in range(6):
            at = (NEAR + i) * 8
            y = 12 if side > 0 else 3
            flat_aux[pl.ds(i * PLANE + 2 * TALL + y, 8, stride=TALL), :] = tiles[at : at + 8]
    pairs = along_x(edges)
    for side_x, lines in zip(SIDES, pairs):
        for where, side_y in ((0, 1), (FACE, -1)):
            for i, (k, layer_x, layer_y) in enumerate(edge_rows(side_x, side_y)):
                x = 9 + layer_x if side_x > 0 else 2 - layer_x
                y = 11 + layer_y if side_y > 0 else 4 - layer_y
                m0[k * WIDE + x, y : y + 1, :] = lines[where + i : where + i + 1]
            for i in range(6):
                x, y = (10 if side_x > 0 else 1), (12 if side_y > 0 else 3)
                at = where + NEAR + i
                aux[i * WIDE + x, y : y + 1, :] = lines[at : at + 1]
    if nx == 2:
        high, low = far[0], far[0]
    else:
        high, low = along_x(far)
    for tile, value in enumerate(weave_x(own[...], high, low)):
        a, b = value[0:32], value[32:64]
        ghosts[0:32, tile * 128 : tile * 128 + 128] = pick(even_z, a, b)
        ghosts[32:64, tile * 128 : tile * 128 + 128] = pick(even_z, b, a)
    ghosts[64:128, :] = jnp.zeros((64, 256), jnp.float32)
    for tile in range(2):
        at = slice(tile * 128, tile * 128 + 128)
        table[at, :] = jnp.transpose(ghosts[:, at])
    center = jnp.concatenate(weave_x(full[...], pairs[0][56:], pairs[1][56:]), axis=1)

    for half, side in enumerate(SIDES):
        place = PLACE[2, side]
        b = []
        for k in range(19):
            cx, cy, cz = lattice[k]
            if cz * side < 0:
                row = half * 8 + (DOWN if side > 0 else UP).index(k)
                value = center[row : row + 1]
            else:
                row = half * 32 + place[k, 2 if cz else 1]
                value = ghosts[row : row + 1, :]
            b.append(turn(value, -(TALL * cx + cy)))
        base = half * 32 + NEAR
        extra = [ghosts[base + i : base + i + 1, :] for i in range(6)]
        damping = 0.5 * (1.0 - extra[3])
        beta = 1.0 / (1.0 + 0.5 * damping)
        result, _ = transpose_collision(b, extra[:3], beta, damping * beta, extra[4] > 0.0)
        for i, k in enumerate(UP if side > 0 else DOWN):
            row = 64 + half * 8 + i
            ghosts[row : row + 1, :] = result[k] * extra[5]

    def shifted(value, ghost, k, column):
        if lattice[k][2] > 0:
            return jnp.where(lane == 127, turn(ghost, 127 - column), turn(value, -1))
        return jnp.where(lane == 0, turn(ghost, -column), turn(value, 1))

    first_column = {k: PLACE[2, 1][k, 1] for k in UP}
    first_column.update({k: 32 + PLACE[2, -1][k, 1] for k in DOWN})
    second_column = {k: 64 + i for i, k in enumerate(UP)}
    second_column.update({k: 72 + i for i, k in enumerate(DOWN)})

    def own_b(ref, columns, x):
        out = []
        for k in range(19):
            cx, cy, cz = lattice[k]
            value = ref[k * WIDE + x + cx, pl.ds(4 + cy, 8), :]
            if cz:
                ghost = table3[x + cx, pl.ds(4 + cy, 8), :]
                value = shifted(value, ghost, k, columns[k])
            out.append(value)
        return out

    table3 = table.reshape(TALL, TALL, 128)

    def first(x, carry):
        x = x + 1
        b = own_b(m0, first_column, x)
        extra = [aux[i * WIDE + x, pl.ds(4, 8), :] for i in range(6)]
        damping = 0.5 * (1.0 - extra[3])
        beta = 1.0 / (1.0 + 0.5 * damping)
        result, gradient = transpose_collision(
            b, extra[:3], beta, damping * beta, extra[4] > 0.0, rho[x, :, :]
        )
        for k in range(19):
            m1[k * WIDE + x, pl.ds(4, 8), :] = result[k] * extra[5]
        rho[x, :, :] = gradient
        return carry

    def density(x, carry):
        at = pl.ds(pl.multiple_of(x * 8, 8), 8)
        rho[x + 2, :, :] = sum((st[19 + k, at, :] for k in range(1, 19)), st[19, at, :])
        return carry

    rho[...] = jnp.zeros_like(rho)
    lax.fori_loop(0, 8, density, 0)
    lax.fori_loop(0, 10, first, 0)
    for y in (3, 12):
        for x0 in (1, 3):
            b = []
            for k in range(19):
                cx, cy, cz = lattice[k]
                start = (x0 + cx) * TALL + y + cy
                value = flat0[pl.ds(k * PLANE + start, 8, stride=TALL), :]
                if cz:
                    ghost = flat_table[pl.ds(start, 8, stride=TALL), :]
                    value = shifted(value, ghost, k, first_column[k])
                b.append(value)
            start = x0 * TALL + y
            extra = [flat_aux[pl.ds(i * PLANE + start, 8, stride=TALL), :] for i in range(6)]
            damping = 0.5 * (1.0 - extra[3])
            beta = 1.0 / (1.0 + 0.5 * damping)
            result, _ = transpose_collision(b, extra[:3], beta, damping * beta, extra[4] > 0.0)
            for k in range(19):
                flat1[pl.ds(k * PLANE + start, 8, stride=TALL), :] = result[k] * extra[5]
    for tile in range(2):
        at = slice(tile * 128, tile * 128 + 128)
        table[at, :] = jnp.transpose(ghosts[:, at])

    def second(x, carry):
        one, two = carry
        at = pl.ds(pl.multiple_of(x * 8, 8), 8)
        b = own_b(m1, second_column, x + 2)
        dense, velocity, beta, alpha = flow([st[k, at, :] for k in range(19)], por[at, :])
        result, gradient = transpose_collision(b, velocity, beta, alpha, sol[at, :] > 0, dense)
        for k in range(19):
            init[k, at, :] = result[k]
        before = rho[x + 2, :, :]
        total = before + gradient
        over[at, :] = total
        return one + before * before, two + total * total

    zero = jnp.zeros((8, 128), jnp.float32)
    one, two = lax.fori_loop(0, 8, second, (zero, zero))
    one, two = jnp.sum(one, axis=0, keepdims=True), jnp.sum(two, axis=0, keepdims=True)
    devices = sums.shape[0]
    sums[:, 0:1, :] = jnp.broadcast_to(one[None], (devices, 1, 128))
    sums[:, 1:2, :] = jnp.broadcast_to(two[None], (devices, 1, 128))


def scale_kernel(over, sums, descent, norms, *, cell_count):
    total = jnp.sum(sums[...], axis=0)
    one, two = jnp.sum(total[0:1, :]), jnp.sum(total[1:2, :])
    norm = [jnp.sqrt(jnp.full((8, 128), value, jnp.float32) / cell_count + 1e-06) for value in (one, two)]
    descent[...] = over[...] / norm[1][0:1, 0:1]
    lane = lanes_of((8, 128))
    norms[...] = jnp.where(lane == 0, norm[0], norm[1])


def call(kernel, outs, scratch=(), **names):
    def run(*arrays):
        return pl.pallas_call(
            functools.partial(kernel, **names),
            out_shape=[jax.ShapeDtypeStruct(shape, jnp.float32) for shape in outs],
            in_specs=[pl.BlockSpec(memory_space=pltpu.VMEM)] * len(arrays),
            out_specs=[pl.BlockSpec(memory_space=pltpu.VMEM)] * len(outs),
            scratch_shapes=[pltpu.VMEM(shape, jnp.float32) for shape in scratch],
            compiler_params=pltpu.CompilerParams(vmem_limit_bytes=32 << 20),
            name=kernel.__name__,
        )(*arrays)

    return run


def swaps(axis):
    count = lax.axis_size(axis)
    ahead = [(i, (i + 1) % count if i % 2 == 0 else i - 1) for i in range(count)]
    behind = [(i, (i - 1) % count if i % 2 == 0 else (i + 1) % count) for i in range(count)]
    return ahead, behind


def both(one, two, axis):
    ahead, behind = swaps(axis)
    second = lax.ppermute(two, axis, behind)
    return lax.ppermute(one, axis, ahead), second


def two_sides(message):
    if lax.axis_size("gx") == 2:
        return lax.ppermute(message, "gx", [(0, 1), (1, 0)])
    return jnp.stack(both(message[0], message[1], "gx"))


def shards(final_adjoint, stored_states, porosity, solid_labels, boundary_mask):
    nx = lax.axis_size("gx")
    devices = nx * lax.axis_size("gy") * lax.axis_size("gz")
    cells = porosity.size
    layout = final_adjoint.shape
    adj, st = final_adjoint.reshape(19, 64, 128), stored_states.reshape(38, 64, 128)
    por, sol, msk = (v.reshape(64, 128) for v in (porosity, solid_labels, boundary_mask))
    za, zb, ya, yb, xm, cen, flw = call(
        pack_kernel,
        [(32, 128), (32, 128), (YROWS, 128), (YROWS, 128), (2, XROWS, 128), (16, 128), (3, 64, 128)],
        [(FACE, 64, 128), (8, TALL, 128)],
        nx=nx,
    )(adj, st[19:], por, sol, msk)
    za, zb = both(za, zb, "gz")
    ya, yb = both(ya, yb, "gy")
    xm = two_sides(xm)
    mine = jnp.concatenate([za, zb], axis=0)
    ga, gb = both(mine, mine, "gy")
    edges, full = call(edge_kernel, [(2, EROWS, 128), (16, 128)], nx=nx)(ya, yb, cen)
    edges = two_sides(edges)
    (own,) = call(ghost_kernel, [(64, 128)])(za, zb, ga, gb)
    if nx == 2:
        far = lax.ppermute(own, "gx", [(0, 1), (1, 0)])[None]
    else:
        far = jnp.stack(both(own, own, "gx"))
    init, over, sums = call(
        main_kernel,
        [(19, 64, 128), (64, 128), (devices, 2, 128)],
        [
            (19 * WIDE, TALL, 128),
            (6 * WIDE, TALL, 128),
            (19 * WIDE, TALL, 128),
            (128, 256),
            (256, 128),
            (WIDE, 8, 128),
        ],
        nx=nx,
    )(adj, st, por, sol, msk, flw, ya, yb, xm, edges, full, own, far)
    sums = lax.all_to_all(sums, AXES, 0, 0, tiled=True)
    descent, norms = call(scale_kernel, [(64, 128), (8, 128)], cell_count=cells * devices)(over, sums)
    return init.reshape(layout), descent.reshape(layout[1:]), norms[0, :2]


def solution(mesh):
    in_specs = (
        P(None, "gx", "gy", "gz"),
        P(None, None, "gx", "gy", "gz"),
        P("gx", "gy", "gz"),
        P("gx", "gy", "gz"),
        P("gx", "gy", "gz"),
    )
    out_specs = (P(None, "gx", "gy", "gz"), P("gx", "gy", "gz"), P())
    return jax.shard_map(shards, mesh=mesh, in_specs=in_specs, out_specs=out_specs, check_vma=False)
```

```python
import functools

import jax
import jax.numpy as jnp
from jax import lax
from jax.experimental import pallas as pl
from jax.experimental.pallas import tpu as pltpu
from jax.sharding import PartitionSpec as P

lattice = (
    (0, 0, 0),
    (1, 0, 0),
    (-1, 0, 0),
    (0, 1, 0),
    (0, -1, 0),
    (0, 0, 1),
    (0, 0, -1),
    (1, 1, 0),
    (-1, -1, 0),
    (1, -1, 0),
    (-1, 1, 0),
    (1, 0, 1),
    (-1, 0, -1),
    (1, 0, -1),
    (-1, 0, 1),
    (0, 1, 1),
    (0, -1, -1),
    (0, 1, -1),
    (0, -1, 1),
)
opposite = (0, 2, 1, 4, 3, 6, 5, 8, 7, 10, 9, 12, 11, 14, 13, 16, 15, 18, 17)
AXES = ("gx", "gy", "gz")
PLANES = ((0, 1, 7), (0, 2, 11), (1, 2, 15))


def flow(stored, porosity):
    density = sum(stored[1:], stored[0])
    momentum = []
    for axis in range(3):
        total = None
        for vector, value in zip(lattice, stored):
            if vector[axis]:
                if total is None:
                    total = value if vector[axis] > 0 else -value
                else:
                    total = total + value if vector[axis] > 0 else total - value
        momentum.append(total)
    damping = 0.5 * (1.0 - porosity)
    beta = 1.0 / (1.0 + 0.5 * damping)
    scale = beta / density
    return density, [value * scale for value in momentum], beta, damping * beta


def transpose_collision(b, velocity, beta, alpha, solid, density=None):
    base = b[0]
    first, second = [], []
    for axis in range(3):
        ahead, behind = b[2 * axis + 1], b[2 * axis + 2]
        first.append(0.5 * (ahead - behind))
        second.append(0.5 * (ahead + behind) - base)
    odd = [None, None, None]
    tee = [None, None, None]
    ring = [None, None, None]
    evens, crosses, parts = [], [], []

    def join(where, axis, value):
        where[axis] = value if where[axis] is None else where[axis] + value

    for one, two, at in PLANES:
        pp, mm, pm, mp = b[at], b[at + 1], b[at + 2], b[at + 3]
        s1, s2, d1, d2 = pp + mm, pm + mp, pp - mm, pm - mp
        both = second[one] + second[two]
        fourth = 0.25 * (s1 + s2) - base - both
        along_one, along_two = 0.25 * (d1 + d2), 0.25 * (d1 - d2)
        even = 1.2 * both + 1.6 * fourth
        cross = 0.3 * (s1 - s2)
        q_one, q_two = 1.4 * (along_one - first[one]), 1.4 * (along_two - first[two])
        join(odd, one, q_one)
        join(odd, two, q_two)
        join(tee, one, along_one)
        join(tee, two, along_two)
        join(ring, one, even)
        join(ring, two, even)
        evens.append(even)
        crosses.append(cross)
        parts.append((q_one, q_two))
    ninth = 1.0 / 9.0
    axial = 2.4 / 18.0
    s0 = axial * (second[0] + second[1] + second[2]) + ninth * (evens[0] + evens[1] + evens[2])
    sone = [ninth * odd[axis] for axis in range(3)]
    stwo = [axial * second[axis] + ninth * ring[axis] for axis in range(3)]
    sxy, sxz, syz = (ninth * value for value in crosses)
    tees = [ninth * (first[axis] + tee[axis]) for axis in range(3)]
    ux, uy, uz = velocity
    wx = stwo[0] * ux + sxy * uy + sxz * uz
    wy = sxy * ux + stwo[1] * uy + syz * uz
    wz = sxz * ux + syz * uy + stwo[2] * uz
    quad = ux * wx + uy * wy + uz * wz
    speed = ux * ux + uy * uy + uz * uz
    scalar = s0 * (1.0 + 1.5 * speed) - 4.5 * quad
    slope = [
        beta * (3.0 * one + 9.0 * two - 3.0 * s0 * three) - 3.0 * alpha * tau
        for one, two, three, tau in zip(sone, (wx, wy, wz), velocity, tees)
    ]
    out = [base + scalar]
    for axis in range(3):
        even = scalar - 1.2 * second[axis]
        out.append(b[2 * axis + 1] + (even + slope[axis]))
        out.append(b[2 * axis + 2] + (even - slope[axis]))
    for (one, two, at), even, cross, (q_one, q_two) in zip(PLANES, evens, crosses, parts):
        same, other = scalar - even - cross, scalar - even + cross
        a_one, a_two = slope[one] - q_one, slope[two] - q_two
        plus, minus = a_one + a_two, a_one - a_two
        out.append(b[at] + (same + plus))
        out.append(b[at + 1] + (same - plus))
        out.append(b[at + 2] + (other + minus))
        out.append(b[at + 3] + (other - minus))
    out = [jnp.where(solid, b[opposite[i]], out[i]) for i in range(19)]
    if density is None:
        return out, None
    gradient = (beta * density) * (
        0.75 * (sone[0] * ux + sone[1] * uy + sone[2] * uz)
        + 2.25 * quad
        - 0.75 * s0 * speed
        + 1.5 * (tees[0] * ux + tees[1] * uy + tees[2] * uz)
    )
    return out, jnp.where(solid, 0.0, gradient)


def face_rows(axis, side):
    near = [(k, 1) for k in range(19) if lattice[k][axis] * side >= 0]
    far = [(k, 2) for k in range(19) if lattice[k][axis] * side > 0]
    return near + far


def edge_rows(side_x, side_y):
    rows = []
    for k in range(19):
        across, along = lattice[k][0] * side_x, lattice[k][1] * side_y
        for layer_x in (1, 2):
            for layer_y in (1, 2):
                fits = across >= layer_x - 1 and along >= layer_y - 1
                if fits:
                    rows.append((k, layer_x, layer_y))
    return rows


NEAR = 19
FACE = 25
UP = [k for k in range(19) if lattice[k][2] > 0]
DOWN = [k for k in range(19) if lattice[k][2] < 0]
TALL = 16
WIDE = 12
PLANE = TALL * WIDE
SIDES = (1, -1)
PLACE = {(axis, side): {row: i for i, row in enumerate(face_rows(axis, side))} for axis in range(3) for side in SIDES}
YROWS = FACE * 8 + 16
XROWS = FACE * 8
EDGES = 56


def lanes_of(shape):
    return lax.broadcasted_iota(jnp.int32, shape, len(shape) - 1)


def turn(value, shift):
    count = value.shape[-1]
    shift = shift % count
    return pltpu.roll(value, shift, value.ndim - 1) if shift else value


def pick(flag, one, two):
    return jnp.where(flag, one, two)


def even_of(axis):
    return lax.axis_index(axis) % 2 == 0


def weave_y(own, high, low):
    place = lanes_of(own.shape) % TALL
    return jnp.where(place < 4, turn(low, -8), jnp.where(place < 12, own, turn(high, 8)))


def weave_x(own, high, low):
    lane = lanes_of(own.shape)
    own = turn(own, 32)
    return jnp.where(lane < 32, turn(low, 32), own), jnp.where(lane < 32, own, turn(high, 32))


def pack_kernel(adj_hbm, st_hbm, por_hbm, sol_hbm, msk_hbm, zb, za, cen, cells, rho, adj, st, por, sol, msk, cols, sems):
    copies = []
    for part in range(4):
        at = pl.ds(part * 2, 2)
        group = [
            (adj_hbm.at[:, at], adj.at[:, at]),
            (st_hbm.at[1, :, at], st.at[:, at]),
            (por_hbm.at[at], por.at[at]),
            (sol_hbm.at[at], sol.at[at]),
            (msk_hbm.at[at], msk.at[at]),
        ]
        copies.append([pltpu.make_async_copy(s, d, sems.at[part, i]) for i, (s, d) in enumerate(group)])
    for group in copies:
        for copy in group:
            copy.start()
    lane = lanes_of((8, 128))
    cols[...] = jnp.zeros_like(cols)

    def step(x, carry):
        at = pl.ds(pl.multiple_of(x * 8, 8), 8)
        free = 1.0 - msk[x].astype(jnp.float32)
        dense, velocity, _, _ = flow([st[k, x] for k in range(19)], por[x])
        rho[at, :] = dense
        tiles = [adj[k, x] * free for k in range(19)]
        tiles += [*velocity, por[x], sol[x].astype(jnp.float32), free]
        for k in range(FACE):
            cells[k, at, :] = tiles[k]
        spread = jnp.zeros((8, 128), jnp.float32)
        for half, side in enumerate(SIDES):
            wanted = face_rows(2, side) + [(NEAR + i, 1) for i in range(6)]
            for i, (k, layer) in enumerate(wanted):
                source = layer - 1 if side > 0 else 128 - layer
                spread = jnp.where(lane == half * 32 + i, turn(tiles[k], half * 32 + i - source), spread)
        cols[x, pl.ds(4, 8), :] = spread
        return carry

    for part, group in enumerate(copies):
        for copy in group:
            copy.wait()
        lax.fori_loop(part * 2, part * 2 + 2, step, 0)
    table = jnp.transpose(cols[...].reshape(128, 128))
    low, high = table[0:32], table[32:64]
    even = even_of("gz")
    za[...] = pick(even, high, low)
    zb[...] = pick(even, low, high)
    cen[...] = jnp.zeros_like(cen)
    for base, side, pops in ((32, -1, DOWN), (0, 1, UP)):
        for i, k in enumerate(pops):
            row = base + PLACE[2, side][k, 1]
            at = (base == 0) * 8 + i
            cen[at : at + 1, :] = table[row : row + 1]


def face_kernel(za, cen, cells, za_out, ya, yb, xm, *, nx):
    za_out[...] = za[...]
    even = even_of("gy")
    for i in range(FACE):
        pair = []
        for side in SIDES:
            k, layer = (face_rows(1, side) + [(NEAR + j, 1) for j in range(6)])[i]
            y = layer - 1 if side > 0 else 8 - layer
            pair.append(cells[k, pl.ds(y, 8, stride=8), :])
        low, high = pair
        ya[i * 8 : i * 8 + 8, :] = pick(even, high, low)
        yb[i * 8 : i * 8 + 8, :] = pick(even, low, high)
    ya[FACE * 8 :, :] = cen[...]
    yb[FACE * 8 :, :] = cen[...]
    even = even_of("gx")
    for i in range(FACE):
        pair = []
        for side in SIDES:
            k, layer = (face_rows(0, side) + [(NEAR + j, 1) for j in range(6)])[i]
            x = layer - 1 if side > 0 else 8 - layer
            pair.append(cells[k, x * 8 : x * 8 + 8, :])
        low, high = pair
        if nx > 2:
            low, high = pick(even, high, low), pick(even, low, high)
        xm[0, i * 8 : i * 8 + 8, :] = low
        xm[1, i * 8 : i * 8 + 8, :] = high


def relay_kernel(mine, ga, gb, ya, yb, cen, own, full, message, *, nx):
    even = even_of("gy")
    a, b = ga[...], gb[...]
    woven = weave_y(mine[...], pick(even, a, b), pick(even, b, a))
    own[...] = woven
    a, b = ya[...], yb[...]
    high, low = pick(even, a, b), pick(even, b, a)
    center = weave_y(cen[...], high[FACE * 8 :], low[FACE * 8 :])
    full[...] = center
    even = even_of("gx")
    for i in range(NEAR + 6):
        for where, side_y, source in ((0, 1, high), (FACE, -1, low)):
            pair = []
            for side_x in SIDES:
                rows = edge_rows(side_x, side_y) + [(NEAR + j, 1, 1) for j in range(6)]
                k, layer_x, layer_y = rows[i]
                row = PLACE[1, side_y][k, layer_y] if k < NEAR else k
                x = layer_x - 1 if side_x > 0 else 8 - layer_x
                pair.append(source[row * 8 + x : row * 8 + x + 1])
            one, two = pair
            if nx > 2:
                one, two = pick(even, two, one), pick(even, one, two)
            for slot, value in enumerate((one, two)):
                at = where + i
                if nx > 2:
                    message[slot, at : at + 1, :] = value
                else:
                    at += slot * EDGES
                    message[at : at + 1, :] = value
    tail = jnp.concatenate([center, woven], axis=0)
    for slot in range(2):
        blank = jnp.zeros((EDGES - 2 * FACE, 128), jnp.float32)
        if nx > 2:
            message[slot, 2 * FACE : EDGES, :] = blank
            message[slot, EDGES:, :] = tail
        else:
            message[slot * EDGES + 2 * FACE : (slot + 1) * EDGES, :] = blank
    if nx == 2:
        message[2 * EDGES :, :] = tail


def relayed(message, nx):
    if nx == 2:
        tail = message[2 * EDGES :]
        parts = [(message[slot * EDGES : (slot + 1) * EDGES], tail[:16], tail[16:]) for slot in range(2)]
    else:
        even = even_of("gx")
        a, b = message[0], message[1]
        parts = [(v[:EDGES], v[EDGES : EDGES + 16], v[EDGES + 16 :]) for v in (pick(even, a, b), pick(even, b, a))]
    return parts


def factors(extra):
    damping = 0.5 * (1.0 - extra[3])
    beta = 1.0 / (1.0 + 0.5 * damping)
    return extra[:3], beta, damping * beta, extra[4] > 0.0


FIRST = {k: PLACE[2, 1][k, 1] for k in UP}
FIRST.update({k: 32 + PLACE[2, -1][k, 1] for k in DOWN})
SECOND = {k: 64 + i for i, k in enumerate(UP)}
SECOND.update({k: 72 + i for i, k in enumerate(DOWN)})


def shifted(value, ghost, k, column):
    lane = lanes_of(value.shape)
    if lattice[k][2] > 0:
        return jnp.where(lane == 127, turn(ghost, 127 - column), turn(value, -1))
    return jnp.where(lane == 0, turn(ghost, -column), turn(value, 1))


def row_b(ref, table, columns, x, skip):
    out = []
    for k in range(19):
        cx, cy, cz = lattice[k]
        value = ref[k * WIDE + x + cx, pl.ds(4 + cy, 8), :]
        if cz:
            value = shifted(value, table[x + cx - skip, pl.ds(4 + cy, 8), :], k, columns[k])
        out.append(value)
    return out


def first_row(m0, aux, m1, rho, table, x, skip):
    extra = [aux[i * WIDE + x, pl.ds(4, 8), :] for i in range(6)]
    result, gradient = transpose_collision(row_b(m0, table, FIRST, x, skip), *factors(extra), rho[x, :, :])
    for k in range(19):
        m1[k * WIDE + x, pl.ds(4, 8), :] = result[k] * extra[5]
    rho[x, :, :] = gradient


def inner_kernel(cells, dense, st_hbm, ya, yb, xm, own, m0, aux, m1, rho, vel, dense_zero, ghosts, table, st, sem, *, nx):
    fetch = pltpu.make_async_copy(st_hbm.at[0], st, sem)
    fetch.start()
    even_y, even_z = even_of("gy"), even_of("gz")
    rho[...] = jnp.zeros_like(rho)

    def fill(x, carry):
        at = pl.ds(pl.multiple_of(x * 8, 8), 8)
        for k in range(19):
            m0[k * WIDE + x + 2, pl.ds(4, 8), :] = cells[k, at, :]
        for i in range(6):
            aux[i * WIDE + x + 2, pl.ds(4, 8), :] = cells[NEAR + i, at, :]
        rho[x + 2, :, :] = dense[at, :]
        return carry

    lax.fori_loop(0, 8, fill, 0)
    a, b = xm[0], xm[1]
    if nx > 2:
        even = even_of("gx")
        a, b = pick(even, a, b), pick(even, b, a)
    for side, tiles in zip(SIDES, (a, b)):
        for i, (k, layer) in enumerate(face_rows(0, side)):
            x = 9 + layer if side > 0 else 2 - layer
            m0[k * WIDE + x, pl.ds(4, 8), :] = tiles[i * 8 : i * 8 + 8]
        for i in range(6):
            at = (NEAR + i) * 8
            aux[i * WIDE + (10 if side > 0 else 1), pl.ds(4, 8), :] = tiles[at : at + 8]
    flat0, flat_aux = (ref.reshape(ref.shape[0] * TALL, 128) for ref in (m0, aux))
    a, b = ya[...], yb[...]
    for side, tiles in ((1, pick(even_y, a, b)), (-1, pick(even_y, b, a))):
        for i, (k, layer) in enumerate(face_rows(1, side)):
            y = 11 + layer if side > 0 else 4 - layer
            flat0[pl.ds(k * PLANE + 2 * TALL + y, 8, stride=TALL), :] = tiles[i * 8 : i * 8 + 8]
        for i in range(6):
            at = (NEAR + i) * 8
            y = 12 if side > 0 else 3
            flat_aux[pl.ds(i * PLANE + 2 * TALL + y, 8, stride=TALL), :] = tiles[at : at + 8]
    b, a = own[0:32, :], own[32:64, :]
    ghosts[0:32, :] = pick(even_z, a, b)
    ghosts[32:64, :] = pick(even_z, b, a)
    ghosts[64:128, :] = jnp.zeros((64, 128), jnp.float32)
    table[...] = jnp.transpose(ghosts[...])
    table3 = table.reshape(8, TALL, 128)

    def first(x, carry):
        first_row(m0, aux, m1, rho, table3, x, 2)
        return carry

    lax.fori_loop(3, 9, first, 0)
    fetch.wait()

    def states(x, carry):
        at = pl.ds(pl.multiple_of(x * 8, 8), 8)
        value, velocity, _, _ = flow([st[k, x] for k in range(19)], cells[NEAR + 3, at, :])
        dense_zero[at, :] = value
        for i in range(3):
            vel[i, at, :] = velocity[i]
        return carry

    lax.fori_loop(0, 8, states, 0)


def outer_kernel(m0_in, aux_in, m1_in, rho_in, vel, dense, own, full, message, m0, aux, m1, rho, table, over, sums, ghosts, *, nx):
    even_z = even_of("gz")
    flat0, flat1, flat_aux = (ref.reshape(ref.shape[0] * TALL, 128) for ref in (m0, m1, aux))
    parts = relayed(message[...], nx)
    for side_x, (lines, _, _) in zip(SIDES, parts):
        for where, side_y in ((0, 1), (FACE, -1)):
            for i, (k, layer_x, layer_y) in enumerate(edge_rows(side_x, side_y)):
                x = 9 + layer_x if side_x > 0 else 2 - layer_x
                y = 11 + layer_y if side_y > 0 else 4 - layer_y
                m0[k * WIDE + x, y : y + 1, :] = lines[where + i : where + i + 1]
            for i in range(6):
                x, y = (10 if side_x > 0 else 1), (12 if side_y > 0 else 3)
                at = where + NEAR + i
                aux[i * WIDE + x, y : y + 1, :] = lines[at : at + 1]
    for tile, value in enumerate(weave_x(own[...], parts[0][2], parts[1][2])):
        b, a = value[0:32], value[32:64]
        ghosts[0:32, tile * 128 : tile * 128 + 128] = pick(even_z, a, b)
        ghosts[32:64, tile * 128 : tile * 128 + 128] = pick(even_z, b, a)
    center = jnp.concatenate(weave_x(full[...], parts[0][1], parts[1][1]), axis=1)
    ghosts[64:128, :] = jnp.zeros((64, 256), jnp.float32)
    for half, side in enumerate(SIDES):
        place = PLACE[2, side]
        b = []
        for k in range(19):
            cx, cy, cz = lattice[k]
            if cz * side < 0:
                row = half * 8 + (DOWN if side > 0 else UP).index(k)
                value = center[row : row + 1]
            else:
                row = half * 32 + place[k, 2 if cz else 1]
                value = ghosts[row : row + 1, :]
            b.append(turn(value, -(TALL * cx + cy)))
        base = half * 32 + NEAR
        extra = [ghosts[base + i : base + i + 1, :] for i in range(6)]
        result, _ = transpose_collision(b, *factors(extra))
        for i, k in enumerate(UP if side > 0 else DOWN):
            row = 64 + half * 8 + i
            ghosts[row : row + 1, :] = result[k] * extra[5]
    for tile in range(2):
        at = slice(tile * 128, tile * 128 + 128)
        table[at, :] = jnp.transpose(ghosts[:, at])
    table3 = table.reshape(TALL, TALL, 128)

    def first(i, carry):
        first_row(m0, aux, m1, rho, table3, i + 1 + 6 * (i // 2), 0)
        return carry

    lax.fori_loop(0, 4, first, 0)
    for y in (3, 12):
        for x0 in (1, 3):
            b = []
            for k in range(19):
                cx, cy, cz = lattice[k]
                start = (x0 + cx) * TALL + y + cy
                value = flat0[pl.ds(k * PLANE + start, 8, stride=TALL), :]
                if cz:
                    value = shifted(value, table[pl.ds(start, 8, stride=TALL), :], k, FIRST[k])
                b.append(value)
            start = x0 * TALL + y
            extra = [flat_aux[pl.ds(i * PLANE + start, 8, stride=TALL), :] for i in range(6)]
            result, _ = transpose_collision(b, *factors(extra))
            for k in range(19):
                flat1[pl.ds(k * PLANE + start, 8, stride=TALL), :] = result[k] * extra[5]

    def second(x, carry):
        one, two = carry
        at = pl.ds(pl.multiple_of(x * 8, 8), 8)
        b = row_b(m1, table3, SECOND, x + 2, 0)
        extra = [vel[i, at, :] for i in range(3)] + [aux[i * WIDE + x + 2, pl.ds(4, 8), :] for i in (3, 4)]
        _, gradient = transpose_collision(b, *factors(extra), dense[at, :])
        before = rho[x + 2, :, :]
        total = before + gradient
        over[at, :] = total
        return one + before * before, two + total * total

    zero = jnp.zeros((8, 128), jnp.float32)
    one, two = lax.fori_loop(0, 8, second, (zero, zero))
    one, two = jnp.sum(one, axis=0, keepdims=True), jnp.sum(two, axis=0, keepdims=True)
    devices = sums.shape[0]
    sums[:, 0:1, :] = jnp.broadcast_to(one[None], (devices, 1, 128))
    sums[:, 1:2, :] = jnp.broadcast_to(two[None], (devices, 1, 128))


def adjoint_kernel(m1, aux, vel, table, init_hbm, init, sems):
    table3 = table.reshape(TALL, TALL, 128)

    def second(x, carry):
        at = pl.ds(pl.multiple_of(x * 8, 8), 8)
        b = row_b(m1, table3, SECOND, x + 2, 0)
        extra = [vel[i, at, :] for i in range(3)] + [aux[i * WIDE + x + 2, pl.ds(4, 8), :] for i in (3, 4)]
        result, _ = transpose_collision(b, *factors(extra))
        for k in range(19):
            init[k, x] = result[k]
        pltpu.make_async_copy(init.at[:, x], init_hbm.at[:, x], sems.at[x]).start()
        return carry

    lax.fori_loop(0, 8, second, 0)
    for x in range(8):
        pltpu.make_async_copy(init.at[:, x], init_hbm.at[:, x], sems.at[x]).wait()


def scale_kernel(over, sums, descent, norms, *, cell_count):
    total = jnp.sum(sums[...], axis=0)
    square = jnp.sum(total, axis=1, keepdims=True)
    norm = jnp.sqrt(square / cell_count + 1e-06)
    descent[...] = over[...] / norm[1:2]
    norms[0] = jnp.sum(norm[0:1])
    norms[1] = jnp.sum(norm[1:2])


VMEM = pl.BlockSpec(memory_space=pltpu.VMEM)
SMEM = pl.BlockSpec(memory_space=pltpu.SMEM)
HBM = pl.BlockSpec(memory_space=pltpu.HBM)


def call(kernel, outs, scratch=(), ins=None, places=None, aliases=None, **names):
    def run(*arrays):
        return pl.pallas_call(
            functools.partial(kernel, **names),
            out_shape=[jax.ShapeDtypeStruct(shape, jnp.float32) for shape in outs],
            in_specs=ins or [VMEM] * len(arrays),
            out_specs=places or [VMEM] * len(outs),
            scratch_shapes=[pltpu.VMEM(v, jnp.float32) if isinstance(v, tuple) else v for v in scratch],
            input_output_aliases=aliases or {},
            compiler_params=pltpu.CompilerParams(vmem_limit_bytes=32 << 20),
            name=kernel.__name__,
        )(*arrays)

    return run


def in_hbm(array):
    return pltpu.with_memory_space_constraint(array, pltpu.HBM)


def swaps(axis):
    count = lax.axis_size(axis)
    ahead = [(i, (i + 1) % count if i % 2 == 0 else i - 1) for i in range(count)]
    behind = [(i, (i - 1) % count if i % 2 == 0 else (i + 1) % count) for i in range(count)]
    return ahead, behind


def both(one, two, axis):
    ahead, behind = swaps(axis)
    second = lax.ppermute(two, axis, behind)
    return lax.ppermute(one, axis, ahead), second


def two_sides(message):
    if lax.axis_size("gx") == 2:
        return lax.ppermute(message, "gx", [(0, 1), (1, 0)])
    return jnp.stack(both(message[0], message[1], "gx"))


def shards(final_adjoint, stored_states, porosity, solid_labels, boundary_mask):
    nx = lax.axis_size("gx")
    devices = nx * lax.axis_size("gy") * lax.axis_size("gz")
    cells = porosity.size
    layout = final_adjoint.shape
    block = layout[1:]
    zb, za, cen, values, dense = call(
        pack_kernel,
        [(32, 128), (32, 128), (16, 128), (FACE, 64, 128), (64, 128)],
        [
            layout,
            layout,
            block,
            pltpu.VMEM(block, jnp.int32),
            pltpu.VMEM(block, jnp.int32),
            (8, TALL, 128),
            pltpu.SemaphoreType.DMA((4, 5)),
        ],
        [HBM] * 5,
    )(*(in_hbm(v) for v in (final_adjoint, stored_states, porosity, solid_labels, boundary_mask)))
    za, ya, yb, xm = call(
        face_kernel, [(32, 128), (YROWS, 128), (YROWS, 128), (2, XROWS, 128)], nx=nx
    )(za, cen, values)
    za, zb = both(za, zb, "gz")
    ya, yb = both(ya, yb, "gy")
    xm = two_sides(xm)
    mine = jnp.concatenate([zb, za], axis=0)
    ga, gb = both(mine, mine, "gy")
    size = (2 * EDGES + 80, 128) if nx == 2 else (2, EDGES + 80, 128)
    own, full, message = call(relay_kernel, [(64, 128), (16, 128), size], nx=nx)(mine, ga, gb, ya, yb, cen)
    message = two_sides(message)
    tall, short = (19 * WIDE, TALL, 128), (6 * WIDE, TALL, 128)
    state = [tall, short, tall, (WIDE, 8, 128)]
    m0, aux, m1, rho, velocity, dense_zero = call(
        inner_kernel,
        [*state, (3, 64, 128), (64, 128)],
        [(128, 128), (128, 128), layout, pltpu.SemaphoreType.DMA],
        [VMEM] * 2 + [HBM] + [VMEM] * 4,
        nx=nx,
    )(values, dense, in_hbm(stored_states), ya, yb, xm, own)
    m0, aux, m1, rho, table, over, sums = call(
        outer_kernel,
        [*state, (256, 128), (64, 128), (devices, 2, 128)],
        [(128, 256)],
        aliases={0: 0, 1: 1, 2: 2, 3: 3},
        nx=nx,
    )(m0, aux, m1, rho, velocity, dense_zero, own, full, message)
    (init,) = call(
        adjoint_kernel, [layout], [layout, pltpu.SemaphoreType.DMA((8,))], places=[HBM]
    )(m1, aux, velocity, table)
    sums = lax.all_to_all(sums, AXES, 0, 0, tiled=True)
    descent, norms = call(scale_kernel, [(64, 128), (2,)], places=[VMEM, SMEM], cell_count=cells * devices)(over, sums)
    return init, descent.reshape(block), norms


def solution(mesh):
    in_specs = (
        P(None, "gx", "gy", "gz"),
        P(None, None, "gx", "gy", "gz"),
        P("gx", "gy", "gz"),
        P("gx", "gy", "gz"),
        P("gx", "gy", "gz"),
    )
    out_specs = (P(None, "gx", "gy", "gz"), P("gx", "gy", "gz"), P())
    return jax.shard_map(shards, mesh=mesh, in_specs=in_specs, out_specs=out_specs, check_vma=False)
```

```python
import functools

import jax
import jax.numpy as jnp
from jax import lax
from jax.experimental import pallas as pl
from jax.experimental.pallas import tpu as pltpu
from jax.sharding import PartitionSpec as P

lattice = (
    (0, 0, 0),
    (1, 0, 0),
    (-1, 0, 0),
    (0, 1, 0),
    (0, -1, 0),
    (0, 0, 1),
    (0, 0, -1),
    (1, 1, 0),
    (-1, -1, 0),
    (1, -1, 0),
    (-1, 1, 0),
    (1, 0, 1),
    (-1, 0, -1),
    (1, 0, -1),
    (-1, 0, 1),
    (0, 1, 1),
    (0, -1, -1),
    (0, 1, -1),
    (0, -1, 1),
)
opposite = (0, 2, 1, 4, 3, 6, 5, 8, 7, 10, 9, 12, 11, 14, 13, 16, 15, 18, 17)
AXES = ("gx", "gy", "gz")
PLANES = ((0, 1, 7), (0, 2, 11), (1, 2, 15))


def flow(stored, porosity):
    density = sum(stored[1:], stored[0])
    momentum = []
    for axis in range(3):
        total = None
        for vector, value in zip(lattice, stored):
            if vector[axis]:
                if total is None:
                    total = value if vector[axis] > 0 else -value
                else:
                    total = total + value if vector[axis] > 0 else total - value
        momentum.append(total)
    damping = 0.5 * (1.0 - porosity)
    beta = 1.0 / (1.0 + 0.5 * damping)
    scale = beta / density
    return density, [value * scale for value in momentum], beta, damping * beta


def transpose_collision(b, velocity, beta, alpha, solid, density=None):
    base = b[0]
    first, second = [], []
    for axis in range(3):
        ahead, behind = b[2 * axis + 1], b[2 * axis + 2]
        first.append(0.5 * (ahead - behind))
        second.append(0.5 * (ahead + behind) - base)
    odd = [None, None, None]
    tee = [None, None, None]
    ring = [None, None, None]
    evens, crosses, parts = [], [], []

    def join(where, axis, value):
        where[axis] = value if where[axis] is None else where[axis] + value

    for one, two, at in PLANES:
        pp, mm, pm, mp = b[at], b[at + 1], b[at + 2], b[at + 3]
        s1, s2, d1, d2 = pp + mm, pm + mp, pp - mm, pm - mp
        both = second[one] + second[two]
        fourth = 0.25 * (s1 + s2) - base - both
        along_one, along_two = 0.25 * (d1 + d2), 0.25 * (d1 - d2)
        even = 1.2 * both + 1.6 * fourth
        cross = 0.3 * (s1 - s2)
        q_one, q_two = 1.4 * (along_one - first[one]), 1.4 * (along_two - first[two])
        join(odd, one, q_one)
        join(odd, two, q_two)
        join(tee, one, along_one)
        join(tee, two, along_two)
        join(ring, one, even)
        join(ring, two, even)
        evens.append(even)
        crosses.append(cross)
        parts.append((q_one, q_two))
    ninth = 1.0 / 9.0
    axial = 2.4 / 18.0
    s0 = axial * (second[0] + second[1] + second[2]) + ninth * (evens[0] + evens[1] + evens[2])
    sone = [ninth * odd[axis] for axis in range(3)]
    stwo = [axial * second[axis] + ninth * ring[axis] for axis in range(3)]
    sxy, sxz, syz = (ninth * value for value in crosses)
    tees = [ninth * (first[axis] + tee[axis]) for axis in range(3)]
    ux, uy, uz = velocity
    wx = stwo[0] * ux + sxy * uy + sxz * uz
    wy = sxy * ux + stwo[1] * uy + syz * uz
    wz = sxz * ux + syz * uy + stwo[2] * uz
    quad = ux * wx + uy * wy + uz * wz
    speed = ux * ux + uy * uy + uz * uz
    scalar = s0 * (1.0 + 1.5 * speed) - 4.5 * quad
    slope = [
        beta * (3.0 * one + 9.0 * two - 3.0 * s0 * three) - 3.0 * alpha * tau
        for one, two, three, tau in zip(sone, (wx, wy, wz), velocity, tees)
    ]
    out = [base + scalar]
    for axis in range(3):
        even = scalar - 1.2 * second[axis]
        out.append(b[2 * axis + 1] + (even + slope[axis]))
        out.append(b[2 * axis + 2] + (even - slope[axis]))
    for (one, two, at), even, cross, (q_one, q_two) in zip(PLANES, evens, crosses, parts):
        same, other = scalar - even - cross, scalar - even + cross
        a_one, a_two = slope[one] - q_one, slope[two] - q_two
        plus, minus = a_one + a_two, a_one - a_two
        out.append(b[at] + (same + plus))
        out.append(b[at + 1] + (same - plus))
        out.append(b[at + 2] + (other + minus))
        out.append(b[at + 3] + (other - minus))
    out = [jnp.where(solid, b[opposite[i]], out[i]) for i in range(19)]
    if density is None:
        return out, None
    gradient = (beta * density) * (
        0.75 * (sone[0] * ux + sone[1] * uy + sone[2] * uz)
        + 2.25 * quad
        - 0.75 * s0 * speed
        + 1.5 * (tees[0] * ux + tees[1] * uy + tees[2] * uz)
    )
    return out, jnp.where(solid, 0.0, gradient)


def face_rows(axis, side):
    near = [(k, 1) for k in range(19) if lattice[k][axis] * side >= 0]
    far = [(k, 2) for k in range(19) if lattice[k][axis] * side > 0]
    return near + far


def edge_rows(side_x, side_y):
    rows = []
    for k in range(19):
        across, along = lattice[k][0] * side_x, lattice[k][1] * side_y
        for layer_x in (1, 2):
            for layer_y in (1, 2):
                fits = across >= layer_x - 1 and along >= layer_y - 1
                if fits:
                    rows.append((k, layer_x, layer_y))
    return rows


NEAR = 19
FACE = 25
UP = [k for k in range(19) if lattice[k][2] > 0]
DOWN = [k for k in range(19) if lattice[k][2] < 0]
TALL = 16
WIDE = 12
PLANE = TALL * WIDE
SIDES = (1, -1)
PLACE = {(axis, side): {row: i for i, row in enumerate(face_rows(axis, side))} for axis in range(3) for side in SIDES}
YROWS = FACE * 8 + 16
XROWS = FACE * 8
EDGES = 52


def lanes_of(shape):
    return lax.broadcasted_iota(jnp.int32, shape, len(shape) - 1)


def turn(value, shift):
    count = value.shape[-1]
    shift = shift % count
    return pltpu.roll(value, shift, value.ndim - 1) if shift else value


def pick(flag, one, two):
    return jnp.where(flag, one, two)


def even_of(axis):
    return lax.axis_index(axis) % 2 == 0


def weave_y(own, high, low):
    place = lanes_of(own.shape) % TALL
    return jnp.where(place < 4, turn(low, -8), jnp.where(place < 12, own, turn(high, 8)))


def weave_x(own, high, low):
    lane = lanes_of(own.shape)
    own = turn(own, 32)
    return jnp.where(lane < 32, turn(low, 32), own), jnp.where(lane < 32, own, turn(high, 32))


def pack_kernel(adj_hbm, st_hbm, por_hbm, sol_hbm, msk_hbm, zb, za, cen, cells, rho, adj, st, por, sol, msk, cols, table, halves, sems):
    copies = []
    for part in range(4):
        at = pl.ds(part * 2, 2)
        group = [
            (adj_hbm.at[:, at], adj.at[:, at]),
            (st_hbm.at[1, :, at], st.at[:, at]),
            (por_hbm.at[at], por.at[at]),
            (sol_hbm.at[at], sol.at[at]),
            (msk_hbm.at[at], msk.at[at]),
        ]
        copies.append([pltpu.make_async_copy(s, d, sems.at[part, i]) for i, (s, d) in enumerate(group)])
    for group in copies:
        for copy in group:
            copy.start()
    lane = lanes_of((8, 128))
    cols[...] = jnp.zeros_like(cols)

    def step(x, carry):
        at = pl.ds(pl.multiple_of(x * 8, 8), 8)
        free = 1.0 - msk[x].astype(jnp.float32)
        dense, velocity, _, _ = flow([st[k, x] for k in range(19)], por[x])
        rho[at, :] = dense
        tiles = [adj[k, x] * free for k in range(19)]
        tiles += [*velocity, por[x], sol[x].astype(jnp.float32), free]
        for k in range(FACE):
            cells[k, at, :] = tiles[k]
        spread = jnp.zeros((8, 128), jnp.float32)
        for k in range(FACE):
            rise = lattice[k][2] if k < NEAR else 0
            moved = turn(tiles[k], 2 * k + (1, 0, 2)[rise])
            spread = jnp.where(lane // 2 == k, moved, spread)
        cols[x, pl.ds(4, 8), :] = spread
        return carry

    for part, group in enumerate(copies):
        for copy in group:
            copy.wait()
        lax.fori_loop(part * 2, part * 2 + 2, step, 0, unroll=True)
    table[...] = jnp.transpose(cols[...].reshape(128, 128))
    for half, side in enumerate(SIDES):
        for i, (k, layer) in enumerate(face_rows(2, side) + [(NEAR + j, 1) for j in range(6)]):
            rise = lattice[k][2] if k < NEAR else 0
            at = 2 * k + ((layer - 1, side > 0, layer == 1)[(1, 0, 2)[rise]])
            halves[half, i : i + 1, :] = table[at : at + 1, :]
        halves[half, FACE:, :] = jnp.zeros((32 - FACE, 128), jnp.float32)
    low, high = halves[0], halves[1]
    even = even_of("gz")
    za[...] = pick(even, high, low)
    zb[...] = pick(even, low, high)
    cen[...] = jnp.zeros_like(cen)
    for half, side, pops in ((1, -1, DOWN), (0, 1, UP)):
        for i, k in enumerate(pops):
            row = PLACE[2, side][k, 1]
            at = (1 - half) * 8 + i
            cen[at : at + 1, :] = halves[half, row : row + 1, :]


def face_kernel(za, cen, cells, za_out, ya, yb, xm, *, nx):
    za_out[...] = za[...]
    even = even_of("gy")
    for i in range(FACE):
        pair = []
        for side in SIDES:
            k, layer = (face_rows(1, side) + [(NEAR + j, 1) for j in range(6)])[i]
            y = layer - 1 if side > 0 else 8 - layer
            pair.append(cells[k, pl.ds(y, 8, stride=8), :])
        low, high = pair
        ya[i * 8 : i * 8 + 8, :] = pick(even, high, low)
        yb[i * 8 : i * 8 + 8, :] = pick(even, low, high)
    ya[FACE * 8 :, :] = cen[...]
    yb[FACE * 8 :, :] = cen[...]
    even = even_of("gx")
    for i in range(FACE):
        pair = []
        for side in SIDES:
            k, layer = (face_rows(0, side) + [(NEAR + j, 1) for j in range(6)])[i]
            x = layer - 1 if side > 0 else 8 - layer
            pair.append(cells[k, x * 8 : x * 8 + 8, :])
        low, high = pair
        if nx > 2:
            low, high = pick(even, high, low), pick(even, low, high)
        xm[0, i * 8 : i * 8 + 8, :] = low
        xm[1, i * 8 : i * 8 + 8, :] = high


def relay_kernel(mine, ga, gb, full, tail):
    even = even_of("gy")
    a, b = ga[...], gb[...]
    tail[0:16, :] = full[...]
    tail[16:, :] = weave_y(mine[...], pick(even, a, b), pick(even, b, a))


def edge_kernel(ya, yb, cen, full, edges, *, nx):
    even = even_of("gy")
    at = slice(FACE * 8, FACE * 8 + 16)
    a, b = ya[at, :], yb[at, :]
    full[...] = weave_y(cen[...], pick(even, a, b), pick(even, b, a))
    even_x = even_of("gx")
    for i in range(NEAR + 6):
        for where, side_y in ((0, 1), (FACE, -1)):
            pair = []
            for side_x in SIDES:
                rows = edge_rows(side_x, side_y) + [(NEAR + j, 1, 1) for j in range(6)]
                k, layer_x, layer_y = rows[i]
                row = PLACE[1, side_y][k, layer_y] if k < NEAR else k
                x = layer_x - 1 if side_x > 0 else 8 - layer_x
                row = row * 8 + x
                a, b = ya[row : row + 1, :], yb[row : row + 1, :]
                pair.append(pick(even, a, b) if side_y > 0 else pick(even, b, a))
            one, two = pair
            if nx > 2:
                one, two = pick(even_x, two, one), pick(even_x, one, two)
            edges[0, where + i : where + i + 1, :] = one
            edges[1, where + i : where + i + 1, :] = two
    for slot in range(2):
        edges[slot, 2 * FACE :, :] = jnp.zeros((EDGES - 2 * FACE, 128), jnp.float32)


def factors(extra):
    damping = 0.5 * (1.0 - extra[3])
    beta = 1.0 / (1.0 + 0.5 * damping)
    return extra[:3], beta, damping * beta, extra[4] > 0.0


FIRST = {k: PLACE[2, 1][k, 1] for k in UP}
FIRST.update({k: 32 + PLACE[2, -1][k, 1] for k in DOWN})
SECOND = {k: 64 + i for i, k in enumerate(UP)}
SECOND.update({k: 72 + i for i, k in enumerate(DOWN)})


def shifted(value, ghost, k, column):
    lane = lanes_of(value.shape)
    if lattice[k][2] > 0:
        return jnp.where(lane == 127, turn(ghost, 127 - column), turn(value, -1))
    return jnp.where(lane == 0, turn(ghost, -column), turn(value, 1))


def row_b(ref, table, columns, x, skip):
    out = []
    for k in range(19):
        cx, cy, cz = lattice[k]
        value = ref[k * WIDE + x + cx, pl.ds(4 + cy, 8), :]
        if cz:
            value = shifted(value, table[x + cx - skip, pl.ds(4 + cy, 8), :], k, columns[k])
        out.append(value)
    return out


def first_row(m0, aux, m1, rho, table, x, skip, wanted=range(19)):
    extra = [aux[i * WIDE + x, pl.ds(4, 8), :] for i in range(6)]
    result, gradient = transpose_collision(row_b(m0, table, FIRST, x, skip), *factors(extra), rho[x, :, :])
    for k in wanted:
        m1[k * WIDE + x, pl.ds(4, 8), :] = result[k] * extra[5]
    if len(wanted) == 19:
        rho[x, :, :] = gradient


def inner_kernel(cells, dense, st_hbm, ya, yb, xm, tail, m0, aux, m1, rho, vel, dense_zero, ghosts, table, st, sem, *, nx):
    fetch = pltpu.make_async_copy(st_hbm.at[0], st, sem)
    fetch.start()
    even_y, even_z = even_of("gy"), even_of("gz")
    rho[...] = jnp.zeros_like(rho)

    def fill(x, carry):
        at = pl.ds(pl.multiple_of(x * 8, 8), 8)
        for k in range(19):
            m0[k * WIDE + x + 2, pl.ds(4, 8), :] = cells[k, at, :]
        for i in range(6):
            aux[i * WIDE + x + 2, pl.ds(4, 8), :] = cells[NEAR + i, at, :]
        rho[x + 2, :, :] = dense[at, :]
        return carry

    lax.fori_loop(0, 8, fill, 0)
    a, b = xm[0], xm[1]
    if nx > 2:
        even = even_of("gx")
        a, b = pick(even, a, b), pick(even, b, a)
    for side, tiles in zip(SIDES, (a, b)):
        for i, (k, layer) in enumerate(face_rows(0, side)):
            x = 9 + layer if side > 0 else 2 - layer
            m0[k * WIDE + x, pl.ds(4, 8), :] = tiles[i * 8 : i * 8 + 8]
        for i in range(6):
            at = (NEAR + i) * 8
            aux[i * WIDE + (10 if side > 0 else 1), pl.ds(4, 8), :] = tiles[at : at + 8]
    flat0, flat_aux = (ref.reshape(ref.shape[0] * TALL, 128) for ref in (m0, aux))
    a, b = ya[...], yb[...]
    for side, tiles in ((1, pick(even_y, a, b)), (-1, pick(even_y, b, a))):
        for i, (k, layer) in enumerate(face_rows(1, side)):
            y = 11 + layer if side > 0 else 4 - layer
            flat0[pl.ds(k * PLANE + 2 * TALL + y, 8, stride=TALL), :] = tiles[i * 8 : i * 8 + 8]
        for i in range(6):
            at = (NEAR + i) * 8
            y = 12 if side > 0 else 3
            flat_aux[pl.ds(i * PLANE + 2 * TALL + y, 8, stride=TALL), :] = tiles[at : at + 8]
    b, a = tail[16:48, :], tail[48:80, :]
    ghosts[0:32, :] = pick(even_z, a, b)
    ghosts[32:64, :] = pick(even_z, b, a)
    ghosts[64:128, :] = jnp.zeros((64, 128), jnp.float32)
    table[...] = jnp.transpose(ghosts[...])
    table3 = table.reshape(8, TALL, 128)

    def first(x, carry):
        first_row(m0, aux, m1, rho, table3, x, 2)
        return carry

    lax.fori_loop(3, 9, first, 0)
    fetch.wait()

    def states(x, carry):
        at = pl.ds(pl.multiple_of(x * 8, 8), 8)
        value, velocity, _, _ = flow([st[k, x] for k in range(19)], cells[NEAR + 3, at, :])
        dense_zero[at, :] = value
        for i in range(3):
            vel[i, at, :] = velocity[i]
        return carry

    lax.fori_loop(0, 8, states, 0)


def outer_kernel(m0_in, aux_in, m1_in, rho_in, vel, dense, tail, far, edges, m0, aux, m1, rho, table, over, sums, ghosts, *, nx):
    even_z = even_of("gz")
    flat0, flat1, flat_aux = (ref.reshape(ref.shape[0] * TALL, 128) for ref in (m0, m1, aux))
    even_x = even_of("gx")

    def along_x(ref, at):
        a, b = ref[0, at, :], ref[min(1, ref.shape[0] - 1), at, :]
        if nx == 2:
            return a, b
        return pick(even_x, a, b), pick(even_x, b, a)

    for where, side_y in ((0, 1), (FACE, -1)):
        for i in range(NEAR + 6):
            pair = along_x(edges, slice(where + i, where + i + 1))
            for side_x, line in zip(SIDES, pair):
                x, y = (10 if side_x > 0 else 1), (12 if side_y > 0 else 3)
                if i >= NEAR:
                    aux[(i - NEAR) * WIDE + x, y : y + 1, :] = line
                else:
                    k, layer_x, layer_y = edge_rows(side_x, side_y)[i]
                    x += side_x * (layer_x - 1)
                    y += side_y * (layer_y - 1)
                    m0[k * WIDE + x, y : y + 1, :] = line
    for tile, value in enumerate(weave_x(tail[16:, :], *along_x(far, slice(16, 80)))):
        b, a = value[0:32], value[32:64]
        ghosts[0:32, tile * 128 : tile * 128 + 128] = pick(even_z, a, b)
        ghosts[32:64, tile * 128 : tile * 128 + 128] = pick(even_z, b, a)
    center = jnp.concatenate(weave_x(tail[0:16, :], *along_x(far, slice(0, 16))), axis=1)
    ghosts[64:128, :] = jnp.zeros((64, 256), jnp.float32)
    b = []
    for k in range(19):
        cx, cy, cz = lattice[k]
        pair = []
        for half, side in enumerate(SIDES):
            if cz * side < 0:
                row = half * 8 + (DOWN if side > 0 else UP).index(k)
                pair.append(center[row : row + 1])
            else:
                row = half * 32 + PLACE[2, side][k, 2 if cz else 1]
                pair.append(ghosts[row : row + 1, :])
        b.append(turn(jnp.concatenate(pair, axis=0), -(TALL * cx + cy)))
    extra = [
        jnp.concatenate([ghosts[at + NEAR + i : at + NEAR + i + 1, :] for at in (0, 32)], axis=0) for i in range(6)
    ]
    result, _ = transpose_collision(b, *factors(extra))
    for half, side in enumerate(SIDES):
        for i, k in enumerate(UP if side > 0 else DOWN):
            row = 64 + half * 8 + i
            ghosts[row : row + 1, :] = (result[k] * extra[5])[half : half + 1]
    for tile in range(2):
        at = slice(tile * 128, tile * 128 + 128)
        table[at, :] = jnp.transpose(ghosts[:, at])
    table3 = table.reshape(TALL, TALL, 128)

    for x, inward in ((1, -1), (2, 0), (9, 0), (10, 1)):
        wanted = [k for k in range(19) if not inward or lattice[k][0] == inward]
        first_row(m0, aux, m1, rho, table3, x, 0, wanted)
    for y in (3, 12):
        for x0 in (1, 3):
            b = []
            for k in range(19):
                cx, cy, cz = lattice[k]
                start = (x0 + cx) * TALL + y + cy
                value = flat0[pl.ds(k * PLANE + start, 8, stride=TALL), :]
                if cz:
                    value = shifted(value, table[pl.ds(start, 8, stride=TALL), :], k, FIRST[k])
                b.append(value)
            start = x0 * TALL + y
            extra = [flat_aux[pl.ds(i * PLANE + start, 8, stride=TALL), :] for i in range(6)]
            result, _ = transpose_collision(b, *factors(extra))
            for k in range(19):
                if lattice[k][1] == (1 if y == 12 else -1):
                    flat1[pl.ds(k * PLANE + start, 8, stride=TALL), :] = result[k] * extra[5]

    def second(x, carry):
        one, two = carry
        at = pl.ds(pl.multiple_of(x * 8, 8), 8)
        b = row_b(m1, table3, SECOND, x + 2, 0)
        extra = [vel[i, at, :] for i in range(3)] + [aux[i * WIDE + x + 2, pl.ds(4, 8), :] for i in (3, 4)]
        _, gradient = transpose_collision(b, *factors(extra), dense[at, :])
        before = rho[x + 2, :, :]
        total = before + gradient
        over[at, :] = total
        return one + before * before, two + total * total

    zero = jnp.zeros((8, 128), jnp.float32)
    one, two = lax.fori_loop(0, 8, second, (zero, zero), unroll=True)
    one, two = jnp.sum(one, axis=0, keepdims=True), jnp.sum(two, axis=0, keepdims=True)
    devices = sums.shape[0]
    sums[:, 0:1, :] = jnp.broadcast_to(one[None], (devices, 1, 128))
    sums[:, 1:2, :] = jnp.broadcast_to(two[None], (devices, 1, 128))


def adjoint_kernel(m1, aux, vel, table, init_hbm, init, sems):
    table3 = table.reshape(TALL, TALL, 128)

    def second(x, carry):
        at = pl.ds(pl.multiple_of(x * 8, 8), 8)
        b = row_b(m1, table3, SECOND, x + 2, 0)
        extra = [vel[i, at, :] for i in range(3)] + [aux[i * WIDE + x + 2, pl.ds(4, 8), :] for i in (3, 4)]
        result, _ = transpose_collision(b, *factors(extra))
        for k in range(19):
            init[k, x] = result[k]
        pltpu.make_async_copy(init.at[:, x], init_hbm.at[:, x], sems.at[x]).start()
        return carry

    lax.fori_loop(0, 8, second, 0, unroll=2)
    for x in range(8):
        pltpu.make_async_copy(init.at[:, x], init_hbm.at[:, x], sems.at[x]).wait()


def scale_kernel(over, sums, descent, norms, *, cell_count):
    total = jnp.sum(sums[...], axis=0)
    square = jnp.sum(total, axis=1, keepdims=True)
    norm = jnp.sqrt(square / cell_count + 1e-06)
    descent[...] = over[...] / norm[1:2]
    norms[0] = jnp.sum(norm[0:1])
    norms[1] = jnp.sum(norm[1:2])


VMEM = pl.BlockSpec(memory_space=pltpu.VMEM)
SMEM = pl.BlockSpec(memory_space=pltpu.SMEM)
HBM = pl.BlockSpec(memory_space=pltpu.HBM)


def call(kernel, outs, scratch=(), ins=None, places=None, aliases=None, **names):
    def run(*arrays):
        return pl.pallas_call(
            functools.partial(kernel, **names),
            out_shape=[jax.ShapeDtypeStruct(shape, jnp.float32) for shape in outs],
            in_specs=ins or [VMEM] * len(arrays),
            out_specs=places or [VMEM] * len(outs),
            scratch_shapes=[pltpu.VMEM(v, jnp.float32) if isinstance(v, tuple) else v for v in scratch],
            input_output_aliases=aliases or {},
            compiler_params=pltpu.CompilerParams(vmem_limit_bytes=32 << 20),
            name=kernel.__name__,
        )(*arrays)

    return run


def in_hbm(array):
    return pltpu.with_memory_space_constraint(array, pltpu.HBM)


def swaps(axis):
    count = lax.axis_size(axis)
    ahead = [(i, (i + 1) % count if i % 2 == 0 else i - 1) for i in range(count)]
    behind = [(i, (i - 1) % count if i % 2 == 0 else (i + 1) % count) for i in range(count)]
    return ahead, behind


def both(one, two, axis):
    ahead, behind = swaps(axis)
    second = lax.ppermute(two, axis, behind)
    return lax.ppermute(one, axis, ahead), second


def two_sides(message):
    if lax.axis_size("gx") == 2:
        return lax.ppermute(message, "gx", [(0, 1), (1, 0)])
    return jnp.stack(both(message[0], message[1], "gx"))


def shards(final_adjoint, stored_states, porosity, solid_labels, boundary_mask):
    nx = lax.axis_size("gx")
    devices = nx * lax.axis_size("gy") * lax.axis_size("gz")
    cells = porosity.size
    layout = final_adjoint.shape
    block = layout[1:]
    zb, za, cen, values, dense = call(
        pack_kernel,
        [(32, 128), (32, 128), (16, 128), (FACE, 64, 128), (64, 128)],
        [
            layout,
            layout,
            block,
            pltpu.VMEM(block, jnp.int32),
            pltpu.VMEM(block, jnp.int32),
            (8, TALL, 128),
            (128, 128),
            (2, 32, 128),
            pltpu.SemaphoreType.DMA((4, 5)),
        ],
        [HBM] * 5,
    )(*(in_hbm(v) for v in (final_adjoint, stored_states, porosity, solid_labels, boundary_mask)))
    za, ya, yb, xm = call(
        face_kernel, [(32, 128), (YROWS, 128), (YROWS, 128), (2, XROWS, 128)], nx=nx
    )(za, cen, values)
    za, zb = both(za, zb, "gz")
    ya, yb = both(ya, yb, "gy")
    xm = two_sides(xm)
    mine = jnp.concatenate([zb, za], axis=0)
    ga, gb = both(mine, mine, "gy")
    full, edges = call(edge_kernel, [(16, 128), (2, EDGES, 128)], nx=nx)(ya, yb, cen)
    edges = two_sides(edges)
    (tail,) = call(relay_kernel, [(80, 128)])(mine, ga, gb, full)
    if nx == 2:
        far = lax.ppermute(tail, "gx", [(0, 1), (1, 0)])[None]
    else:
        far = jnp.stack(both(tail, tail, "gx"))
    tall, short = (19 * WIDE, TALL, 128), (6 * WIDE, TALL, 128)
    state = [tall, short, tall, (WIDE, 8, 128)]
    m0, aux, m1, rho, velocity, dense_zero = call(
        inner_kernel,
        [*state, (3, 64, 128), (64, 128)],
        [(128, 128), (128, 128), layout, pltpu.SemaphoreType.DMA],
        [VMEM] * 2 + [HBM] + [VMEM] * 4,
        nx=nx,
    )(values, dense, in_hbm(stored_states), ya, yb, xm, tail)
    m0, aux, m1, rho, table, over, sums = call(
        outer_kernel,
        [*state, (256, 128), (64, 128), (devices, 2, 128)],
        [(128, 256)],
        aliases={0: 0, 1: 1, 2: 2, 3: 3},
        nx=nx,
    )(m0, aux, m1, rho, velocity, dense_zero, tail, far, edges)
    (init,) = call(
        adjoint_kernel, [layout], [layout, pltpu.SemaphoreType.DMA((8,))], places=[HBM]
    )(m1, aux, velocity, table)
    sums = lax.all_to_all(sums, AXES, 0, 0, tiled=True)
    descent, norms = call(scale_kernel, [(64, 128), (2,)], places=[VMEM, SMEM], cell_count=cells * devices)(over, sums)
    return init, descent.reshape(block), norms


def solution(mesh):
    in_specs = (
        P(None, "gx", "gy", "gz"),
        P(None, None, "gx", "gy", "gz"),
        P("gx", "gy", "gz"),
        P("gx", "gy", "gz"),
        P("gx", "gy", "gz"),
    )
    out_specs = (P(None, "gx", "gy", "gz"), P("gx", "gy", "gz"), P())
    return jax.shard_map(shards, mesh=mesh, in_specs=in_specs, out_specs=out_specs, check_vma=False)
```

```python
import functools

import jax
import jax.numpy as jnp
from jax import lax
from jax.experimental import pallas as pl
from jax.experimental.pallas import tpu as pltpu
from jax.sharding import PartitionSpec as P

lattice = (
    (0, 0, 0),
    (1, 0, 0),
    (-1, 0, 0),
    (0, 1, 0),
    (0, -1, 0),
    (0, 0, 1),
    (0, 0, -1),
    (1, 1, 0),
    (-1, -1, 0),
    (1, -1, 0),
    (-1, 1, 0),
    (1, 0, 1),
    (-1, 0, -1),
    (1, 0, -1),
    (-1, 0, 1),
    (0, 1, 1),
    (0, -1, -1),
    (0, 1, -1),
    (0, -1, 1),
)
opposite = (0, 2, 1, 4, 3, 6, 5, 8, 7, 10, 9, 12, 11, 14, 13, 16, 15, 18, 17)
AXES = ("gx", "gy", "gz")
RINGS = ()
PLANES = ((0, 1, 7), (0, 2, 11), (1, 2, 15))


def flow(stored, porosity):
    density = sum(stored[1:], stored[0])
    momentum = []
    for axis in range(3):
        total = None
        for vector, value in zip(lattice, stored):
            if vector[axis]:
                if total is None:
                    total = value if vector[axis] > 0 else -value
                else:
                    total = total + value if vector[axis] > 0 else total - value
        momentum.append(total)
    damping = 0.5 * (1.0 - porosity)
    beta = 1.0 / (1.0 + 0.5 * damping)
    scale = beta / density
    return density, [value * scale for value in momentum], beta, damping * beta


def transpose_collision(b, velocity, beta, alpha, solid, density=None):
    base = b[0]
    first, second = [], []
    for axis in range(3):
        ahead, behind = b[2 * axis + 1], b[2 * axis + 2]
        first.append(0.5 * (ahead - behind))
        second.append(0.5 * (ahead + behind) - base)
    odd = [None, None, None]
    tee = [None, None, None]
    ring = [None, None, None]
    evens, crosses, parts = [], [], []

    def join(where, axis, value):
        where[axis] = value if where[axis] is None else where[axis] + value

    for one, two, at in PLANES:
        pp, mm, pm, mp = b[at], b[at + 1], b[at + 2], b[at + 3]
        s1, s2, d1, d2 = pp + mm, pm + mp, pp - mm, pm - mp
        both = second[one] + second[two]
        fourth = 0.25 * (s1 + s2) - base - both
        along_one, along_two = 0.25 * (d1 + d2), 0.25 * (d1 - d2)
        even = 1.2 * both + 1.6 * fourth
        cross = 0.3 * (s1 - s2)
        q_one, q_two = 1.4 * (along_one - first[one]), 1.4 * (along_two - first[two])
        join(odd, one, q_one)
        join(odd, two, q_two)
        join(tee, one, along_one)
        join(tee, two, along_two)
        join(ring, one, even)
        join(ring, two, even)
        evens.append(even)
        crosses.append(cross)
        parts.append((q_one, q_two))
    ninth = 1.0 / 9.0
    axial = 2.4 / 18.0
    s0 = axial * (second[0] + second[1] + second[2]) + ninth * (evens[0] + evens[1] + evens[2])
    sone = [ninth * odd[axis] for axis in range(3)]
    stwo = [axial * second[axis] + ninth * ring[axis] for axis in range(3)]
    sxy, sxz, syz = (ninth * value for value in crosses)
    tees = [ninth * (first[axis] + tee[axis]) for axis in range(3)]
    ux, uy, uz = velocity
    wx = stwo[0] * ux + sxy * uy + sxz * uz
    wy = sxy * ux + stwo[1] * uy + syz * uz
    wz = sxz * ux + syz * uy + stwo[2] * uz
    quad = ux * wx + uy * wy + uz * wz
    speed = ux * ux + uy * uy + uz * uz
    scalar = s0 * (1.0 + 1.5 * speed) - 4.5 * quad
    slope = [
        beta * (3.0 * one + 9.0 * two - 3.0 * s0 * three) - 3.0 * alpha * tau
        for one, two, three, tau in zip(sone, (wx, wy, wz), velocity, tees)
    ]
    out = [base + scalar]
    for axis in range(3):
        even = scalar - 1.2 * second[axis]
        out.append(b[2 * axis + 1] + (even + slope[axis]))
        out.append(b[2 * axis + 2] + (even - slope[axis]))
    for (one, two, at), even, cross, (q_one, q_two) in zip(PLANES, evens, crosses, parts):
        same, other = scalar - even - cross, scalar - even + cross
        a_one, a_two = slope[one] - q_one, slope[two] - q_two
        plus, minus = a_one + a_two, a_one - a_two
        out.append(b[at] + (same + plus))
        out.append(b[at + 1] + (same - plus))
        out.append(b[at + 2] + (other + minus))
        out.append(b[at + 3] + (other - minus))
    out = [jnp.where(solid, b[opposite[i]], out[i]) for i in range(19)]
    if density is None:
        return out, None
    gradient = (beta * density) * (
        0.75 * (sone[0] * ux + sone[1] * uy + sone[2] * uz)
        + 2.25 * quad
        - 0.75 * s0 * speed
        + 1.5 * (tees[0] * ux + tees[1] * uy + tees[2] * uz)
    )
    return out, jnp.where(solid, 0.0, gradient)


def face_rows(axis, side):
    near = [(k, 1) for k in range(19) if lattice[k][axis] * side >= 0]
    far = [(k, 2) for k in range(19) if lattice[k][axis] * side > 0]
    return near + far


def edge_rows(side_x, side_y):
    rows = []
    for k in range(19):
        across, along = lattice[k][0] * side_x, lattice[k][1] * side_y
        for layer_x in (1, 2):
            for layer_y in (1, 2):
                fits = across >= layer_x - 1 and along >= layer_y - 1
                if fits:
                    rows.append((k, layer_x, layer_y))
    return rows


NEAR = 19
FACE = 25
UP = [k for k in range(19) if lattice[k][2] > 0]
DOWN = [k for k in range(19) if lattice[k][2] < 0]
TALL = 16
WIDE = 12
PLANE = TALL * WIDE
SIDES = (1, -1)
PLACE = {(axis, side): {row: i for i, row in enumerate(face_rows(axis, side))} for axis in range(3) for side in SIDES}
YROWS = FACE * 8 + 16
XROWS = FACE * 8
EDGES = 52


def lanes_of(shape):
    return lax.broadcasted_iota(jnp.int32, shape, len(shape) - 1)


def turn(value, shift):
    count = value.shape[-1]
    shift = shift % count
    return pltpu.roll(value, shift, value.ndim - 1) if shift else value


def pick(flag, one, two):
    if isinstance(flag, bool):
        return one if flag else two
    return jnp.where(flag, one, two)


def even_of(axis):
    return True if axis in RINGS else lax.axis_index(axis) % 2 == 0


def weave_y(own, high, low):
    place = lanes_of(own.shape) % TALL
    return jnp.where(place < 4, turn(low, -8), jnp.where(place < 12, own, turn(high, 8)))


def fold(one, two):
    lane = lanes_of(one.shape)
    return jnp.where((lane < 32) | (lane >= 96), one, turn(two, 64))


def unfold(value):
    return jnp.concatenate([value, turn(value, 64)], axis=0)


def weave_x(own, high, low):
    lane = lanes_of(own.shape)
    own = turn(own, 32)
    return jnp.where(lane < 32, turn(low, 32), own), jnp.where(lane < 32, own, turn(high, 32))


def pack_kernel(adj_hbm, st_hbm, por_hbm, sol_hbm, msk_hbm, zb, za, cen, cells, rho, adj, st, por, sol, msk, cols, table, halves, sems):
    copies = []
    for part in range(4):
        at = pl.ds(part * 2, 2)
        group = [
            (adj_hbm.at[:, at], adj.at[:, at]),
            (st_hbm.at[1, :, at], st.at[:, at]),
            (por_hbm.at[at], por.at[at]),
            (sol_hbm.at[at], sol.at[at]),
            (msk_hbm.at[at], msk.at[at]),
        ]
        copies.append([pltpu.make_async_copy(s, d, sems.at[part, i]) for i, (s, d) in enumerate(group)])
    for group in copies:
        for copy in group:
            copy.start()
    lane = lanes_of((8, 128))
    cols[...] = jnp.zeros_like(cols)

    def step(x, carry):
        at = pl.ds(pl.multiple_of(x * 8, 8), 8)
        free = 1.0 - msk[x].astype(jnp.float32)
        dense, velocity, _, _ = flow([st[k, x] for k in range(19)], por[x])
        rho[at, :] = dense
        tiles = [adj[k, x] * free for k in range(19)]
        tiles += [*velocity, por[x], sol[x].astype(jnp.float32), free]
        for k in range(FACE):
            cells[k, at, :] = tiles[k]
        spread = jnp.zeros((8, 128), jnp.float32)
        for k in range(FACE):
            rise = lattice[k][2] if k < NEAR else 0
            moved = turn(tiles[k], 2 * k + (1, 0, 2)[rise])
            spread = jnp.where(lane // 2 == k, moved, spread)
        cols[x, pl.ds(4, 8), :] = spread
        return carry

    for part, group in enumerate(copies):
        for copy in group:
            copy.wait()
        lax.fori_loop(part * 2, part * 2 + 2, step, 0, unroll=True)
    table[...] = jnp.transpose(cols[...].reshape(128, 128))
    for half, side in enumerate(SIDES):
        for i, (k, layer) in enumerate(face_rows(2, side) + [(NEAR + j, 1) for j in range(6)]):
            rise = lattice[k][2] if k < NEAR else 0
            at = 2 * k + ((layer - 1, side > 0, layer == 1)[(1, 0, 2)[rise]])
            halves[half, i : i + 1, :] = table[at : at + 1, :]
        halves[half, FACE:, :] = jnp.zeros((32 - FACE, 128), jnp.float32)
    low, high = halves[0], halves[1]
    even = even_of("gz")
    za[...] = pick(even, high, low)
    zb[...] = pick(even, low, high)
    cen[...] = jnp.zeros_like(cen)
    for half, side, pops in ((1, -1, DOWN), (0, 1, UP)):
        for i, k in enumerate(pops):
            row = PLACE[2, side][k, 1]
            at = (1 - half) * 8 + i
            cen[at : at + 1, :] = halves[half, row : row + 1, :]


def face_kernel(za, cen, cells, za_out, ya, yb, xm, *, nx):
    za_out[...] = za[...]
    even = even_of("gy")
    for i in range(FACE):
        pair = []
        for side in SIDES:
            k, layer = (face_rows(1, side) + [(NEAR + j, 1) for j in range(6)])[i]
            y = layer - 1 if side > 0 else 8 - layer
            pair.append(cells[k, pl.ds(y, 8, stride=8), :])
        low, high = pair
        ya[i * 8 : i * 8 + 8, :] = pick(even, high, low)
        yb[i * 8 : i * 8 + 8, :] = pick(even, low, high)
    ya[FACE * 8 :, :] = cen[...]
    yb[FACE * 8 :, :] = cen[...]
    even = even_of("gx")
    for i in range(FACE):
        pair = []
        for side in SIDES:
            k, layer = (face_rows(0, side) + [(NEAR + j, 1) for j in range(6)])[i]
            x = layer - 1 if side > 0 else 8 - layer
            pair.append(cells[k, x * 8 : x * 8 + 8, :])
        low, high = pair
        if nx > 2:
            low, high = pick(even, high, low), pick(even, low, high)
        xm[0, i * 8 : i * 8 + 8, :] = low
        xm[1, i * 8 : i * 8 + 8, :] = high


def relay_kernel(mine, ga, gb, full, tail, packed):
    even = even_of("gy")
    a, b = ga[...], gb[...]
    tail[0:16, :] = full[...]
    woven = weave_y(mine[...], pick(even, a, b), pick(even, b, a))
    tail[16:, :] = woven
    packed[0:8, :] = fold(full[0:8, :], full[8:16, :])
    packed[8:, :] = fold(woven[:32], woven[32:])


def edge_kernel(ya, yb, cen, full, edges, *, nx):
    even = even_of("gy")
    at = slice(FACE * 8, FACE * 8 + 16)
    a, b = ya[at, :], yb[at, :]
    full[...] = weave_y(cen[...], pick(even, a, b), pick(even, b, a))
    even_x = even_of("gx")
    for i in range(NEAR + 6):
        for where, side_y in ((0, 1), (FACE, -1)):
            pair = []
            for side_x in SIDES:
                rows = edge_rows(side_x, side_y) + [(NEAR + j, 1, 1) for j in range(6)]
                k, layer_x, layer_y = rows[i]
                row = PLACE[1, side_y][k, layer_y] if k < NEAR else k
                x = layer_x - 1 if side_x > 0 else 8 - layer_x
                row = row * 8 + x
                a, b = ya[row : row + 1, :], yb[row : row + 1, :]
                pair.append(pick(even, a, b) if side_y > 0 else pick(even, b, a))
            one, two = pair
            if nx > 2:
                one, two = pick(even_x, two, one), pick(even_x, one, two)
            edges[0, where + i : where + i + 1, :] = one
            edges[1, where + i : where + i + 1, :] = two
    for slot in range(2):
        edges[slot, 2 * FACE :, :] = jnp.zeros((EDGES - 2 * FACE, 128), jnp.float32)


def factors(extra):
    damping = 0.5 * (1.0 - extra[3])
    beta = 1.0 / (1.0 + 0.5 * damping)
    return extra[:3], beta, damping * beta, extra[4] > 0.0


FIRST = {k: PLACE[2, 1][k, 1] for k in UP}
FIRST.update({k: 32 + PLACE[2, -1][k, 1] for k in DOWN})
SECOND = {k: 64 + i for i, k in enumerate(UP)}
SECOND.update({k: 72 + i for i, k in enumerate(DOWN)})


def shifted(value, ghost, k, column):
    lane = lanes_of(value.shape)
    if lattice[k][2] > 0:
        return jnp.where(lane == 127, turn(ghost, 127 - column), turn(value, -1))
    return jnp.where(lane == 0, turn(ghost, -column), turn(value, 1))


def row_b(ref, table, columns, x, skip):
    out = []
    for k in range(19):
        cx, cy, cz = lattice[k]
        value = ref[k * WIDE + x + cx, pl.ds(4 + cy, 8), :]
        if cz:
            value = shifted(value, table[x + cx - skip, pl.ds(4 + cy, 8), :], k, columns[k])
        out.append(value)
    return out


def first_row(m0, aux, m1, rho, table, x, skip, wanted=range(19)):
    extra = [aux[i * WIDE + x, pl.ds(4, 8), :] for i in range(6)]
    result, gradient = transpose_collision(row_b(m0, table, FIRST, x, skip), *factors(extra), rho[x, :, :])
    for k in wanted:
        m1[k * WIDE + x, pl.ds(4, 8), :] = result[k] * extra[5]
    if len(wanted) == 19:
        rho[x, :, :] = gradient


def caps(ghosts, center):
    b = []
    for k in range(19):
        cx, cy, cz = lattice[k]
        pair = []
        for half, side in enumerate(SIDES):
            if cz * side < 0:
                row = half * 8 + (DOWN if side > 0 else UP).index(k)
                pair.append(center[row : row + 1])
            else:
                row = half * 32 + PLACE[2, side][k, 2 if cz else 1]
                pair.append(ghosts[row : row + 1, :])
        b.append(turn(jnp.concatenate(pair, axis=0), -(TALL * cx + cy)))
    extra = [
        jnp.concatenate([ghosts[at + NEAR + i : at + NEAR + i + 1, :] for at in (0, 32)], axis=0) for i in range(6)
    ]
    result, _ = transpose_collision(b, *factors(extra))
    for half, side in enumerate(SIDES):
        for i, k in enumerate(UP if side > 0 else DOWN):
            row = 64 + half * 8 + i
            ghosts[row : row + 1, :] = (result[k] * extra[5])[half : half + 1]


def first_side(flat0, flat1, flat_aux, table, y, x0, skip):
    b = []
    for k in range(19):
        cx, cy, cz = lattice[k]
        start = (x0 + cx) * TALL + y + cy
        value = flat0[pl.ds(k * PLANE + start, 8, stride=TALL), :]
        if cz:
            value = shifted(value, table[pl.ds(start - skip * TALL, 8, stride=TALL), :], k, FIRST[k])
        b.append(value)
    start = x0 * TALL + y
    extra = [flat_aux[pl.ds(i * PLANE + start, 8, stride=TALL), :] for i in range(6)]
    result, _ = transpose_collision(b, *factors(extra))
    for k in range(19):
        if lattice[k][1] == (1 if y == 12 else -1):
            flat1[pl.ds(k * PLANE + start, 8, stride=TALL), :] = result[k] * extra[5]


def second_row(m1, aux, vel, dense, table, rho, over, x, skip):
    at = slice((x - 2) * 8, (x - 1) * 8)
    b = row_b(m1, table, SECOND, x, skip)
    extra = [vel[i, at, :] for i in range(3)] + [aux[i * WIDE + x, pl.ds(4, 8), :] for i in (3, 4)]
    _, gradient = transpose_collision(b, *factors(extra), dense[at, :])
    over[at, :] = rho[x, :, :] + gradient


def inner_kernel(cells, dense, st_hbm, ya, yb, tail, m0, aux, m1, rho, over, vel, dense_zero, ghosts, table, st, sem):
    fetch = pltpu.make_async_copy(st_hbm.at[0], st, sem)
    fetch.start()
    even_y, even_z = even_of("gy"), even_of("gz")
    rho[...] = jnp.zeros_like(rho)

    def fill(x, carry):
        at = pl.ds(pl.multiple_of(x * 8, 8), 8)
        for k in range(19):
            m0[k * WIDE + x + 2, pl.ds(4, 8), :] = cells[k, at, :]
        for i in range(6):
            aux[i * WIDE + x + 2, pl.ds(4, 8), :] = cells[NEAR + i, at, :]
        rho[x + 2, :, :] = dense[at, :]
        return carry

    lax.fori_loop(0, 8, fill, 0)
    flat0, flat_aux = (ref.reshape(ref.shape[0] * TALL, 128) for ref in (m0, aux))
    a, b = ya[...], yb[...]
    for side, tiles in ((1, pick(even_y, a, b)), (-1, pick(even_y, b, a))):
        for i, (k, layer) in enumerate(face_rows(1, side)):
            y = 11 + layer if side > 0 else 4 - layer
            flat0[pl.ds(k * PLANE + 2 * TALL + y, 8, stride=TALL), :] = tiles[i * 8 : i * 8 + 8]
        for i in range(6):
            at = (NEAR + i) * 8
            y = 12 if side > 0 else 3
            flat_aux[pl.ds(i * PLANE + 2 * TALL + y, 8, stride=TALL), :] = tiles[at : at + 8]
    b, a = tail[16:48, :], tail[48:80, :]
    ghosts[0:32, :] = pick(even_z, a, b)
    ghosts[32:64, :] = pick(even_z, b, a)
    ghosts[64:128, :] = jnp.zeros((64, 128), jnp.float32)
    caps(ghosts, tail[0:16, :])
    table[0:128, :] = jnp.transpose(ghosts[...])
    table[128:, :] = jnp.zeros((64, 128), jnp.float32)
    table3 = table.reshape(WIDE, TALL, 128)

    def first(x, carry):
        first_row(m0, aux, m1, rho, table3, x, 2)
        return carry

    lax.fori_loop(3, 9, first, 0)
    fetch.wait()

    def states(x, carry):
        at = pl.ds(pl.multiple_of(x * 8, 8), 8)
        value, velocity, _, _ = flow([st[k, x] for k in range(19)], cells[NEAR + 3, at, :])
        dense_zero[at, :] = value
        for i in range(3):
            vel[i, at, :] = velocity[i]
        return carry

    lax.fori_loop(0, 8, states, 0)
    flat1 = m1.reshape(19 * PLANE, 128)
    for y in (3, 12):
        first_side(flat0, flat1, flat_aux, table, y, 3, 2)
    for x in range(4, 8):
        second_row(m1, aux, vel, dense_zero, table3, rho, over, x, 2)


def outer_kernel(m0_in, aux_in, m1_in, rho_in, over_in, vel, dense, tail, xm, far, edges, m0, aux, m1, rho, over, table, sums, init_hbm, ghosts, init, sems, *, nx):
    even_z = even_of("gz")
    flat0, flat1, flat_aux = (ref.reshape(ref.shape[0] * TALL, 128) for ref in (m0, m1, aux))
    even_x = even_of("gx")
    a, b = xm[0], xm[1]
    if nx > 2:
        even = even_of("gx")
        a, b = pick(even, a, b), pick(even, b, a)
    for side, tiles in zip(SIDES, (a, b)):
        for i, (k, layer) in enumerate(face_rows(0, side)):
            x = 9 + layer if side > 0 else 2 - layer
            m0[k * WIDE + x, pl.ds(4, 8), :] = tiles[i * 8 : i * 8 + 8]
        for i in range(6):
            at = (NEAR + i) * 8
            aux[i * WIDE + (10 if side > 0 else 1), pl.ds(4, 8), :] = tiles[at : at + 8]

    def along_x(ref, at):
        a, b = ref[0, at, :], ref[min(1, ref.shape[0] - 1), at, :]
        if nx == 2:
            return a, b
        return pick(even_x, a, b), pick(even_x, b, a)

    for where, side_y in ((0, 1), (FACE, -1)):
        for i in range(NEAR + 6):
            pair = along_x(edges, slice(where + i, where + i + 1))
            for side_x, line in zip(SIDES, pair):
                x, y = (10 if side_x > 0 else 1), (12 if side_y > 0 else 3)
                if i >= NEAR:
                    aux[(i - NEAR) * WIDE + x, y : y + 1, :] = line
                else:
                    k, layer_x, layer_y = edge_rows(side_x, side_y)[i]
                    x += side_x * (layer_x - 1)
                    y += side_y * (layer_y - 1)
                    m0[k * WIDE + x, y : y + 1, :] = line
    for tile, value in enumerate(weave_x(tail[16:, :], *map(unfold, along_x(far, slice(8, 40))))):
        b, a = value[0:32], value[32:64]
        ghosts[0:32, tile * 128 : tile * 128 + 128] = pick(even_z, a, b)
        ghosts[32:64, tile * 128 : tile * 128 + 128] = pick(even_z, b, a)
    center = jnp.concatenate(weave_x(tail[0:16, :], *map(unfold, along_x(far, slice(0, 8)))), axis=1)
    ghosts[64:128, :] = jnp.zeros((64, 256), jnp.float32)
    caps(ghosts, center)
    for tile in range(2):
        at = slice(tile * 128, tile * 128 + 128)
        table[at, :] = jnp.transpose(ghosts[:, at])
    table3 = table.reshape(TALL, TALL, 128)

    for x, inward in ((1, -1), (2, 0), (9, 0), (10, 1)):
        wanted = [k for k in range(19) if not inward or lattice[k][0] == inward]
        first_row(m0, aux, m1, rho, table3, x, 0, wanted)
    for y in (3, 12):
        for x0 in (1, 3):
            first_side(flat0, flat1, flat_aux, table, y, x0, 0)
    for x in (2, 3, 8, 9):
        second_row(m1, aux, vel, dense, table3, rho, over, x, 0)
    one = two = jnp.zeros((8, 128), jnp.float32)
    for x in range(8):
        before, total = rho[x + 2, :, :], over[x * 8 : x * 8 + 8, :]
        one, two = one + before * before, two + total * total
    one, two = jnp.sum(one, axis=0, keepdims=True), jnp.sum(two, axis=0, keepdims=True)
    devices = sums.shape[0]
    sums[:, 0:1, :] = jnp.broadcast_to(one[None], (devices, 1, 128))
    sums[:, 1:2, :] = jnp.broadcast_to(two[None], (devices, 1, 128))

    @pl.when(early())
    def _():
        second_all(m1, aux, vel, table3, init, init_hbm, sems)


def early():
    return lax.axis_index("gz") * 2 < lax.axis_size("gz")


def second_all(m1, aux, vel, table, init, init_hbm, sems):
    copies = []
    for x in range(8):
        at = slice(x * 8, x * 8 + 8)
        b = row_b(m1, table, SECOND, x + 2, 0)
        extra = [vel[i, at, :] for i in range(3)] + [aux[i * WIDE + x + 2, pl.ds(4, 8), :] for i in (3, 4)]
        result, _ = transpose_collision(b, *factors(extra))
        for k in range(19):
            init[k, x] = result[k]
        copies.append(pltpu.make_async_copy(init.at[:, x], init_hbm.at[:, x], sems.at[x]))
        copies[-1].start()
    for copy in copies:
        copy.wait()


def final_kernel(m1, aux, vel, table, over, sums, init_in, init_hbm, descent, norms, init, sems, *, cell_count):
    @pl.when(jnp.logical_not(early()))
    def _():
        second_all(m1, aux, vel, table.reshape(TALL, TALL, 128), init, init_hbm, sems)

    total = jnp.sum(sums[...], axis=0)
    square = jnp.sum(total, axis=1, keepdims=True)
    norm = jnp.sqrt(square / cell_count + 1e-06)
    descent[...] = over[...] / norm[1:2]
    norms[0] = jnp.sum(norm[0:1])
    norms[1] = jnp.sum(norm[1:2])


VMEM = pl.BlockSpec(memory_space=pltpu.VMEM)
SMEM = pl.BlockSpec(memory_space=pltpu.SMEM)
HBM = pl.BlockSpec(memory_space=pltpu.HBM)


def call(kernel, outs, scratch=(), ins=None, places=None, aliases=None, **names):
    def run(*arrays):
        return pl.pallas_call(
            functools.partial(kernel, **names),
            out_shape=[jax.ShapeDtypeStruct(shape, jnp.float32) for shape in outs],
            in_specs=ins or [VMEM] * len(arrays),
            out_specs=places or [VMEM] * len(outs),
            scratch_shapes=[pltpu.VMEM(v, jnp.float32) if isinstance(v, tuple) else v for v in scratch],
            input_output_aliases=aliases or {},
            compiler_params=pltpu.CompilerParams(vmem_limit_bytes=32 << 20),
            name=kernel.__name__,
        )(*arrays)

    return run


def in_hbm(array):
    return pltpu.with_memory_space_constraint(array, pltpu.HBM)


def swaps(axis):
    count = lax.axis_size(axis)
    ahead = [(i, (i + 1) % count if i % 2 == 0 else i - 1) for i in range(count)]
    behind = [(i, (i - 1) % count if i % 2 == 0 else (i + 1) % count) for i in range(count)]
    return ahead, behind


def both(one, two, axis):
    if axis in RINGS:
        count = lax.axis_size(axis)
        up = lax.ppermute(one, axis, [(i, (i + 1) % count) for i in range(count)])
        return lax.ppermute(two, axis, [((i + 1) % count, i) for i in range(count)]), up
    ahead, behind = swaps(axis)
    second = lax.ppermute(two, axis, behind)
    return lax.ppermute(one, axis, ahead), second


def two_sides(message):
    if lax.axis_size("gx") == 2:
        return lax.ppermute(message, "gx", [(0, 1), (1, 0)])
    return jnp.stack(both(message[0], message[1], "gx"))


def shards(final_adjoint, stored_states, porosity, solid_labels, boundary_mask):
    nx = lax.axis_size("gx")
    devices = nx * lax.axis_size("gy") * lax.axis_size("gz")
    cells = porosity.size
    layout = final_adjoint.shape
    block = layout[1:]
    zb, za, cen, values, dense = call(
        pack_kernel,
        [(32, 128), (32, 128), (16, 128), (FACE, 64, 128), (64, 128)],
        [
            layout,
            layout,
            block,
            pltpu.VMEM(block, jnp.int32),
            pltpu.VMEM(block, jnp.int32),
            (8, TALL, 128),
            (128, 128),
            (2, 32, 128),
            pltpu.SemaphoreType.DMA((4, 5)),
        ],
        [HBM] * 5,
    )(*(in_hbm(v) for v in (final_adjoint, stored_states, porosity, solid_labels, boundary_mask)))
    za, ya, yb, xm = call(
        face_kernel, [(32, 128), (YROWS, 128), (YROWS, 128), (2, XROWS, 128)], nx=nx
    )(za, cen, values)
    za, zb = both(za, zb, "gz")
    ya, yb = both(ya, yb, "gy")
    xm = two_sides(xm)
    mine = jnp.concatenate([zb, za], axis=0)
    ga, gb = both(mine, mine, "gy")
    full, edges = call(edge_kernel, [(16, 128), (2, EDGES, 128)], nx=nx)(ya, yb, cen)
    edges = two_sides(edges)
    tail, packed = call(relay_kernel, [(80, 128), (40, 128)])(mine, ga, gb, full)
    if nx == 2:
        far = lax.ppermute(packed, "gx", [(0, 1), (1, 0)])[None]
    else:
        far = jnp.stack(both(packed, packed, "gx"))
    tall, short = (19 * WIDE, TALL, 128), (6 * WIDE, TALL, 128)
    state = [tall, short, tall, (WIDE, 8, 128), (64, 128)]
    m0, aux, m1, rho, over, velocity, dense_zero = call(
        inner_kernel,
        [*state, (3, 64, 128), (64, 128)],
        [(128, 128), (PLANE, 128), layout, pltpu.SemaphoreType.DMA],
        [VMEM] * 2 + [HBM] + [VMEM] * 3,
    )(values, dense, in_hbm(stored_states), ya, yb, tail)
    m0, aux, m1, rho, over, table, sums, init = call(
        outer_kernel,
        [*state, (256, 128), (devices, 2, 128), layout],
        [(128, 256), layout, pltpu.SemaphoreType.DMA((8,))],
        places=[VMEM] * 7 + [HBM],
        aliases={i: i for i in range(5)},
        nx=nx,
    )(m0, aux, m1, rho, over, velocity, dense_zero, tail, xm, far, edges)
    sums = lax.all_to_all(sums, AXES, 0, 0, tiled=True)
    init, descent, norms = call(
        final_kernel,
        [layout, (64, 128), (2,)],
        [layout, pltpu.SemaphoreType.DMA((8,))],
        [VMEM] * 6 + [HBM],
        [HBM, VMEM, SMEM],
        {6: 0},
        cell_count=cells * devices,
    )(m1, aux, velocity, table, over, sums, init)
    return init, descent.reshape(block), norms


def solution(mesh):
    in_specs = (
        P(None, "gx", "gy", "gz"),
        P(None, None, "gx", "gy", "gz"),
        P("gx", "gy", "gz"),
        P("gx", "gy", "gz"),
        P("gx", "gy", "gz"),
    )
    out_specs = (P(None, "gx", "gy", "gz"), P("gx", "gy", "gz"), P())
    return jax.shard_map(shards, mesh=mesh, in_specs=in_specs, out_specs=out_specs, check_vma=False)
```

```python
import functools

import jax
import jax.numpy as jnp
from jax import lax
from jax.experimental import pallas as pl
from jax.experimental.pallas import tpu as pltpu
from jax.sharding import PartitionSpec as P

lattice = (
    (0, 0, 0),
    (1, 0, 0),
    (-1, 0, 0),
    (0, 1, 0),
    (0, -1, 0),
    (0, 0, 1),
    (0, 0, -1),
    (1, 1, 0),
    (-1, -1, 0),
    (1, -1, 0),
    (-1, 1, 0),
    (1, 0, 1),
    (-1, 0, -1),
    (1, 0, -1),
    (-1, 0, 1),
    (0, 1, 1),
    (0, -1, -1),
    (0, 1, -1),
    (0, -1, 1),
)
opposite = (0, 2, 1, 4, 3, 6, 5, 8, 7, 10, 9, 12, 11, 14, 13, 16, 15, 18, 17)
AXES = ("gx", "gy", "gz")
RINGS = ()
PLANES = ((0, 1, 7), (0, 2, 11), (1, 2, 15))


def flow(stored, porosity):
    density = sum(stored[1:], stored[0])
    momentum = []
    for axis in range(3):
        total = None
        for vector, value in zip(lattice, stored):
            if vector[axis]:
                if total is None:
                    total = value if vector[axis] > 0 else -value
                else:
                    total = total + value if vector[axis] > 0 else total - value
        momentum.append(total)
    damping = 0.5 * (1.0 - porosity)
    beta = 1.0 / (1.0 + 0.5 * damping)
    scale = beta / density
    return density, [value * scale for value in momentum], beta, damping * beta


def transpose_collision(b, velocity, beta, alpha, solid, density=None):
    base = b[0]
    first, second = [], []
    for axis in range(3):
        ahead, behind = b[2 * axis + 1], b[2 * axis + 2]
        first.append(0.5 * (ahead - behind))
        second.append(0.5 * (ahead + behind) - base)
    odd = [None, None, None]
    tee = [None, None, None]
    ring = [None, None, None]
    evens, crosses, parts = [], [], []

    def join(where, axis, value):
        where[axis] = value if where[axis] is None else where[axis] + value

    for one, two, at in PLANES:
        pp, mm, pm, mp = b[at], b[at + 1], b[at + 2], b[at + 3]
        s1, s2, d1, d2 = pp + mm, pm + mp, pp - mm, pm - mp
        both = second[one] + second[two]
        fourth = 0.25 * (s1 + s2) - base - both
        along_one, along_two = 0.25 * (d1 + d2), 0.25 * (d1 - d2)
        even = 1.2 * both + 1.6 * fourth
        cross = 0.3 * (s1 - s2)
        q_one, q_two = 1.4 * (along_one - first[one]), 1.4 * (along_two - first[two])
        join(odd, one, q_one)
        join(odd, two, q_two)
        join(tee, one, along_one)
        join(tee, two, along_two)
        join(ring, one, even)
        join(ring, two, even)
        evens.append(even)
        crosses.append(cross)
        parts.append((q_one, q_two))
    ninth = 1.0 / 9.0
    axial = 2.4 / 18.0
    s0 = axial * (second[0] + second[1] + second[2]) + ninth * (evens[0] + evens[1] + evens[2])
    sone = [ninth * odd[axis] for axis in range(3)]
    stwo = [axial * second[axis] + ninth * ring[axis] for axis in range(3)]
    sxy, sxz, syz = (ninth * value for value in crosses)
    tees = [ninth * (first[axis] + tee[axis]) for axis in range(3)]
    ux, uy, uz = velocity
    wx = stwo[0] * ux + sxy * uy + sxz * uz
    wy = sxy * ux + stwo[1] * uy + syz * uz
    wz = sxz * ux + syz * uy + stwo[2] * uz
    quad = ux * wx + uy * wy + uz * wz
    speed = ux * ux + uy * uy + uz * uz
    scalar = s0 * (1.0 + 1.5 * speed) - 4.5 * quad
    slope = [
        beta * (3.0 * one + 9.0 * two - 3.0 * s0 * three) - 3.0 * alpha * tau
        for one, two, three, tau in zip(sone, (wx, wy, wz), velocity, tees)
    ]
    out = [base + scalar]
    for axis in range(3):
        even = scalar - 1.2 * second[axis]
        out.append(b[2 * axis + 1] + (even + slope[axis]))
        out.append(b[2 * axis + 2] + (even - slope[axis]))
    for (one, two, at), even, cross, (q_one, q_two) in zip(PLANES, evens, crosses, parts):
        same, other = scalar - even - cross, scalar - even + cross
        a_one, a_two = slope[one] - q_one, slope[two] - q_two
        plus, minus = a_one + a_two, a_one - a_two
        out.append(b[at] + (same + plus))
        out.append(b[at + 1] + (same - plus))
        out.append(b[at + 2] + (other + minus))
        out.append(b[at + 3] + (other - minus))
    out = [jnp.where(solid, b[opposite[i]], out[i]) for i in range(19)]
    if density is None:
        return out, None
    gradient = (beta * density) * (
        0.75 * (sone[0] * ux + sone[1] * uy + sone[2] * uz)
        + 2.25 * quad
        - 0.75 * s0 * speed
        + 1.5 * (tees[0] * ux + tees[1] * uy + tees[2] * uz)
    )
    return out, jnp.where(solid, 0.0, gradient)


def face_rows(axis, side):
    near = [(k, 1) for k in range(19) if lattice[k][axis] * side >= 0]
    far = [(k, 2) for k in range(19) if lattice[k][axis] * side > 0]
    return near + far


def edge_rows(side_x, side_y):
    rows = []
    for k in range(19):
        across, along = lattice[k][0] * side_x, lattice[k][1] * side_y
        for layer_x in (1, 2):
            for layer_y in (1, 2):
                fits = across >= layer_x - 1 and along >= layer_y - 1
                if fits:
                    rows.append((k, layer_x, layer_y))
    return rows


NEAR = 19
FACE = 25
UP = [k for k in range(19) if lattice[k][2] > 0]
DOWN = [k for k in range(19) if lattice[k][2] < 0]
TALL = 16
WIDE = 12
PLANE = TALL * WIDE
SIDES = (1, -1)
PLACE = {(axis, side): {row: i for i, row in enumerate(face_rows(axis, side))} for axis in range(2) for side in SIDES}
FLAT = [k for k in range(19) if lattice[k][2] == 0]
COEF = len(FLAT)
CROSS = COEF + 6
for side, pops in zip(SIDES, (UP, DOWN)):
    PLACE[2, side] = {(k, 1): i for i, k in enumerate(FLAT)}
    for i, k in enumerate(pops):
        for layer in (1, 2):
            PLACE[2, side][k, layer] = CROSS + 2 * i + (layer - 1 if side > 0 else 2 - layer)
YROWS = FACE * 8 + 16
XROWS = FACE * 8
EDGES = 52


def lanes_of(shape):
    return lax.broadcasted_iota(jnp.int32, shape, len(shape) - 1)


def turn(value, shift):
    count = value.shape[-1]
    shift = shift % count
    return pltpu.roll(value, shift, value.ndim - 1) if shift else value


def pick(flag, one, two):
    if isinstance(flag, bool):
        return one if flag else two
    return jnp.where(flag, one, two)


def even_of(axis):
    return True if axis in RINGS else lax.axis_index(axis) % 2 == 0


def weave_y(own, high, low):
    place = lanes_of(own.shape) % TALL
    return jnp.where(place < 4, turn(low, -8), jnp.where(place < 12, own, turn(high, 8)))


def fold(one, two):
    lane = lanes_of(one.shape)
    return jnp.where((lane < 32) | (lane >= 96), one, turn(two, 64))


def unfold(value):
    return jnp.concatenate([value, turn(value, 64)], axis=0)


def weave_x(own, high, low):
    lane = lanes_of(own.shape)
    own = turn(own, 32)
    return jnp.where(lane < 32, turn(low, 32), own), jnp.where(lane < 32, own, turn(high, 32))


def pack_kernel(adj_hbm, st_hbm, por_hbm, sol_hbm, msk_hbm, zb, za, cen, cells, rho, adj, st, por, sol, msk, cols, table, halves, sems):
    copies = []
    spans = ((0, 4), (4, 4))
    for part, (first, count) in enumerate(spans):
        at = pl.ds(first, count)
        group = [
            (adj_hbm.at[:, at], adj.at[:, at]),
            (st_hbm.at[1, :, at], st.at[:, at]),
            (por_hbm.at[at], por.at[at]),
            (sol_hbm.at[at], sol.at[at]),
            (msk_hbm.at[at], msk.at[at]),
        ]
        copies.append([pltpu.make_async_copy(s, d, sems.at[part, i]) for i, (s, d) in enumerate(group)])
    for group in copies:
        for copy in group:
            copy.start()
    lane = lanes_of((8, 128))
    cols[...] = jnp.zeros_like(cols)

    def step(x, carry):
        at = pl.ds(pl.multiple_of(x * 8, 8), 8)
        free = 1.0 - msk[x].astype(jnp.float32)
        dense, velocity, _, _ = flow([st[k, x] for k in range(19)], por[x])
        rho[at, :] = dense
        tiles = [adj[k, x] * free for k in range(19)]
        tiles += [*velocity, por[x], sol[x].astype(jnp.float32), free]
        for k in range(FACE):
            cells[k, at, :] = tiles[k]
        spread = jnp.zeros((8, 128), jnp.float32)
        for i, k in enumerate([*FLAT, *range(NEAR, FACE), *UP, *DOWN]):
            rise = lattice[k][2] if k < NEAR else 0
            spread = jnp.where(lane // 2 == i, turn(tiles[k], 2 * i + (1, 0, 2)[rise]), spread)
        cols[x, pl.ds(4, 8), :] = spread
        return carry

    for part, group in enumerate(copies):
        for copy in group:
            copy.wait()
        lax.fori_loop(spans[part][0], sum(spans[part]), step, 0, unroll=True)
    table[...] = jnp.transpose(cols[...].reshape(128, 128))
    for half in range(2):
        halves[half, 0:16, :] = table[pl.ds(1 - half, 16, stride=2), :]
        at = 2 * CROSS + 10 * half
        halves[half, CROSS : CROSS + 10, :] = table[at : at + 10, :]
        halves[half, CROSS + 10 :, :] = jnp.zeros((32 - CROSS - 10, 128), jnp.float32)
    low, high = halves[0], halves[1]
    even = even_of("gz")
    za[...] = pick(even, high, low)
    zb[...] = pick(even, low, high)
    cen[...] = jnp.zeros_like(cen)
    for half in range(2):
        at = 2 * CROSS + 10 * half + half
        cen[8 - 8 * half : 13 - 8 * half, :] = table[pl.ds(at, 5, stride=2), :]


def face_kernel(za, cen, cells, za_out, ya, yb, xm, *, nx):
    za_out[...] = za[...]
    even = even_of("gy")
    for i in range(FACE):
        pair = []
        for side in SIDES:
            k, layer = (face_rows(1, side) + [(NEAR + j, 1) for j in range(6)])[i]
            y = layer - 1 if side > 0 else 8 - layer
            pair.append(cells[k, pl.ds(y, 8, stride=8), :])
        low, high = pair
        ya[i * 8 : i * 8 + 8, :] = pick(even, high, low)
        yb[i * 8 : i * 8 + 8, :] = pick(even, low, high)
    ya[FACE * 8 :, :] = cen[...]
    yb[FACE * 8 :, :] = cen[...]
    even = even_of("gx")
    for i in range(FACE):
        pair = []
        for side in SIDES:
            k, layer = (face_rows(0, side) + [(NEAR + j, 1) for j in range(6)])[i]
            x = layer - 1 if side > 0 else 8 - layer
            pair.append(cells[k, x * 8 : x * 8 + 8, :])
        low, high = pair
        if nx > 2:
            low, high = pick(even, high, low), pick(even, low, high)
        xm[0, i * 8 : i * 8 + 8, :] = low
        xm[1, i * 8 : i * 8 + 8, :] = high


def relay_kernel(mine, ga, gb, full, tail, packed):
    even = even_of("gy")
    a, b = ga[...], gb[...]
    tail[0:16, :] = full[...]
    woven = weave_y(mine[...], pick(even, a, b), pick(even, b, a))
    tail[16:, :] = woven
    packed[0:8, :] = fold(full[0:8, :], full[8:16, :])
    packed[8:, :] = fold(woven[:32], woven[32:])


def edge_kernel(ya, yb, cen, full, edges, *, nx):
    even = even_of("gy")
    at = slice(FACE * 8, FACE * 8 + 16)
    a, b = ya[at, :], yb[at, :]
    full[...] = weave_y(cen[...], pick(even, a, b), pick(even, b, a))
    even_x = even_of("gx")
    for i in range(NEAR + 6):
        for where, side_y in ((0, 1), (FACE, -1)):
            pair = []
            for side_x in SIDES:
                rows = edge_rows(side_x, side_y) + [(NEAR + j, 1, 1) for j in range(6)]
                k, layer_x, layer_y = rows[i]
                row = PLACE[1, side_y][k, layer_y] if k < NEAR else k
                x = layer_x - 1 if side_x > 0 else 8 - layer_x
                row = row * 8 + x
                a, b = ya[row : row + 1, :], yb[row : row + 1, :]
                pair.append(pick(even, a, b) if side_y > 0 else pick(even, b, a))
            one, two = pair
            if nx > 2:
                one, two = pick(even_x, two, one), pick(even_x, one, two)
            edges[0, where + i : where + i + 1, :] = one
            edges[1, where + i : where + i + 1, :] = two
    for slot in range(2):
        edges[slot, 2 * FACE :, :] = jnp.zeros((EDGES - 2 * FACE, 128), jnp.float32)


def factors(extra):
    damping = 0.5 * (1.0 - extra[3])
    beta = 1.0 / (1.0 + 0.5 * damping)
    return extra[:3], beta, damping * beta, extra[4] > 0.0


FIRST = {k: PLACE[2, 1][k, 1] for k in UP}
FIRST.update({k: 32 + PLACE[2, -1][k, 1] for k in DOWN})
SECOND = {k: 64 + i for i, k in enumerate(UP)}
SECOND.update({k: 72 + i for i, k in enumerate(DOWN)})


def shifted(value, ghost, k, column):
    lane = lanes_of(value.shape)
    if lattice[k][2] > 0:
        return jnp.where(lane == 127, turn(ghost, 127 - column), turn(value, -1))
    return jnp.where(lane == 0, turn(ghost, -column), turn(value, 1))


def row_b(ref, table, columns, x, skip):
    out = []
    for k in range(19):
        cx, cy, cz = lattice[k]
        value = ref[k * WIDE + x + cx, pl.ds(4 + cy, 8), :]
        if cz:
            value = shifted(value, table[x + cx - skip, pl.ds(4 + cy, 8), :], k, columns[k])
        out.append(value)
    return out


def first_row(m0, aux, m1, rho, table, x, skip, wanted=range(19)):
    extra = [aux[i * WIDE + x, pl.ds(4, 8), :] for i in range(6)]
    result, gradient = transpose_collision(row_b(m0, table, FIRST, x, skip), *factors(extra), rho[x, :, :])
    for k in wanted:
        m1[k * WIDE + x, pl.ds(4, 8), :] = result[k] * extra[5]
    if len(wanted) == 19:
        rho[x, :, :] = gradient


def caps(ghosts, center):
    b = []
    for k in range(19):
        cx, cy, cz = lattice[k]
        pair = []
        for half, side in enumerate(SIDES):
            if cz * side < 0:
                row = half * 8 + (DOWN if side > 0 else UP).index(k)
                pair.append(center[row : row + 1])
            else:
                row = half * 32 + PLACE[2, side][k, 2 if cz else 1]
                pair.append(ghosts[row : row + 1, :])
        b.append(turn(jnp.concatenate(pair, axis=0), -(TALL * cx + cy)))
    extra = [
        jnp.concatenate([ghosts[at + COEF + i : at + COEF + i + 1, :] for at in (0, 32)], axis=0) for i in range(6)
    ]
    result, _ = transpose_collision(b, *factors(extra))
    for half, side in enumerate(SIDES):
        for i, k in enumerate(UP if side > 0 else DOWN):
            row = 64 + half * 8 + i
            ghosts[row : row + 1, :] = (result[k] * extra[5])[half : half + 1]


def first_side(flat0, flat1, flat_aux, table, y, x0, skip):
    b = []
    for k in range(19):
        cx, cy, cz = lattice[k]
        start = (x0 + cx) * TALL + y + cy
        value = flat0[pl.ds(k * PLANE + start, 8, stride=TALL), :]
        if cz:
            value = shifted(value, table[pl.ds(start - skip * TALL, 8, stride=TALL), :], k, FIRST[k])
        b.append(value)
    start = x0 * TALL + y
    extra = [flat_aux[pl.ds(i * PLANE + start, 8, stride=TALL), :] for i in range(6)]
    result, _ = transpose_collision(b, *factors(extra))
    for k in range(19):
        if lattice[k][1] == (1 if y == 12 else -1):
            flat1[pl.ds(k * PLANE + start, 8, stride=TALL), :] = result[k] * extra[5]


def second_row(m1, aux, vel, dense, table, rho, over, x, skip):
    at = slice((x - 2) * 8, (x - 1) * 8)
    b = row_b(m1, table, SECOND, x, skip)
    extra = [vel[i, at, :] for i in range(3)] + [aux[i * WIDE + x, pl.ds(4, 8), :] for i in (3, 4)]
    _, gradient = transpose_collision(b, *factors(extra), dense[at, :])
    over[at, :] = rho[x, :, :] + gradient


def inner_kernel(cells, dense, st_hbm, ya, yb, tail, m0, aux, m1, rho, over, vel, dense_zero, ghosts, table, st, sem):
    fetch = pltpu.make_async_copy(st_hbm.at[0], st, sem)
    fetch.start()
    even_y, even_z = even_of("gy"), even_of("gz")
    rho[...] = jnp.zeros_like(rho)

    def fill(x, carry):
        at = pl.ds(pl.multiple_of(x * 8, 8), 8)
        for k in range(19):
            m0[k * WIDE + x + 2, pl.ds(4, 8), :] = cells[k, at, :]
        for i in range(6):
            aux[i * WIDE + x + 2, pl.ds(4, 8), :] = cells[NEAR + i, at, :]
        rho[x + 2, :, :] = dense[at, :]
        return carry

    lax.fori_loop(0, 8, fill, 0)
    flat0, flat_aux = (ref.reshape(ref.shape[0] * TALL, 128) for ref in (m0, aux))
    a, b = ya[...], yb[...]
    for side, tiles in ((1, pick(even_y, a, b)), (-1, pick(even_y, b, a))):
        for i, (k, layer) in enumerate(face_rows(1, side)):
            y = 11 + layer if side > 0 else 4 - layer
            flat0[pl.ds(k * PLANE + 2 * TALL + y, 8, stride=TALL), :] = tiles[i * 8 : i * 8 + 8]
        for i in range(6):
            at = (NEAR + i) * 8
            y = 12 if side > 0 else 3
            flat_aux[pl.ds(i * PLANE + 2 * TALL + y, 8, stride=TALL), :] = tiles[at : at + 8]
    b, a = tail[16:48, :], tail[48:80, :]
    ghosts[0:32, :] = pick(even_z, a, b)
    ghosts[32:64, :] = pick(even_z, b, a)
    ghosts[64:128, :] = jnp.zeros((64, 128), jnp.float32)
    caps(ghosts, tail[0:16, :])
    table[0:128, :] = jnp.transpose(ghosts[...])
    table[128:, :] = jnp.zeros((64, 128), jnp.float32)
    table3 = table.reshape(WIDE, TALL, 128)

    def first(x, carry):
        first_row(m0, aux, m1, rho, table3, x, 2)
        return carry

    lax.fori_loop(3, 9, first, 0)
    fetch.wait()

    def states(x, carry):
        at = pl.ds(pl.multiple_of(x * 8, 8), 8)
        value, velocity, _, _ = flow([st[k, x] for k in range(19)], cells[NEAR + 3, at, :])
        dense_zero[at, :] = value
        for i in range(3):
            vel[i, at, :] = velocity[i]
        return carry

    lax.fori_loop(0, 8, states, 0)
    flat1 = m1.reshape(19 * PLANE, 128)
    for y in (3, 12):
        first_side(flat0, flat1, flat_aux, table, y, 3, 2)
    for x in range(4, 8):
        second_row(m1, aux, vel, dense_zero, table3, rho, over, x, 2)


def outer_kernel(m0_in, aux_in, m1_in, rho_in, over_in, vel, dense, tail, xm, far, edges, m0, aux, m1, rho, over, table, sums, init_hbm, ghosts, init, sems, *, nx):
    even_z = even_of("gz")
    flat0, flat1, flat_aux = (ref.reshape(ref.shape[0] * TALL, 128) for ref in (m0, m1, aux))
    even_x = even_of("gx")
    a, b = xm[0], xm[1]
    if nx > 2:
        even = even_of("gx")
        a, b = pick(even, a, b), pick(even, b, a)
    for side, tiles in zip(SIDES, (a, b)):
        for i, (k, layer) in enumerate(face_rows(0, side)):
            x = 9 + layer if side > 0 else 2 - layer
            m0[k * WIDE + x, pl.ds(4, 8), :] = tiles[i * 8 : i * 8 + 8]
        for i in range(6):
            at = (NEAR + i) * 8
            aux[i * WIDE + (10 if side > 0 else 1), pl.ds(4, 8), :] = tiles[at : at + 8]

    def along_x(ref, at):
        a, b = ref[0, at, :], ref[min(1, ref.shape[0] - 1), at, :]
        if nx == 2:
            return a, b
        return pick(even_x, a, b), pick(even_x, b, a)

    for where, side_y in ((0, 1), (FACE, -1)):
        for i in range(NEAR + 6):
            pair = along_x(edges, slice(where + i, where + i + 1))
            for side_x, line in zip(SIDES, pair):
                x, y = (10 if side_x > 0 else 1), (12 if side_y > 0 else 3)
                if i >= NEAR:
                    aux[(i - NEAR) * WIDE + x, y : y + 1, :] = line
                else:
                    k, layer_x, layer_y = edge_rows(side_x, side_y)[i]
                    x += side_x * (layer_x - 1)
                    y += side_y * (layer_y - 1)
                    m0[k * WIDE + x, y : y + 1, :] = line
    for tile, value in enumerate(weave_x(tail[16:, :], *map(unfold, along_x(far, slice(8, 40))))):
        b, a = value[0:32], value[32:64]
        ghosts[0:32, tile * 128 : tile * 128 + 128] = pick(even_z, a, b)
        ghosts[32:64, tile * 128 : tile * 128 + 128] = pick(even_z, b, a)
    center = jnp.concatenate(weave_x(tail[0:16, :], *map(unfold, along_x(far, slice(0, 8)))), axis=1)
    ghosts[64:128, :] = jnp.zeros((64, 256), jnp.float32)
    caps(ghosts, center)
    for tile in range(2):
        at = slice(tile * 128, tile * 128 + 128)
        table[at, :] = jnp.transpose(ghosts[:, at])
    table3 = table.reshape(TALL, TALL, 128)

    for x, inward in ((1, -1), (2, 0), (9, 0), (10, 1)):
        wanted = [k for k in range(19) if not inward or lattice[k][0] == inward]
        first_row(m0, aux, m1, rho, table3, x, 0, wanted)
    for y in (3, 12):
        for x0 in (1, 3):
            first_side(flat0, flat1, flat_aux, table, y, x0, 0)
    for x in (2, 3, 8, 9):
        second_row(m1, aux, vel, dense, table3, rho, over, x, 0)
    one = two = jnp.zeros((8, 128), jnp.float32)
    for x in range(8):
        before, total = rho[x + 2, :, :], over[x * 8 : x * 8 + 8, :]
        one, two = one + before * before, two + total * total
    one, two = jnp.sum(one, axis=0, keepdims=True), jnp.sum(two, axis=0, keepdims=True)
    devices = sums.shape[0]
    both_sums = jnp.where(lanes_of(one.shape) < 64, one + turn(one, 64), two + turn(two, 64))
    sums[...] = jnp.broadcast_to(both_sums[None], (devices, 1, 128))

    @pl.when(early())
    def _():
        second_all(m1, aux, vel, table3, init, init_hbm, sems)


def early():
    return lax.axis_index("gz") * 2 < lax.axis_size("gz")


def second_all(m1, aux, vel, table, init, init_hbm, sems):
    copies = []
    for x in range(8):
        at = slice(x * 8, x * 8 + 8)
        b = row_b(m1, table, SECOND, x + 2, 0)
        extra = [vel[i, at, :] for i in range(3)] + [aux[i * WIDE + x + 2, pl.ds(4, 8), :] for i in (3, 4)]
        result, _ = transpose_collision(b, *factors(extra))
        for k in range(19):
            init[k, x] = result[k]
        copies.append(pltpu.make_async_copy(init.at[:, x], init_hbm.at[:, x], sems.at[x]))
        copies[-1].start()
    for copy in copies:
        copy.wait()


def final_kernel(m1, aux, vel, table, over, sums, init_in, init_hbm, descent, norms, init, sems, *, cell_count):
    @pl.when(jnp.logical_not(early()))
    def _():
        second_all(m1, aux, vel, table.reshape(TALL, TALL, 128), init, init_hbm, sems)

    total = jnp.sum(sums[...], axis=0)
    below = lanes_of(total.shape) < 64
    squares = [jnp.sum(jnp.where(below == first, total, 0.0), axis=1, keepdims=True) for first in (True, False)]
    norm = [jnp.sqrt(square / cell_count + 1e-06) for square in squares]
    descent[...] = over[...] / norm[1]
    norms[0] = jnp.sum(norm[0])
    norms[1] = jnp.sum(norm[1])


VMEM = pl.BlockSpec(memory_space=pltpu.VMEM)
SMEM = pl.BlockSpec(memory_space=pltpu.SMEM)
HBM = pl.BlockSpec(memory_space=pltpu.HBM)


def call(kernel, outs, scratch=(), ins=None, places=None, aliases=None, **names):
    def run(*arrays):
        return pl.pallas_call(
            functools.partial(kernel, **names),
            out_shape=[jax.ShapeDtypeStruct(shape, jnp.float32) for shape in outs],
            in_specs=ins or [VMEM] * len(arrays),
            out_specs=places or [VMEM] * len(outs),
            scratch_shapes=[pltpu.VMEM(v, jnp.float32) if isinstance(v, tuple) else v for v in scratch],
            input_output_aliases=aliases or {},
            compiler_params=pltpu.CompilerParams(vmem_limit_bytes=32 << 20),
            name=kernel.__name__,
        )(*arrays)

    return run


def in_hbm(array):
    return pltpu.with_memory_space_constraint(array, pltpu.HBM)


def swaps(axis):
    count = lax.axis_size(axis)
    ahead = [(i, (i + 1) % count if i % 2 == 0 else i - 1) for i in range(count)]
    behind = [(i, (i - 1) % count if i % 2 == 0 else (i + 1) % count) for i in range(count)]
    return ahead, behind


def both(one, two, axis):
    if axis in RINGS:
        count = lax.axis_size(axis)
        up = lax.ppermute(one, axis, [(i, (i + 1) % count) for i in range(count)])
        return lax.ppermute(two, axis, [((i + 1) % count, i) for i in range(count)]), up
    ahead, behind = swaps(axis)
    second = lax.ppermute(two, axis, behind)
    return lax.ppermute(one, axis, ahead), second


def two_sides(message):
    if lax.axis_size("gx") == 2:
        return lax.ppermute(message, "gx", [(0, 1), (1, 0)])
    return jnp.stack(both(message[0], message[1], "gx"))


def shards(final_adjoint, stored_states, porosity, solid_labels, boundary_mask):
    nx = lax.axis_size("gx")
    devices = nx * lax.axis_size("gy") * lax.axis_size("gz")
    cells = porosity.size
    layout = final_adjoint.shape
    block = layout[1:]
    zb, za, cen, values, dense = call(
        pack_kernel,
        [(32, 128), (32, 128), (16, 128), (FACE, 64, 128), (64, 128)],
        [
            layout,
            layout,
            block,
            pltpu.VMEM(block, jnp.int32),
            pltpu.VMEM(block, jnp.int32),
            (8, TALL, 128),
            (128, 128),
            (2, 32, 128),
            pltpu.SemaphoreType.DMA((4, 5)),
        ],
        [HBM] * 5,
    )(*(in_hbm(v) for v in (final_adjoint, stored_states, porosity, solid_labels, boundary_mask)))
    za, ya, yb, xm = call(
        face_kernel, [(32, 128), (YROWS, 128), (YROWS, 128), (2, XROWS, 128)], nx=nx
    )(za, cen, values)
    za, zb = both(za, zb, "gz")
    ya, yb = both(ya, yb, "gy")
    xm = two_sides(xm)
    mine = jnp.concatenate([zb, za], axis=0)
    ga, gb = both(mine, mine, "gy")
    full, edges = call(edge_kernel, [(16, 128), (2, EDGES, 128)], nx=nx)(ya, yb, cen)
    edges = two_sides(edges)
    tail, packed = call(relay_kernel, [(80, 128), (40, 128)])(mine, ga, gb, full)
    if nx == 2:
        far = lax.ppermute(packed, "gx", [(0, 1), (1, 0)])[None]
    else:
        far = jnp.stack(both(packed, packed, "gx"))
    tall, short = (19 * WIDE, TALL, 128), (6 * WIDE, TALL, 128)
    state = [tall, short, tall, (WIDE, 8, 128), (64, 128)]
    m0, aux, m1, rho, over, velocity, dense_zero = call(
        inner_kernel,
        [*state, (3, 64, 128), (64, 128)],
        [(128, 128), (PLANE, 128), layout, pltpu.SemaphoreType.DMA],
        [VMEM] * 2 + [HBM] + [VMEM] * 3,
    )(values, dense, in_hbm(stored_states), ya, yb, tail)
    m0, aux, m1, rho, over, table, sums, init = call(
        outer_kernel,
        [*state, (256, 128), (devices, 1, 128), layout],
        [(128, 256), layout, pltpu.SemaphoreType.DMA((8,))],
        places=[VMEM] * 7 + [HBM],
        aliases={i: i for i in range(5)},
        nx=nx,
    )(m0, aux, m1, rho, over, velocity, dense_zero, tail, xm, far, edges)
    sums = lax.all_to_all(sums, AXES, 0, 0, tiled=True)
    init, descent, norms = call(
        final_kernel,
        [layout, (64, 128), (2,)],
        [layout, pltpu.SemaphoreType.DMA((8,))],
        [VMEM] * 6 + [HBM],
        [HBM, VMEM, SMEM],
        {6: 0},
        cell_count=cells * devices,
    )(m1, aux, velocity, table, over, sums, init)
    return init, descent.reshape(block), norms


def solution(mesh):
    in_specs = (
        P(None, "gx", "gy", "gz"),
        P(None, None, "gx", "gy", "gz"),
        P("gx", "gy", "gz"),
        P("gx", "gy", "gz"),
        P("gx", "gy", "gz"),
    )
    out_specs = (P(None, "gx", "gy", "gz"), P("gx", "gy", "gz"), P())
    return jax.shard_map(shards, mesh=mesh, in_specs=in_specs, out_specs=out_specs, check_vma=False)
```

```python
import functools

import jax
import jax.numpy as jnp
from jax import lax
from jax.experimental import pallas as pl
from jax.experimental.pallas import tpu as pltpu
from jax.sharding import PartitionSpec as P

lattice = (
    (0, 0, 0),
    (1, 0, 0),
    (-1, 0, 0),
    (0, 1, 0),
    (0, -1, 0),
    (0, 0, 1),
    (0, 0, -1),
    (1, 1, 0),
    (-1, -1, 0),
    (1, -1, 0),
    (-1, 1, 0),
    (1, 0, 1),
    (-1, 0, -1),
    (1, 0, -1),
    (-1, 0, 1),
    (0, 1, 1),
    (0, -1, -1),
    (0, 1, -1),
    (0, -1, 1),
)
opposite = (0, 2, 1, 4, 3, 6, 5, 8, 7, 10, 9, 12, 11, 14, 13, 16, 15, 18, 17)
AXES = ("gx", "gy", "gz")
RINGS = ()
PLANES = ((0, 1, 7), (0, 2, 11), (1, 2, 15))


def flow(stored, porosity):
    density = sum(stored[1:], stored[0])
    momentum = []
    for axis in range(3):
        total = None
        for vector, value in zip(lattice, stored):
            if vector[axis]:
                if total is None:
                    total = value if vector[axis] > 0 else -value
                else:
                    total = total + value if vector[axis] > 0 else total - value
        momentum.append(total)
    damping = 0.5 * (1.0 - porosity)
    beta = 1.0 / (1.0 + 0.5 * damping)
    scale = beta / density
    return density, [value * scale for value in momentum], beta, damping * beta


def transpose_collision(b, velocity, beta, alpha, solid, density=None):
    base = b[0]
    first, second = [], []
    for axis in range(3):
        ahead, behind = b[2 * axis + 1], b[2 * axis + 2]
        first.append(0.5 * (ahead - behind))
        second.append(0.5 * (ahead + behind) - base)
    odd = [None, None, None]
    tee = [None, None, None]
    ring = [None, None, None]
    evens, crosses, parts = [], [], []

    def join(where, axis, value):
        where[axis] = value if where[axis] is None else where[axis] + value

    for one, two, at in PLANES:
        pp, mm, pm, mp = b[at], b[at + 1], b[at + 2], b[at + 3]
        s1, s2, d1, d2 = pp + mm, pm + mp, pp - mm, pm - mp
        both = second[one] + second[two]
        fourth = 0.25 * (s1 + s2) - base - both
        along_one, along_two = 0.25 * (d1 + d2), 0.25 * (d1 - d2)
        even = 1.2 * both + 1.6 * fourth
        cross = 0.3 * (s1 - s2)
        q_one, q_two = 1.4 * (along_one - first[one]), 1.4 * (along_two - first[two])
        join(odd, one, q_one)
        join(odd, two, q_two)
        join(tee, one, along_one)
        join(tee, two, along_two)
        join(ring, one, even)
        join(ring, two, even)
        evens.append(even)
        crosses.append(cross)
        parts.append((q_one, q_two))
    ninth = 1.0 / 9.0
    axial = 2.4 / 18.0
    s0 = axial * (second[0] + second[1] + second[2]) + ninth * (evens[0] + evens[1] + evens[2])
    sone = [ninth * odd[axis] for axis in range(3)]
    stwo = [axial * second[axis] + ninth * ring[axis] for axis in range(3)]
    sxy, sxz, syz = (ninth * value for value in crosses)
    tees = [ninth * (first[axis] + tee[axis]) for axis in range(3)]
    ux, uy, uz = velocity
    wx = stwo[0] * ux + sxy * uy + sxz * uz
    wy = sxy * ux + stwo[1] * uy + syz * uz
    wz = sxz * ux + syz * uy + stwo[2] * uz
    quad = ux * wx + uy * wy + uz * wz
    speed = ux * ux + uy * uy + uz * uz
    scalar = s0 * (1.0 + 1.5 * speed) - 4.5 * quad
    slope = [
        beta * (3.0 * one + 9.0 * two - 3.0 * s0 * three) - 3.0 * alpha * tau
        for one, two, three, tau in zip(sone, (wx, wy, wz), velocity, tees)
    ]
    out = [base + scalar]
    for axis in range(3):
        even = scalar - 1.2 * second[axis]
        out.append(b[2 * axis + 1] + (even + slope[axis]))
        out.append(b[2 * axis + 2] + (even - slope[axis]))
    for (one, two, at), even, cross, (q_one, q_two) in zip(PLANES, evens, crosses, parts):
        same, other = scalar - even - cross, scalar - even + cross
        a_one, a_two = slope[one] - q_one, slope[two] - q_two
        plus, minus = a_one + a_two, a_one - a_two
        out.append(b[at] + (same + plus))
        out.append(b[at + 1] + (same - plus))
        out.append(b[at + 2] + (other + minus))
        out.append(b[at + 3] + (other - minus))
    out = [jnp.where(solid, b[opposite[i]], out[i]) for i in range(19)]
    if density is None:
        return out, None
    gradient = (beta * density) * (
        0.75 * (sone[0] * ux + sone[1] * uy + sone[2] * uz)
        + 2.25 * quad
        - 0.75 * s0 * speed
        + 1.5 * (tees[0] * ux + tees[1] * uy + tees[2] * uz)
    )
    return out, jnp.where(solid, 0.0, gradient)


def face_rows(axis, side):
    near = [(k, 1) for k in range(19) if lattice[k][axis] * side >= 0]
    far = [(k, 2) for k in range(19) if lattice[k][axis] * side > 0]
    return near + far


def edge_rows(side_x, side_y):
    rows = []
    for k in range(19):
        across, along = lattice[k][0] * side_x, lattice[k][1] * side_y
        for layer_x in (1, 2):
            for layer_y in (1, 2):
                fits = across >= layer_x - 1 and along >= layer_y - 1
                if fits:
                    rows.append((k, layer_x, layer_y))
    return rows


NEAR = 19
FACE = 25
UP = [k for k in range(19) if lattice[k][2] > 0]
DOWN = [k for k in range(19) if lattice[k][2] < 0]
TALL = 16
WIDE = 12
PLANE = TALL * WIDE
SIDES = (1, -1)
PLACE = {(axis, side): {row: i for i, row in enumerate(face_rows(axis, side))} for axis in range(2) for side in SIDES}
FLAT = [k for k in range(19) if lattice[k][2] == 0]
COEF = len(FLAT)
CROSS = COEF + 6
for side, pops in zip(SIDES, (UP, DOWN)):
    PLACE[2, side] = {(k, 1): i for i, k in enumerate(FLAT)}
    for i, k in enumerate(pops):
        for layer in (1, 2):
            PLACE[2, side][k, layer] = CROSS + 2 * i + (layer - 1 if side > 0 else 2 - layer)
YROWS = FACE * 8 + 16
XROWS = FACE * 8
EDGES = 52


def lanes_of(shape):
    return lax.broadcasted_iota(jnp.int32, shape, len(shape) - 1)


def turn(value, shift):
    count = value.shape[-1]
    shift = shift % count
    return pltpu.roll(value, shift, value.ndim - 1) if shift else value


def pick(flag, one, two):
    if isinstance(flag, bool):
        return one if flag else two
    return jnp.where(flag, one, two)


def even_of(axis):
    return True if axis in RINGS else lax.axis_index(axis) % 2 == 0


def weave_y(own, high, low):
    place = lanes_of(own.shape) % TALL
    return jnp.where(place < 4, turn(low, -8), jnp.where(place < 12, own, turn(high, 8)))


def fold(one, two):
    lane = lanes_of(one.shape)
    return jnp.where((lane < 32) | (lane >= 96), one, turn(two, 64))


def unfold(value):
    return jnp.concatenate([value, turn(value, 64)], axis=0)


def weave_x(own, high, low):
    lane = lanes_of(own.shape)
    own = turn(own, 32)
    return jnp.where(lane < 32, turn(low, 32), own), jnp.where(lane < 32, own, turn(high, 32))


def pack_kernel(adj_hbm, st_hbm, por_hbm, sol_hbm, msk_hbm, zb, za, cen, cells, rho, adj, st, por, sol, msk, cols, table, halves, sems):
    copies = []
    spans = ((0, 4), (4, 4))
    for part, (first, count) in enumerate(spans):
        at = pl.ds(first, count)
        group = [
            (adj_hbm.at[:, at], adj.at[:, at]),
            (st_hbm.at[1, :, at], st.at[:, at]),
            (por_hbm.at[at], por.at[at]),
            (sol_hbm.at[at], sol.at[at]),
            (msk_hbm.at[at], msk.at[at]),
        ]
        copies.append([pltpu.make_async_copy(s, d, sems.at[part, i]) for i, (s, d) in enumerate(group)])
    for group in copies:
        for copy in group:
            copy.start()
    lane = lanes_of((8, 128))
    cols[...] = jnp.zeros_like(cols)

    def step(x, carry):
        at = pl.ds(pl.multiple_of(x * 8, 8), 8)
        free = 1.0 - msk[x].astype(jnp.float32)
        dense, velocity, _, _ = flow([st[k, x] for k in range(19)], por[x])
        rho[at, :] = dense
        tiles = [adj[k, x] * free for k in range(19)]
        tiles += [*velocity, por[x], sol[x].astype(jnp.float32), free]
        for k in range(FACE):
            cells[k, at, :] = tiles[k]
        spread = jnp.zeros((8, 128), jnp.float32)
        for i, k in enumerate([*FLAT, *range(NEAR, FACE), *UP, *DOWN]):
            rise = lattice[k][2] if k < NEAR else 0
            spread = jnp.where(lane // 2 == i, turn(tiles[k], 2 * i + (1, 0, 2)[rise]), spread)
        cols[x, pl.ds(4, 8), :] = spread
        return carry

    for part, group in enumerate(copies):
        for copy in group:
            copy.wait()
        lax.fori_loop(spans[part][0], sum(spans[part]), step, 0, unroll=True)
    table[...] = jnp.transpose(cols[...].reshape(128, 128))
    for half in range(2):
        halves[half, 0:16, :] = table[pl.ds(1 - half, 16, stride=2), :]
        at = 2 * CROSS + 10 * half
        halves[half, CROSS : CROSS + 10, :] = table[at : at + 10, :]
        halves[half, CROSS + 10 :, :] = jnp.zeros((32 - CROSS - 10, 128), jnp.float32)
    low, high = halves[0], halves[1]
    even = even_of("gz")
    za[...] = pick(even, high, low)
    zb[...] = pick(even, low, high)
    cen[...] = jnp.zeros_like(cen)
    for half in range(2):
        at = 2 * CROSS + 10 * half + half
        cen[8 - 8 * half : 13 - 8 * half, :] = table[pl.ds(at, 5, stride=2), :]


def face_kernel(za, cen, cells, za_out, ya, yb, xm, *, nx):
    za_out[...] = za[...]
    even = even_of("gy")
    for i in range(FACE):
        pair = []
        for side in SIDES:
            k, layer = (face_rows(1, side) + [(NEAR + j, 1) for j in range(6)])[i]
            y = layer - 1 if side > 0 else 8 - layer
            pair.append(cells[k, pl.ds(y, 8, stride=8), :])
        low, high = pair
        ya[i * 8 : i * 8 + 8, :] = pick(even, high, low)
        yb[i * 8 : i * 8 + 8, :] = pick(even, low, high)
    ya[FACE * 8 :, :] = cen[...]
    yb[FACE * 8 :, :] = cen[...]
    even = even_of("gx")
    for i in range(FACE):
        pair = []
        for side in SIDES:
            k, layer = (face_rows(0, side) + [(NEAR + j, 1) for j in range(6)])[i]
            x = layer - 1 if side > 0 else 8 - layer
            pair.append(cells[k, x * 8 : x * 8 + 8, :])
        low, high = pair
        if nx > 2:
            low, high = pick(even, high, low), pick(even, low, high)
        xm[0, i * 8 : i * 8 + 8, :] = low
        xm[1, i * 8 : i * 8 + 8, :] = high


def relay_kernel(mine, ga, gb, full, tail, packed):
    even = even_of("gy")
    a, b = ga[...], gb[...]
    tail[0:16, :] = full[...]
    woven = weave_y(mine[...], pick(even, a, b), pick(even, b, a))
    tail[16:, :] = woven
    packed[0:8, :] = fold(full[0:8, :], full[8:16, :])
    packed[8:, :] = fold(woven[:32], woven[32:])


def edge_kernel(ya, yb, cen, full, edges, *, nx):
    even = even_of("gy")
    at = slice(FACE * 8, FACE * 8 + 16)
    a, b = ya[at, :], yb[at, :]
    full[...] = weave_y(cen[...], pick(even, a, b), pick(even, b, a))
    even_x = even_of("gx")
    for i in range(NEAR + 6):
        for where, side_y in ((0, 1), (FACE, -1)):
            pair = []
            for side_x in SIDES:
                rows = edge_rows(side_x, side_y) + [(NEAR + j, 1, 1) for j in range(6)]
                k, layer_x, layer_y = rows[i]
                row = PLACE[1, side_y][k, layer_y] if k < NEAR else k
                x = layer_x - 1 if side_x > 0 else 8 - layer_x
                row = row * 8 + x
                a, b = ya[row : row + 1, :], yb[row : row + 1, :]
                pair.append(pick(even, a, b) if side_y > 0 else pick(even, b, a))
            one, two = pair
            if nx > 2:
                one, two = pick(even_x, two, one), pick(even_x, one, two)
            edges[0, where + i : where + i + 1, :] = one
            edges[1, where + i : where + i + 1, :] = two
    for slot in range(2):
        edges[slot, 2 * FACE :, :] = jnp.zeros((EDGES - 2 * FACE, 128), jnp.float32)


def factors(extra):
    damping = 0.5 * (1.0 - extra[3])
    beta = 1.0 / (1.0 + 0.5 * damping)
    return extra[:3], beta, damping * beta, extra[4] > 0.0


FIRST = {k: PLACE[2, 1][k, 1] for k in UP}
FIRST.update({k: 32 + PLACE[2, -1][k, 1] for k in DOWN})
SECOND = {k: 64 + i for i, k in enumerate(UP)}
SECOND.update({k: 72 + i for i, k in enumerate(DOWN)})


def shifted(value, ghost, k, column):
    lane = lanes_of(value.shape)
    if lattice[k][2] > 0:
        return jnp.where(lane == 127, turn(ghost, 127 - column), turn(value, -1))
    return jnp.where(lane == 0, turn(ghost, -column), turn(value, 1))


def row_b(ref, table, columns, x, skip):
    out = []
    for k in range(19):
        cx, cy, cz = lattice[k]
        value = ref[k * WIDE + x + cx, pl.ds(4 + cy, 8), :]
        if cz:
            value = shifted(value, table[x + cx - skip, pl.ds(4 + cy, 8), :], k, columns[k])
        out.append(value)
    return out


def first_row(m0, aux, m1, rho, table, x, skip, wanted=range(19)):
    extra = [aux[i * WIDE + x, pl.ds(4, 8), :] for i in range(6)]
    result, gradient = transpose_collision(row_b(m0, table, FIRST, x, skip), *factors(extra), rho[x, :, :])
    for k in wanted:
        m1[k * WIDE + x, pl.ds(4, 8), :] = result[k] * extra[5]
    if len(wanted) == 19:
        rho[x, :, :] = gradient


def caps(ghosts, center):
    b = []
    for k in range(19):
        cx, cy, cz = lattice[k]
        pair = []
        for half, side in enumerate(SIDES):
            if cz * side < 0:
                row = half * 8 + (DOWN if side > 0 else UP).index(k)
                pair.append(center[row : row + 1])
            else:
                row = half * 32 + PLACE[2, side][k, 2 if cz else 1]
                pair.append(ghosts[row : row + 1, :])
        b.append(turn(jnp.concatenate(pair, axis=0), -(TALL * cx + cy)))
    extra = [
        jnp.concatenate([ghosts[at + COEF + i : at + COEF + i + 1, :] for at in (0, 32)], axis=0) for i in range(6)
    ]
    result, _ = transpose_collision(b, *factors(extra))
    for half, side in enumerate(SIDES):
        for i, k in enumerate(UP if side > 0 else DOWN):
            row = 64 + half * 8 + i
            ghosts[row : row + 1, :] = (result[k] * extra[5])[half : half + 1]


def first_side(flat0, flat1, flat_aux, table, y, x0, skip):
    b = []
    for k in range(19):
        cx, cy, cz = lattice[k]
        start = (x0 + cx) * TALL + y + cy
        value = flat0[pl.ds(k * PLANE + start, 8, stride=TALL), :]
        if cz:
            value = shifted(value, table[pl.ds(start - skip * TALL, 8, stride=TALL), :], k, FIRST[k])
        b.append(value)
    start = x0 * TALL + y
    extra = [flat_aux[pl.ds(i * PLANE + start, 8, stride=TALL), :] for i in range(6)]
    result, _ = transpose_collision(b, *factors(extra))
    for k in range(19):
        if lattice[k][1] == (1 if y == 12 else -1):
            flat1[pl.ds(k * PLANE + start, 8, stride=TALL), :] = result[k] * extra[5]


def second_row(m1, aux, vel, dense, table, rho, over, x, skip):
    at = slice((x - 2) * 8, (x - 1) * 8)
    b = row_b(m1, table, SECOND, x, skip)
    extra = [vel[i, at, :] for i in range(3)] + [aux[i * WIDE + x, pl.ds(4, 8), :] for i in (3, 4)]
    _, gradient = transpose_collision(b, *factors(extra), dense[at, :])
    over[at, :] = rho[x, :, :] + gradient


def inner_kernel(cells, dense, st_hbm, ya, yb, tail, m0, aux, m1, rho, over, vel, dense_zero, partial, ghosts, table, st, sem):
    fetch = pltpu.make_async_copy(st_hbm.at[0], st, sem)
    fetch.start()
    even_y, even_z = even_of("gy"), even_of("gz")
    rho[...] = jnp.zeros_like(rho)

    def fill(x, carry):
        at = pl.ds(pl.multiple_of(x * 8, 8), 8)
        for k in range(19):
            m0[k * WIDE + x + 2, pl.ds(4, 8), :] = cells[k, at, :]
        for i in range(6):
            aux[i * WIDE + x + 2, pl.ds(4, 8), :] = cells[NEAR + i, at, :]
        rho[x + 2, :, :] = dense[at, :]
        return carry

    lax.fori_loop(0, 8, fill, 0, unroll=True)
    flat0, flat_aux = (ref.reshape(ref.shape[0] * TALL, 128) for ref in (m0, aux))
    a, b = ya[...], yb[...]
    for side, tiles in ((1, pick(even_y, a, b)), (-1, pick(even_y, b, a))):
        for i, (k, layer) in enumerate(face_rows(1, side)):
            y = 11 + layer if side > 0 else 4 - layer
            flat0[pl.ds(k * PLANE + 2 * TALL + y, 8, stride=TALL), :] = tiles[i * 8 : i * 8 + 8]
        for i in range(6):
            at = (NEAR + i) * 8
            y = 12 if side > 0 else 3
            flat_aux[pl.ds(i * PLANE + 2 * TALL + y, 8, stride=TALL), :] = tiles[at : at + 8]
    b, a = tail[16:48, :], tail[48:80, :]
    ghosts[0:32, :] = pick(even_z, a, b)
    ghosts[32:64, :] = pick(even_z, b, a)
    ghosts[64:128, :] = jnp.zeros((64, 128), jnp.float32)
    caps(ghosts, tail[0:16, :])
    table[0:128, :] = jnp.transpose(ghosts[...])
    table[128:, :] = jnp.zeros((64, 128), jnp.float32)
    table3 = table.reshape(WIDE, TALL, 128)

    def first(x, carry):
        first_row(m0, aux, m1, rho, table3, x, 2)
        return carry

    lax.fori_loop(3, 9, first, 0, unroll=True)
    fetch.wait()

    def states(x, carry):
        at = pl.ds(pl.multiple_of(x * 8, 8), 8)
        value, velocity, _, _ = flow([st[k, x] for k in range(19)], cells[NEAR + 3, at, :])
        dense_zero[at, :] = value
        for i in range(3):
            vel[i, at, :] = velocity[i]
        return carry

    lax.fori_loop(0, 8, states, 0, unroll=True)
    flat1 = m1.reshape(19 * PLANE, 128)
    for y in (3, 12):
        first_side(flat0, flat1, flat_aux, table, y, 3, 2)
    for x in range(4, 8):
        second_row(m1, aux, vel, dense_zero, table3, rho, over, x, 2)
    one = two = jnp.zeros((8, 128), jnp.float32)
    for x in range(4, 8):
        before, total = rho[x, :, :], over[x * 8 - 16 : x * 8 - 8, :]
        one, two = one + before * before, two + total * total
    partial[0, :, :] = one
    partial[1, :, :] = two


def outer_kernel(m0_in, aux_in, m1_in, rho_in, over_in, vel, dense, partial, tail, xm, far, edges, m0, aux, m1, rho, over, table, sums, init_hbm, ghosts, init, sems, *, nx):
    even_z = even_of("gz")
    flat0, flat1, flat_aux = (ref.reshape(ref.shape[0] * TALL, 128) for ref in (m0, m1, aux))
    even_x = even_of("gx")
    a, b = xm[0], xm[1]
    if nx > 2:
        even = even_of("gx")
        a, b = pick(even, a, b), pick(even, b, a)
    for side, tiles in zip(SIDES, (a, b)):
        for i, (k, layer) in enumerate(face_rows(0, side)):
            x = 9 + layer if side > 0 else 2 - layer
            m0[k * WIDE + x, pl.ds(4, 8), :] = tiles[i * 8 : i * 8 + 8]
        for i in range(6):
            at = (NEAR + i) * 8
            aux[i * WIDE + (10 if side > 0 else 1), pl.ds(4, 8), :] = tiles[at : at + 8]

    def along_x(ref, at):
        a, b = ref[0, at, :], ref[min(1, ref.shape[0] - 1), at, :]
        if nx == 2:
            return a, b
        return pick(even_x, a, b), pick(even_x, b, a)

    for where, side_y in ((0, 1), (FACE, -1)):
        for i in range(NEAR + 6):
            pair = along_x(edges, slice(where + i, where + i + 1))
            for side_x, line in zip(SIDES, pair):
                x, y = (10 if side_x > 0 else 1), (12 if side_y > 0 else 3)
                if i >= NEAR:
                    aux[(i - NEAR) * WIDE + x, y : y + 1, :] = line
                else:
                    k, layer_x, layer_y = edge_rows(side_x, side_y)[i]
                    x += side_x * (layer_x - 1)
                    y += side_y * (layer_y - 1)
                    m0[k * WIDE + x, y : y + 1, :] = line
    for tile, value in enumerate(weave_x(tail[16:, :], *map(unfold, along_x(far, slice(8, 40))))):
        b, a = value[0:32], value[32:64]
        ghosts[0:32, tile * 128 : tile * 128 + 128] = pick(even_z, a, b)
        ghosts[32:64, tile * 128 : tile * 128 + 128] = pick(even_z, b, a)
    center = jnp.concatenate(weave_x(tail[0:16, :], *map(unfold, along_x(far, slice(0, 8)))), axis=1)
    ghosts[64:128, :] = jnp.zeros((64, 256), jnp.float32)
    caps(ghosts, center)
    for tile in range(2):
        at = slice(tile * 128, tile * 128 + 128)
        table[at, :] = jnp.transpose(ghosts[:, at])
    table3 = table.reshape(TALL, TALL, 128)

    for x, inward in ((1, -1), (2, 0), (9, 0), (10, 1)):
        wanted = [k for k in range(19) if not inward or lattice[k][0] == inward]
        first_row(m0, aux, m1, rho, table3, x, 0, wanted)
    for y in (3, 12):
        for x0 in (1, 3):
            first_side(flat0, flat1, flat_aux, table, y, x0, 0)
    for x in (2, 3, 8, 9):
        second_row(m1, aux, vel, dense, table3, rho, over, x, 0)
    one, two = partial[0, :, :], partial[1, :, :]
    for x in (0, 1, 6, 7):
        before, total = rho[x + 2, :, :], over[x * 8 : x * 8 + 8, :]
        one, two = one + before * before, two + total * total
    one, two = jnp.sum(one, axis=0, keepdims=True), jnp.sum(two, axis=0, keepdims=True)
    devices = sums.shape[0]
    both_sums = jnp.where(lanes_of(one.shape) < 64, one + turn(one, 64), two + turn(two, 64))
    sums[...] = jnp.broadcast_to(both_sums[None], (devices, 1, 128))

    @pl.when(early())
    def _():
        second_all(m1, aux, vel, table3, init, init_hbm, sems)


def early():
    return lax.axis_index("gz") == 0


def second_all(m1, aux, vel, table, init, init_hbm, sems):
    copies = []
    for x in range(8):
        at = slice(x * 8, x * 8 + 8)
        b = row_b(m1, table, SECOND, x + 2, 0)
        extra = [vel[i, at, :] for i in range(3)] + [aux[i * WIDE + x + 2, pl.ds(4, 8), :] for i in (3, 4)]
        result, _ = transpose_collision(b, *factors(extra))
        for k in range(19):
            init[k, x] = result[k]
        copies.append(pltpu.make_async_copy(init.at[:, x], init_hbm.at[:, x], sems.at[x]))
        copies[-1].start()
    for copy in copies:
        copy.wait()


def final_kernel(m1, aux, vel, table, over, sums, init_in, init_hbm, descent, norms, init, sems, *, cell_count):
    @pl.when(jnp.logical_not(early()))
    def _():
        second_all(m1, aux, vel, table.reshape(TALL, TALL, 128), init, init_hbm, sems)

    total = jnp.sum(sums[...], axis=0)
    below = lanes_of(total.shape) < 64
    squares = [jnp.sum(jnp.where(below == first, total, 0.0), axis=1, keepdims=True) for first in (True, False)]
    norm = [jnp.sqrt(square / cell_count + 1e-06) for square in squares]
    descent[...] = over[...] / norm[1]
    norms[0] = jnp.sum(norm[0])
    norms[1] = jnp.sum(norm[1])


VMEM = pl.BlockSpec(memory_space=pltpu.VMEM)
SMEM = pl.BlockSpec(memory_space=pltpu.SMEM)
HBM = pl.BlockSpec(memory_space=pltpu.HBM)


def call(kernel, outs, scratch=(), ins=None, places=None, aliases=None, **names):
    def run(*arrays):
        return pl.pallas_call(
            functools.partial(kernel, **names),
            out_shape=[jax.ShapeDtypeStruct(shape, jnp.float32) for shape in outs],
            in_specs=ins or [VMEM] * len(arrays),
            out_specs=places or [VMEM] * len(outs),
            scratch_shapes=[pltpu.VMEM(v, jnp.float32) if isinstance(v, tuple) else v for v in scratch],
            input_output_aliases=aliases or {},
            compiler_params=pltpu.CompilerParams(vmem_limit_bytes=32 << 20),
            name=kernel.__name__,
        )(*arrays)

    return run


def in_hbm(array):
    return pltpu.with_memory_space_constraint(array, pltpu.HBM)


def swaps(axis):
    count = lax.axis_size(axis)
    ahead = [(i, (i + 1) % count if i % 2 == 0 else i - 1) for i in range(count)]
    behind = [(i, (i - 1) % count if i % 2 == 0 else (i + 1) % count) for i in range(count)]
    return ahead, behind


def both(one, two, axis):
    if axis in RINGS:
        count = lax.axis_size(axis)
        up = lax.ppermute(one, axis, [(i, (i + 1) % count) for i in range(count)])
        return lax.ppermute(two, axis, [((i + 1) % count, i) for i in range(count)]), up
    ahead, behind = swaps(axis)
    second = lax.ppermute(two, axis, behind)
    return lax.ppermute(one, axis, ahead), second


def two_sides(message):
    if lax.axis_size("gx") == 2:
        return lax.ppermute(message, "gx", [(0, 1), (1, 0)])
    return jnp.stack(both(message[0], message[1], "gx"))


def shards(final_adjoint, stored_states, porosity, solid_labels, boundary_mask):
    nx = lax.axis_size("gx")
    devices = nx * lax.axis_size("gy") * lax.axis_size("gz")
    cells = porosity.size
    layout = final_adjoint.shape
    block = layout[1:]
    zb, za, cen, values, dense = call(
        pack_kernel,
        [(32, 128), (32, 128), (16, 128), (FACE, 64, 128), (64, 128)],
        [
            layout,
            layout,
            block,
            pltpu.VMEM(block, jnp.int32),
            pltpu.VMEM(block, jnp.int32),
            (8, TALL, 128),
            (128, 128),
            (2, 32, 128),
            pltpu.SemaphoreType.DMA((4, 5)),
        ],
        [HBM] * 5,
    )(*(in_hbm(v) for v in (final_adjoint, stored_states, porosity, solid_labels, boundary_mask)))
    za, ya, yb, xm = call(
        face_kernel, [(32, 128), (YROWS, 128), (YROWS, 128), (2, XROWS, 128)], nx=nx
    )(za, cen, values)
    za, zb = both(za, zb, "gz")
    ya, yb = both(ya, yb, "gy")
    xm = two_sides(xm)
    mine = jnp.concatenate([zb, za], axis=0)
    ga, gb = both(mine, mine, "gy")
    full, edges = call(edge_kernel, [(16, 128), (2, EDGES, 128)], nx=nx)(ya, yb, cen)
    edges = two_sides(edges)
    tail, packed = call(relay_kernel, [(80, 128), (40, 128)])(mine, ga, gb, full)
    if nx == 2:
        far = lax.ppermute(packed, "gx", [(0, 1), (1, 0)])[None]
    else:
        far = jnp.stack(both(packed, packed, "gx"))
    tall, short = (19 * WIDE, TALL, 128), (6 * WIDE, TALL, 128)
    state = [tall, short, tall, (WIDE, 8, 128), (64, 128)]
    m0, aux, m1, rho, over, velocity, dense_zero, partial = call(
        inner_kernel,
        [*state, (3, 64, 128), (64, 128), (2, 8, 128)],
        [(128, 128), (PLANE, 128), layout, pltpu.SemaphoreType.DMA],
        [VMEM] * 2 + [HBM] + [VMEM] * 3,
    )(values, dense, in_hbm(stored_states), ya, yb, tail)
    m0, aux, m1, rho, over, table, sums, init = call(
        outer_kernel,
        [*state, (256, 128), (devices, 1, 128), layout],
        [(128, 256), layout, pltpu.SemaphoreType.DMA((8,))],
        places=[VMEM] * 7 + [HBM],
        aliases={i: i for i in range(5)},
        nx=nx,
    )(m0, aux, m1, rho, over, velocity, dense_zero, partial, tail, xm, far, edges)
    sums = lax.all_to_all(sums, AXES, 0, 0, tiled=True)
    init, descent, norms = call(
        final_kernel,
        [layout, (64, 128), (2,)],
        [layout, pltpu.SemaphoreType.DMA((8,))],
        [VMEM] * 6 + [HBM],
        [HBM, VMEM, SMEM],
        {6: 0},
        cell_count=cells * devices,
    )(m1, aux, velocity, table, over, sums, init)
    return init, descent.reshape(block), norms


def solution(mesh):
    in_specs = (
        P(None, "gx", "gy", "gz"),
        P(None, None, "gx", "gy", "gz"),
        P("gx", "gy", "gz"),
        P("gx", "gy", "gz"),
        P("gx", "gy", "gz"),
    )
    out_specs = (P(None, "gx", "gy", "gz"), P("gx", "gy", "gz"), P())
    return jax.shard_map(shards, mesh=mesh, in_specs=in_specs, out_specs=out_specs, check_vma=False)
```

```python
import functools

import jax
import jax.numpy as jnp
from jax import lax
from jax.experimental import pallas as pl
from jax.experimental.pallas import tpu as pltpu
from jax.sharding import PartitionSpec as P

lattice = (
    (0, 0, 0),
    (1, 0, 0),
    (-1, 0, 0),
    (0, 1, 0),
    (0, -1, 0),
    (0, 0, 1),
    (0, 0, -1),
    (1, 1, 0),
    (-1, -1, 0),
    (1, -1, 0),
    (-1, 1, 0),
    (1, 0, 1),
    (-1, 0, -1),
    (1, 0, -1),
    (-1, 0, 1),
    (0, 1, 1),
    (0, -1, -1),
    (0, 1, -1),
    (0, -1, 1),
)
opposite = (0, 2, 1, 4, 3, 6, 5, 8, 7, 10, 9, 12, 11, 14, 13, 16, 15, 18, 17)
AXES = ("gx", "gy", "gz")
RINGS = ()
PLANES = ((0, 1, 7), (0, 2, 11), (1, 2, 15))


def flow(stored, porosity):
    density = sum(stored[1:], stored[0])
    momentum = []
    for axis in range(3):
        total = None
        for vector, value in zip(lattice, stored):
            if vector[axis]:
                if total is None:
                    total = value if vector[axis] > 0 else -value
                else:
                    total = total + value if vector[axis] > 0 else total - value
        momentum.append(total)
    damping = 0.5 * (1.0 - porosity)
    beta = 1.0 / (1.0 + 0.5 * damping)
    scale = beta / density
    return density, [value * scale for value in momentum], beta, damping * beta


def transpose_collision(b, velocity, beta, alpha, solid, density=None):
    base = b[0]
    first, second = [], []
    for axis in range(3):
        ahead, behind = b[2 * axis + 1], b[2 * axis + 2]
        first.append(0.5 * (ahead - behind))
        second.append(0.5 * (ahead + behind) - base)
    odd = [None, None, None]
    tee = [None, None, None]
    ring = [None, None, None]
    evens, crosses, parts = [], [], []

    def join(where, axis, value):
        where[axis] = value if where[axis] is None else where[axis] + value

    for one, two, at in PLANES:
        pp, mm, pm, mp = b[at], b[at + 1], b[at + 2], b[at + 3]
        s1, s2, d1, d2 = pp + mm, pm + mp, pp - mm, pm - mp
        both = second[one] + second[two]
        fourth = 0.25 * (s1 + s2) - base - both
        along_one, along_two = 0.25 * (d1 + d2), 0.25 * (d1 - d2)
        even = 1.2 * both + 1.6 * fourth
        cross = 0.3 * (s1 - s2)
        q_one, q_two = 1.4 * (along_one - first[one]), 1.4 * (along_two - first[two])
        join(odd, one, q_one)
        join(odd, two, q_two)
        join(tee, one, along_one)
        join(tee, two, along_two)
        join(ring, one, even)
        join(ring, two, even)
        evens.append(even)
        crosses.append(cross)
        parts.append((q_one, q_two))
    ninth = 1.0 / 9.0
    axial = 2.4 / 18.0
    s0 = axial * (second[0] + second[1] + second[2]) + ninth * (evens[0] + evens[1] + evens[2])
    sone = [ninth * odd[axis] for axis in range(3)]
    stwo = [axial * second[axis] + ninth * ring[axis] for axis in range(3)]
    sxy, sxz, syz = (ninth * value for value in crosses)
    tees = [ninth * (first[axis] + tee[axis]) for axis in range(3)]
    ux, uy, uz = velocity
    wx = stwo[0] * ux + sxy * uy + sxz * uz
    wy = sxy * ux + stwo[1] * uy + syz * uz
    wz = sxz * ux + syz * uy + stwo[2] * uz
    quad = ux * wx + uy * wy + uz * wz
    speed = ux * ux + uy * uy + uz * uz
    scalar = s0 * (1.0 + 1.5 * speed) - 4.5 * quad
    slope = [
        beta * (3.0 * one + 9.0 * two - 3.0 * s0 * three) - 3.0 * alpha * tau
        for one, two, three, tau in zip(sone, (wx, wy, wz), velocity, tees)
    ]
    out = [base + scalar]
    for axis in range(3):
        even = scalar - 1.2 * second[axis]
        out.append(b[2 * axis + 1] + (even + slope[axis]))
        out.append(b[2 * axis + 2] + (even - slope[axis]))
    for (one, two, at), even, cross, (q_one, q_two) in zip(PLANES, evens, crosses, parts):
        same, other = scalar - even - cross, scalar - even + cross
        a_one, a_two = slope[one] - q_one, slope[two] - q_two
        plus, minus = a_one + a_two, a_one - a_two
        out.append(b[at] + (same + plus))
        out.append(b[at + 1] + (same - plus))
        out.append(b[at + 2] + (other + minus))
        out.append(b[at + 3] + (other - minus))
    out = [jnp.where(solid, b[opposite[i]], out[i]) for i in range(19)]
    if density is None:
        return out, None
    gradient = (beta * density) * (
        0.75 * (sone[0] * ux + sone[1] * uy + sone[2] * uz)
        + 2.25 * quad
        - 0.75 * s0 * speed
        + 1.5 * (tees[0] * ux + tees[1] * uy + tees[2] * uz)
    )
    return out, jnp.where(solid, 0.0, gradient)


def face_rows(axis, side):
    near = [(k, 1) for k in range(19) if lattice[k][axis] * side >= 0]
    far = [(k, 2) for k in range(19) if lattice[k][axis] * side > 0]
    return near + far


def edge_rows(side_x, side_y):
    rows = []
    for k in range(19):
        across, along = lattice[k][0] * side_x, lattice[k][1] * side_y
        for layer_x in (1, 2):
            for layer_y in (1, 2):
                fits = across >= layer_x - 1 and along >= layer_y - 1
                if fits:
                    rows.append((k, layer_x, layer_y))
    return rows


NEAR = 19
FACE = 25
UP = [k for k in range(19) if lattice[k][2] > 0]
DOWN = [k for k in range(19) if lattice[k][2] < 0]
TALL = 16
WIDE = 12
PLANE = TALL * WIDE
SIDES = (1, -1)
PLACE = {(axis, side): {row: i for i, row in enumerate(face_rows(axis, side))} for axis in range(2) for side in SIDES}
FLAT = [k for k in range(19) if lattice[k][2] == 0]
COEF = len(FLAT)
CROSS = COEF + 6
for side, pops in zip(SIDES, (UP, DOWN)):
    PLACE[2, side] = {(k, 1): i for i, k in enumerate(FLAT)}
    for i, k in enumerate(pops):
        for layer in (1, 2):
            PLACE[2, side][k, layer] = CROSS + 2 * i + (layer - 1 if side > 0 else 2 - layer)
YROWS = FACE * 8 + 16
XROWS = FACE * 8
EDGES = 52


def lanes_of(shape):
    return lax.broadcasted_iota(jnp.int32, shape, len(shape) - 1)


def turn(value, shift):
    count = value.shape[-1]
    shift = shift % count
    return pltpu.roll(value, shift, value.ndim - 1) if shift else value


def pick(flag, one, two):
    if isinstance(flag, bool):
        return one if flag else two
    return jnp.where(flag, one, two)


def even_of(axis):
    return True if axis in RINGS else lax.axis_index(axis) % 2 == 0


def weave_y(own, high, low):
    place = lanes_of(own.shape) % TALL
    return jnp.where(place < 4, turn(low, -8), jnp.where(place < 12, own, turn(high, 8)))


def fold(one, two):
    lane = lanes_of(one.shape)
    return jnp.where((lane < 32) | (lane >= 96), one, turn(two, 64))


def unfold(value):
    return jnp.concatenate([value, turn(value, 64)], axis=0)


def weave_x(own, high, low):
    lane = lanes_of(own.shape)
    own = turn(own, 32)
    return jnp.where(lane < 32, turn(low, 32), own), jnp.where(lane < 32, own, turn(high, 32))


def pack_kernel(adj_hbm, st_hbm, por_hbm, sol_hbm, msk_hbm, zb, za, cen, cells, rho, adj, st, por, sol, msk, cols, table, halves, sems):
    copies = []
    spans = ((0, 4), (4, 4))
    for part, (first, count) in enumerate(spans):
        at = pl.ds(first, count)
        group = [
            (adj_hbm.at[:, at], adj.at[:, at]),
            (st_hbm.at[1, :, at], st.at[:, at]),
            (por_hbm.at[at], por.at[at]),
            (sol_hbm.at[at], sol.at[at]),
            (msk_hbm.at[at], msk.at[at]),
        ]
        copies.append([pltpu.make_async_copy(s, d, sems.at[part, i]) for i, (s, d) in enumerate(group)])
    for group in copies:
        for copy in group:
            copy.start()
    lane = lanes_of((8, 128))
    cols[...] = jnp.zeros_like(cols)

    def step(x, carry):
        at = pl.ds(pl.multiple_of(x * 8, 8), 8)
        free = 1.0 - msk[x].astype(jnp.float32)
        dense, velocity, _, _ = flow([st[k, x] for k in range(19)], por[x])
        rho[at, :] = dense
        tiles = [adj[k, x] * free for k in range(19)]
        tiles += [*velocity, por[x], sol[x].astype(jnp.float32), free]
        for k in range(FACE):
            cells[k, at, :] = tiles[k]
        spread = jnp.zeros((8, 128), jnp.float32)
        for i, k in enumerate([*FLAT, *range(NEAR, FACE), *UP, *DOWN]):
            rise = lattice[k][2] if k < NEAR else 0
            spread = jnp.where(lane // 2 == i, turn(tiles[k], 2 * i + (1, 0, 2)[rise]), spread)
        cols[x, pl.ds(4, 8), :] = spread
        return carry

    for part, group in enumerate(copies):
        for copy in group:
            copy.wait()
        lax.fori_loop(spans[part][0], sum(spans[part]), step, 0, unroll=True)
    table[...] = jnp.transpose(cols[...].reshape(128, 128))
    for half in range(2):
        halves[half, 0:16, :] = table[pl.ds(1 - half, 16, stride=2), :]
        at = 2 * CROSS + 10 * half
        halves[half, CROSS : CROSS + 10, :] = table[at : at + 10, :]
        halves[half, CROSS + 10 :, :] = jnp.zeros((32 - CROSS - 10, 128), jnp.float32)
    low, high = halves[0], halves[1]
    even = even_of("gz")
    za[...] = pick(even, high, low)
    zb[...] = pick(even, low, high)
    cen[...] = jnp.zeros_like(cen)
    for half in range(2):
        at = 2 * CROSS + 10 * half + half
        cen[8 - 8 * half : 13 - 8 * half, :] = table[pl.ds(at, 5, stride=2), :]


def face_kernel(za, cen, cells, za_out, ya, yb, xm, *, nx):
    za_out[...] = za[...]
    even = even_of("gy")
    for i in range(FACE):
        pair = []
        for side in SIDES:
            k, layer = (face_rows(1, side) + [(NEAR + j, 1) for j in range(6)])[i]
            y = layer - 1 if side > 0 else 8 - layer
            pair.append(cells[k, pl.ds(y, 8, stride=8), :])
        low, high = pair
        ya[i * 8 : i * 8 + 8, :] = pick(even, high, low)
        yb[i * 8 : i * 8 + 8, :] = pick(even, low, high)
    ya[FACE * 8 :, :] = cen[...]
    yb[FACE * 8 :, :] = cen[...]
    even = even_of("gx")
    for i in range(FACE):
        pair = []
        for side in SIDES:
            k, layer = (face_rows(0, side) + [(NEAR + j, 1) for j in range(6)])[i]
            x = layer - 1 if side > 0 else 8 - layer
            pair.append(cells[k, x * 8 : x * 8 + 8, :])
        low, high = pair
        if nx > 2:
            low, high = pick(even, high, low), pick(even, low, high)
        xm[0, i * 8 : i * 8 + 8, :] = low
        xm[1, i * 8 : i * 8 + 8, :] = high


def relay_kernel(mine, ga, gb, full, tail, packed):
    even = even_of("gy")
    a, b = ga[...], gb[...]
    tail[0:16, :] = full[...]
    woven = weave_y(mine[...], pick(even, a, b), pick(even, b, a))
    tail[16:, :] = woven
    packed[0:8, :] = fold(full[0:8, :], full[8:16, :])
    packed[8:, :] = fold(woven[:32], woven[32:])


def edge_kernel(ya, yb, cen, full, edges, *, nx):
    even = even_of("gy")
    at = slice(FACE * 8, FACE * 8 + 16)
    a, b = ya[at, :], yb[at, :]
    full[...] = weave_y(cen[...], pick(even, a, b), pick(even, b, a))
    even_x = even_of("gx")
    for i in range(NEAR + 6):
        for where, side_y in ((0, 1), (FACE, -1)):
            pair = []
            for side_x in SIDES:
                rows = edge_rows(side_x, side_y) + [(NEAR + j, 1, 1) for j in range(6)]
                k, layer_x, layer_y = rows[i]
                row = PLACE[1, side_y][k, layer_y] if k < NEAR else k
                x = layer_x - 1 if side_x > 0 else 8 - layer_x
                row = row * 8 + x
                a, b = ya[row : row + 1, :], yb[row : row + 1, :]
                pair.append(pick(even, a, b) if side_y > 0 else pick(even, b, a))
            one, two = pair
            if nx > 2:
                one, two = pick(even_x, two, one), pick(even_x, one, two)
            edges[0, where + i : where + i + 1, :] = one
            edges[1, where + i : where + i + 1, :] = two
    for slot in range(2):
        edges[slot, 2 * FACE :, :] = jnp.zeros((EDGES - 2 * FACE, 128), jnp.float32)


def factors(extra):
    damping = 0.5 * (1.0 - extra[3])
    beta = 1.0 / (1.0 + 0.5 * damping)
    return extra[:3], beta, damping * beta, extra[4] > 0.0


FIRST = {k: PLACE[2, 1][k, 1] for k in UP}
FIRST.update({k: 32 + PLACE[2, -1][k, 1] for k in DOWN})
SECOND = {k: 64 + i for i, k in enumerate(UP)}
SECOND.update({k: 72 + i for i, k in enumerate(DOWN)})


def shifted(value, ghost, k, column):
    lane = lanes_of(value.shape)
    if lattice[k][2] > 0:
        return jnp.where(lane == 127, turn(ghost, 127 - column), turn(value, -1))
    return jnp.where(lane == 0, turn(ghost, -column), turn(value, 1))


def row_b(ref, table, columns, x, skip):
    out = []
    for k in range(19):
        cx, cy, cz = lattice[k]
        value = ref[k * WIDE + x + cx, pl.ds(4 + cy, 8), :]
        if cz:
            value = shifted(value, table[x + cx - skip, pl.ds(4 + cy, 8), :], k, columns[k])
        out.append(value)
    return out


def first_row(m0, aux, m1, rho, table, x, skip, wanted=range(19)):
    extra = [aux[i * WIDE + x, pl.ds(4, 8), :] for i in range(6)]
    result, gradient = transpose_collision(row_b(m0, table, FIRST, x, skip), *factors(extra), rho[x, :, :])
    for k in wanted:
        m1[k * WIDE + x, pl.ds(4, 8), :] = result[k] * extra[5]
    if len(wanted) == 19:
        rho[x, :, :] = gradient


def caps(ghosts, center):
    b = []
    for k in range(19):
        cx, cy, cz = lattice[k]
        pair = []
        for half, side in enumerate(SIDES):
            if cz * side < 0:
                row = half * 8 + (DOWN if side > 0 else UP).index(k)
                pair.append(center[row : row + 1])
            else:
                row = half * 32 + PLACE[2, side][k, 2 if cz else 1]
                pair.append(ghosts[row : row + 1, :])
        b.append(turn(jnp.concatenate(pair, axis=0), -(TALL * cx + cy)))
    extra = [
        jnp.concatenate([ghosts[at + COEF + i : at + COEF + i + 1, :] for at in (0, 32)], axis=0) for i in range(6)
    ]
    result, _ = transpose_collision(b, *factors(extra))
    for half, side in enumerate(SIDES):
        for i, k in enumerate(UP if side > 0 else DOWN):
            row = 64 + half * 8 + i
            ghosts[row : row + 1, :] = (result[k] * extra[5])[half : half + 1]


def first_side(flat0, flat1, flat_aux, table, y, x0, skip):
    b = []
    for k in range(19):
        cx, cy, cz = lattice[k]
        start = (x0 + cx) * TALL + y + cy
        value = flat0[pl.ds(k * PLANE + start, 8, stride=TALL), :]
        if cz:
            value = shifted(value, table[pl.ds(start - skip * TALL, 8, stride=TALL), :], k, FIRST[k])
        b.append(value)
    start = x0 * TALL + y
    extra = [flat_aux[pl.ds(i * PLANE + start, 8, stride=TALL), :] for i in range(6)]
    result, _ = transpose_collision(b, *factors(extra))
    for k in range(19):
        if lattice[k][1] == (1 if y == 12 else -1):
            flat1[pl.ds(k * PLANE + start, 8, stride=TALL), :] = result[k] * extra[5]


def second_row(m1, aux, vel, dense, table, rho, over, x, skip):
    at = slice((x - 2) * 8, (x - 1) * 8)
    b = row_b(m1, table, SECOND, x, skip)
    extra = [vel[i, at, :] for i in range(3)] + [aux[i * WIDE + x, pl.ds(4, 8), :] for i in (3, 4)]
    _, gradient = transpose_collision(b, *factors(extra), dense[at, :])
    over[at, :] = rho[x, :, :] + gradient


def inner_kernel(cells, dense, st_hbm, ya, yb, tail, m0, aux, m1, rho, over, vel, dense_zero, partial, ghosts, table, st, sem):
    fetch = pltpu.make_async_copy(st_hbm.at[0], st, sem)
    fetch.start()
    even_y, even_z = even_of("gy"), even_of("gz")
    rho[...] = jnp.zeros_like(rho)

    def fill(x, carry):
        at = pl.ds(pl.multiple_of(x * 8, 8), 8)
        for k in range(19):
            m0[k * WIDE + x + 2, pl.ds(4, 8), :] = cells[k, at, :]
        for i in range(6):
            aux[i * WIDE + x + 2, pl.ds(4, 8), :] = cells[NEAR + i, at, :]
        rho[x + 2, :, :] = dense[at, :]
        return carry

    lax.fori_loop(0, 8, fill, 0, unroll=True)
    flat0, flat_aux = (ref.reshape(ref.shape[0] * TALL, 128) for ref in (m0, aux))
    a, b = ya[...], yb[...]
    for side, tiles in ((1, pick(even_y, a, b)), (-1, pick(even_y, b, a))):
        for i, (k, layer) in enumerate(face_rows(1, side)):
            y = 11 + layer if side > 0 else 4 - layer
            flat0[pl.ds(k * PLANE + 2 * TALL + y, 8, stride=TALL), :] = tiles[i * 8 : i * 8 + 8]
        for i in range(6):
            at = (NEAR + i) * 8
            y = 12 if side > 0 else 3
            flat_aux[pl.ds(i * PLANE + 2 * TALL + y, 8, stride=TALL), :] = tiles[at : at + 8]
    b, a = tail[16:48, :], tail[48:80, :]
    ghosts[0:32, :] = pick(even_z, a, b)
    ghosts[32:64, :] = pick(even_z, b, a)
    ghosts[64:128, :] = jnp.zeros((64, 128), jnp.float32)
    caps(ghosts, tail[0:16, :])
    table[0:128, :] = jnp.transpose(ghosts[...])
    table[128:, :] = jnp.zeros((64, 128), jnp.float32)
    table3 = table.reshape(WIDE, TALL, 128)

    def first(x, carry):
        first_row(m0, aux, m1, rho, table3, x, 2)
        return carry

    lax.fori_loop(3, 9, first, 0, unroll=True)
    fetch.wait()

    def states(x, carry):
        at = pl.ds(pl.multiple_of(x * 8, 8), 8)
        value, velocity, _, _ = flow([st[k, x] for k in range(19)], cells[NEAR + 3, at, :])
        dense_zero[at, :] = value
        for i in range(3):
            vel[i, at, :] = velocity[i]
        return carry

    lax.fori_loop(0, 8, states, 0, unroll=True)
    flat1 = m1.reshape(19 * PLANE, 128)
    for y in (3, 12):
        first_side(flat0, flat1, flat_aux, table, y, 3, 2)
    for x in range(4, 8):
        second_row(m1, aux, vel, dense_zero, table3, rho, over, x, 2)
    one = two = jnp.zeros((8, 128), jnp.float32)
    for x in range(4, 8):
        before, total = rho[x, :, :], over[x * 8 - 16 : x * 8 - 8, :]
        one, two = one + before * before, two + total * total
    partial[0, :, :] = one
    partial[1, :, :] = two


def outer_kernel(m0_in, aux_in, m1_in, rho_in, over_in, vel, dense, partial, tail, xm, far, edges, m0, aux, m1, rho, over, table, sums, init_hbm, ghosts, init, sems, *, nx):
    even_z = even_of("gz")
    flat0, flat1, flat_aux = (ref.reshape(ref.shape[0] * TALL, 128) for ref in (m0, m1, aux))
    even_x = even_of("gx")
    a, b = xm[0], xm[1]
    if nx > 2:
        even = even_of("gx")
        a, b = pick(even, a, b), pick(even, b, a)
    for side, tiles in zip(SIDES, (a, b)):
        for i, (k, layer) in enumerate(face_rows(0, side)):
            x = 9 + layer if side > 0 else 2 - layer
            m0[k * WIDE + x, pl.ds(4, 8), :] = tiles[i * 8 : i * 8 + 8]
        for i in range(6):
            at = (NEAR + i) * 8
            aux[i * WIDE + (10 if side > 0 else 1), pl.ds(4, 8), :] = tiles[at : at + 8]

    def along_x(ref, at):
        a, b = ref[0, at, :], ref[min(1, ref.shape[0] - 1), at, :]
        if nx == 2:
            return a, b
        return pick(even_x, a, b), pick(even_x, b, a)

    for where, side_y in ((0, 1), (FACE, -1)):
        for i in range(NEAR + 6):
            pair = along_x(edges, slice(where + i, where + i + 1))
            for side_x, line in zip(SIDES, pair):
                x, y = (10 if side_x > 0 else 1), (12 if side_y > 0 else 3)
                if i >= NEAR:
                    aux[(i - NEAR) * WIDE + x, y : y + 1, :] = line
                else:
                    k, layer_x, layer_y = edge_rows(side_x, side_y)[i]
                    x += side_x * (layer_x - 1)
                    y += side_y * (layer_y - 1)
                    m0[k * WIDE + x, y : y + 1, :] = line
    for tile, value in enumerate(weave_x(tail[16:, :], *map(unfold, along_x(far, slice(8, 40))))):
        b, a = value[0:32], value[32:64]
        ghosts[0:32, tile * 128 : tile * 128 + 128] = pick(even_z, a, b)
        ghosts[32:64, tile * 128 : tile * 128 + 128] = pick(even_z, b, a)
    center = jnp.concatenate(weave_x(tail[0:16, :], *map(unfold, along_x(far, slice(0, 8)))), axis=1)
    ghosts[64:128, :] = jnp.zeros((64, 256), jnp.float32)
    caps(ghosts, center)
    for tile in range(2):
        at = slice(tile * 128, tile * 128 + 128)
        table[at, :] = jnp.transpose(ghosts[:, at])
    table3 = table.reshape(TALL, TALL, 128)

    for x, inward in ((1, -1), (2, 0), (9, 0), (10, 1)):
        wanted = [k for k in range(19) if not inward or lattice[k][0] == inward]
        first_row(m0, aux, m1, rho, table3, x, 0, wanted)
    for y in (3, 12):
        for x0 in (1, 3):
            first_side(flat0, flat1, flat_aux, table, y, x0, 0)
    for x in (2, 3, 8, 9):
        second_row(m1, aux, vel, dense, table3, rho, over, x, 0)
    one, two = partial[0, :, :], partial[1, :, :]
    for x in (0, 1, 6, 7):
        before, total = rho[x + 2, :, :], over[x * 8 : x * 8 + 8, :]
        one, two = one + before * before, two + total * total
    one, two = jnp.sum(one, axis=0, keepdims=True), jnp.sum(two, axis=0, keepdims=True)
    devices = sums.shape[0]
    both_sums = jnp.where(lanes_of(one.shape) < 64, one + turn(one, 64), two + turn(two, 64))
    sums[...] = jnp.broadcast_to(both_sums[None], (devices, 1, 128))

    @pl.when(early())
    def _():
        second_all(m1, aux, vel, table3, init, init_hbm, sems)


def early():
    return (lax.axis_index("gz") == 0) & (lax.axis_index("gx") == 0) & (lax.axis_index("gy") < 2)


def second_all(m1, aux, vel, table, init, init_hbm, sems):
    copies = []
    for x in range(8):
        at = slice(x * 8, x * 8 + 8)
        b = row_b(m1, table, SECOND, x + 2, 0)
        extra = [vel[i, at, :] for i in range(3)] + [aux[i * WIDE + x + 2, pl.ds(4, 8), :] for i in (3, 4)]
        result, _ = transpose_collision(b, *factors(extra))
        for k in range(19):
            init[k, x] = result[k]
        copies.append(pltpu.make_async_copy(init.at[:, x], init_hbm.at[:, x], sems.at[x]))
        copies[-1].start()
    for copy in copies:
        copy.wait()


def final_kernel(m1, aux, vel, table, over, sums, init_in, init_hbm, descent, norms, init, sems, *, cell_count):
    @pl.when(jnp.logical_not(early()))
    def _():
        second_all(m1, aux, vel, table.reshape(TALL, TALL, 128), init, init_hbm, sems)

    total = jnp.sum(sums[...], axis=0)
    below = lanes_of(total.shape) < 64
    squares = [jnp.sum(jnp.where(below == first, total, 0.0), axis=1, keepdims=True) for first in (True, False)]
    norm = [jnp.sqrt(square / cell_count + 1e-06) for square in squares]
    descent[...] = over[...] / norm[1]
    norms[0] = jnp.sum(norm[0])
    norms[1] = jnp.sum(norm[1])


VMEM = pl.BlockSpec(memory_space=pltpu.VMEM)
SMEM = pl.BlockSpec(memory_space=pltpu.SMEM)
HBM = pl.BlockSpec(memory_space=pltpu.HBM)


def call(kernel, outs, scratch=(), ins=None, places=None, aliases=None, **names):
    def run(*arrays):
        return pl.pallas_call(
            functools.partial(kernel, **names),
            out_shape=[jax.ShapeDtypeStruct(shape, jnp.float32) for shape in outs],
            in_specs=ins or [VMEM] * len(arrays),
            out_specs=places or [VMEM] * len(outs),
            scratch_shapes=[pltpu.VMEM(v, jnp.float32) if isinstance(v, tuple) else v for v in scratch],
            input_output_aliases=aliases or {},
            compiler_params=pltpu.CompilerParams(vmem_limit_bytes=32 << 20),
            name=kernel.__name__,
        )(*arrays)

    return run


def in_hbm(array):
    return pltpu.with_memory_space_constraint(array, pltpu.HBM)


def swaps(axis):
    count = lax.axis_size(axis)
    ahead = [(i, (i + 1) % count if i % 2 == 0 else i - 1) for i in range(count)]
    behind = [(i, (i - 1) % count if i % 2 == 0 else (i + 1) % count) for i in range(count)]
    return ahead, behind


def both(one, two, axis):
    if axis in RINGS:
        count = lax.axis_size(axis)
        up = lax.ppermute(one, axis, [(i, (i + 1) % count) for i in range(count)])
        return lax.ppermute(two, axis, [((i + 1) % count, i) for i in range(count)]), up
    ahead, behind = swaps(axis)
    second = lax.ppermute(two, axis, behind)
    return lax.ppermute(one, axis, ahead), second


def two_sides(message):
    if lax.axis_size("gx") == 2:
        return lax.ppermute(message, "gx", [(0, 1), (1, 0)])
    return jnp.stack(both(message[0], message[1], "gx"))


def shards(final_adjoint, stored_states, porosity, solid_labels, boundary_mask):
    nx = lax.axis_size("gx")
    devices = nx * lax.axis_size("gy") * lax.axis_size("gz")
    cells = porosity.size
    layout = final_adjoint.shape
    block = layout[1:]
    zb, za, cen, values, dense = call(
        pack_kernel,
        [(32, 128), (32, 128), (16, 128), (FACE, 64, 128), (64, 128)],
        [
            layout,
            layout,
            block,
            pltpu.VMEM(block, jnp.int32),
            pltpu.VMEM(block, jnp.int32),
            (8, TALL, 128),
            (128, 128),
            (2, 32, 128),
            pltpu.SemaphoreType.DMA((4, 5)),
        ],
        [HBM] * 5,
    )(*(in_hbm(v) for v in (final_adjoint, stored_states, porosity, solid_labels, boundary_mask)))
    za, ya, yb, xm = call(
        face_kernel, [(32, 128), (YROWS, 128), (YROWS, 128), (2, XROWS, 128)], nx=nx
    )(za, cen, values)
    za, zb = both(za, zb, "gz")
    ya, yb = both(ya, yb, "gy")
    xm = two_sides(xm)
    mine = jnp.concatenate([zb, za], axis=0)
    ga, gb = both(mine, mine, "gy")
    full, edges = call(edge_kernel, [(16, 128), (2, EDGES, 128)], nx=nx)(ya, yb, cen)
    edges = two_sides(edges)
    tail, packed = call(relay_kernel, [(80, 128), (40, 128)])(mine, ga, gb, full)
    if nx == 2:
        far = lax.ppermute(packed, "gx", [(0, 1), (1, 0)])[None]
    else:
        far = jnp.stack(both(packed, packed, "gx"))
    tall, short = (19 * WIDE, TALL, 128), (6 * WIDE, TALL, 128)
    state = [tall, short, tall, (WIDE, 8, 128), (64, 128)]
    m0, aux, m1, rho, over, velocity, dense_zero, partial = call(
        inner_kernel,
        [*state, (3, 64, 128), (64, 128), (2, 8, 128)],
        [(128, 128), (PLANE, 128), layout, pltpu.SemaphoreType.DMA],
        [VMEM] * 2 + [HBM] + [VMEM] * 3,
    )(values, dense, in_hbm(stored_states), ya, yb, tail)
    m0, aux, m1, rho, over, table, sums, init = call(
        outer_kernel,
        [*state, (256, 128), (devices, 1, 128), layout],
        [(128, 256), layout, pltpu.SemaphoreType.DMA((8,))],
        places=[VMEM] * 7 + [HBM],
        aliases={i: i for i in range(5)},
        nx=nx,
    )(m0, aux, m1, rho, over, velocity, dense_zero, partial, tail, xm, far, edges)
    sums = lax.all_to_all(sums, AXES, 0, 0, tiled=True)
    init, descent, norms = call(
        final_kernel,
        [layout, (64, 128), (2,)],
        [layout, pltpu.SemaphoreType.DMA((8,))],
        [VMEM] * 6 + [HBM],
        [HBM, VMEM, SMEM],
        {6: 0},
        cell_count=cells * devices,
    )(m1, aux, velocity, table, over, sums, init)
    return init, descent.reshape(block), norms


def solution(mesh):
    in_specs = (
        P(None, "gx", "gy", "gz"),
        P(None, None, "gx", "gy", "gz"),
        P("gx", "gy", "gz"),
        P("gx", "gy", "gz"),
        P("gx", "gy", "gz"),
    )
    out_specs = (P(None, "gx", "gy", "gz"), P("gx", "gy", "gz"), P())
    return jax.shard_map(shards, mesh=mesh, in_specs=in_specs, out_specs=out_specs, check_vma=False)
```

```python
import functools

import jax
import jax.numpy as jnp
from jax import lax
from jax.experimental import pallas as pl
from jax.experimental.pallas import tpu as pltpu
from jax.sharding import PartitionSpec as P

lattice = (
    (0, 0, 0),
    (1, 0, 0),
    (-1, 0, 0),
    (0, 1, 0),
    (0, -1, 0),
    (0, 0, 1),
    (0, 0, -1),
    (1, 1, 0),
    (-1, -1, 0),
    (1, -1, 0),
    (-1, 1, 0),
    (1, 0, 1),
    (-1, 0, -1),
    (1, 0, -1),
    (-1, 0, 1),
    (0, 1, 1),
    (0, -1, -1),
    (0, 1, -1),
    (0, -1, 1),
)
opposite = (0, 2, 1, 4, 3, 6, 5, 8, 7, 10, 9, 12, 11, 14, 13, 16, 15, 18, 17)
AXES = ("gx", "gy", "gz")
RINGS = ("gz",)
PLANES = ((0, 1, 7), (0, 2, 11), (1, 2, 15))


def flow(stored, porosity):
    density = sum(stored[1:], stored[0])
    momentum = []
    for axis in range(3):
        total = None
        for vector, value in zip(lattice, stored):
            if vector[axis]:
                if total is None:
                    total = value if vector[axis] > 0 else -value
                else:
                    total = total + value if vector[axis] > 0 else total - value
        momentum.append(total)
    damping = 0.5 * (1.0 - porosity)
    beta = 1.0 / (1.0 + 0.5 * damping)
    scale = beta / density
    return density, [value * scale for value in momentum], beta, damping * beta


def transpose_collision(b, velocity, beta, alpha, solid, density=None):
    base = b[0]
    first, second = [], []
    for axis in range(3):
        ahead, behind = b[2 * axis + 1], b[2 * axis + 2]
        first.append(0.5 * (ahead - behind))
        second.append(0.5 * (ahead + behind) - base)
    odd = [None, None, None]
    tee = [None, None, None]
    ring = [None, None, None]
    evens, crosses, parts = [], [], []

    def join(where, axis, value):
        where[axis] = value if where[axis] is None else where[axis] + value

    for one, two, at in PLANES:
        pp, mm, pm, mp = b[at], b[at + 1], b[at + 2], b[at + 3]
        s1, s2, d1, d2 = pp + mm, pm + mp, pp - mm, pm - mp
        both = second[one] + second[two]
        fourth = 0.25 * (s1 + s2) - base - both
        along_one, along_two = 0.25 * (d1 + d2), 0.25 * (d1 - d2)
        even = 1.2 * both + 1.6 * fourth
        cross = 0.3 * (s1 - s2)
        q_one, q_two = 1.4 * (along_one - first[one]), 1.4 * (along_two - first[two])
        join(odd, one, q_one)
        join(odd, two, q_two)
        join(tee, one, along_one)
        join(tee, two, along_two)
        join(ring, one, even)
        join(ring, two, even)
        evens.append(even)
        crosses.append(cross)
        parts.append((q_one, q_two))
    ninth = 1.0 / 9.0
    axial = 2.4 / 18.0
    s0 = axial * (second[0] + second[1] + second[2]) + ninth * (evens[0] + evens[1] + evens[2])
    sone = [ninth * odd[axis] for axis in range(3)]
    stwo = [axial * second[axis] + ninth * ring[axis] for axis in range(3)]
    sxy, sxz, syz = (ninth * value for value in crosses)
    tees = [ninth * (first[axis] + tee[axis]) for axis in range(3)]
    ux, uy, uz = velocity
    wx = stwo[0] * ux + sxy * uy + sxz * uz
    wy = sxy * ux + stwo[1] * uy + syz * uz
    wz = sxz * ux + syz * uy + stwo[2] * uz
    quad = ux * wx + uy * wy + uz * wz
    speed = ux * ux + uy * uy + uz * uz
    scalar = s0 * (1.0 + 1.5 * speed) - 4.5 * quad
    slope = [
        beta * (3.0 * one + 9.0 * two - 3.0 * s0 * three) - 3.0 * alpha * tau
        for one, two, three, tau in zip(sone, (wx, wy, wz), velocity, tees)
    ]
    out = [base + scalar]
    for axis in range(3):
        even = scalar - 1.2 * second[axis]
        out.append(b[2 * axis + 1] + (even + slope[axis]))
        out.append(b[2 * axis + 2] + (even - slope[axis]))
    for (one, two, at), even, cross, (q_one, q_two) in zip(PLANES, evens, crosses, parts):
        same, other = scalar - even - cross, scalar - even + cross
        a_one, a_two = slope[one] - q_one, slope[two] - q_two
        plus, minus = a_one + a_two, a_one - a_two
        out.append(b[at] + (same + plus))
        out.append(b[at + 1] + (same - plus))
        out.append(b[at + 2] + (other + minus))
        out.append(b[at + 3] + (other - minus))
    out = [jnp.where(solid, b[opposite[i]], out[i]) for i in range(19)]
    if density is None:
        return out, None
    gradient = (beta * density) * (
        0.75 * (sone[0] * ux + sone[1] * uy + sone[2] * uz)
        + 2.25 * quad
        - 0.75 * s0 * speed
        + 1.5 * (tees[0] * ux + tees[1] * uy + tees[2] * uz)
    )
    return out, jnp.where(solid, 0.0, gradient)


def face_rows(axis, side):
    near = [(k, 1) for k in range(19) if lattice[k][axis] * side >= 0]
    far = [(k, 2) for k in range(19) if lattice[k][axis] * side > 0]
    return near + far


def edge_rows(side_x, side_y):
    rows = []
    for k in range(19):
        across, along = lattice[k][0] * side_x, lattice[k][1] * side_y
        for layer_x in (1, 2):
            for layer_y in (1, 2):
                fits = across >= layer_x - 1 and along >= layer_y - 1
                if fits:
                    rows.append((k, layer_x, layer_y))
    return rows


NEAR = 19
FACE = 25
UP = [k for k in range(19) if lattice[k][2] > 0]
DOWN = [k for k in range(19) if lattice[k][2] < 0]
TALL = 16
WIDE = 12
PLANE = TALL * WIDE
SIDES = (1, -1)
PLACE = {(axis, side): {row: i for i, row in enumerate(face_rows(axis, side))} for axis in range(2) for side in SIDES}
FLAT = [k for k in range(19) if lattice[k][2] == 0]
COEF = len(FLAT)
CROSS = COEF + 6
for side, pops in zip(SIDES, (UP, DOWN)):
    PLACE[2, side] = {(k, 1): i for i, k in enumerate(FLAT)}
    for i, k in enumerate(pops):
        for layer in (1, 2):
            PLACE[2, side][k, layer] = CROSS + 2 * i + (layer - 1 if side > 0 else 2 - layer)
YROWS = FACE * 8 + 16
XROWS = FACE * 8
EDGES = 52


def lanes_of(shape):
    return lax.broadcasted_iota(jnp.int32, shape, len(shape) - 1)


def turn(value, shift):
    count = value.shape[-1]
    shift = shift % count
    return pltpu.roll(value, shift, value.ndim - 1) if shift else value


def pick(flag, one, two):
    if isinstance(flag, bool):
        return one if flag else two
    return jnp.where(flag, one, two)


def even_of(axis):
    return True if axis in RINGS else lax.axis_index(axis) % 2 == 0


def weave_y(own, high, low):
    place = lanes_of(own.shape) % TALL
    return jnp.where(place < 4, turn(low, -8), jnp.where(place < 12, own, turn(high, 8)))


def fold(one, two):
    lane = lanes_of(one.shape)
    return jnp.where((lane < 32) | (lane >= 96), one, turn(two, 64))


def unfold(value):
    return jnp.concatenate([value, turn(value, 64)], axis=0)


def weave_x(own, high, low):
    lane = lanes_of(own.shape)
    own = turn(own, 32)
    return jnp.where(lane < 32, turn(low, 32), own), jnp.where(lane < 32, own, turn(high, 32))


def pack_kernel(adj_hbm, st_hbm, por_hbm, sol_hbm, msk_hbm, zb, za, cen, cells, rho, adj, st, por, sol, msk, cols, table, halves, sems):
    copies = []
    spans = ((0, 4), (4, 4))
    for part, (first, count) in enumerate(spans):
        at = pl.ds(first, count)
        group = [
            (adj_hbm.at[:, at], adj.at[:, at]),
            (st_hbm.at[1, :, at], st.at[:, at]),
            (por_hbm.at[at], por.at[at]),
            (sol_hbm.at[at], sol.at[at]),
            (msk_hbm.at[at], msk.at[at]),
        ]
        copies.append([pltpu.make_async_copy(s, d, sems.at[part, i]) for i, (s, d) in enumerate(group)])
    for group in copies:
        for copy in group:
            copy.start()
    lane = lanes_of((8, 128))
    cols[...] = jnp.zeros_like(cols)

    def step(x, carry):
        at = pl.ds(pl.multiple_of(x * 8, 8), 8)
        free = 1.0 - msk[x].astype(jnp.float32)
        dense, velocity, _, _ = flow([st[k, x] for k in range(19)], por[x])
        rho[at, :] = dense
        tiles = [adj[k, x] * free for k in range(19)]
        tiles += [*velocity, por[x], sol[x].astype(jnp.float32), free]
        for k in range(FACE):
            cells[k, at, :] = tiles[k]
        spread = jnp.zeros((8, 128), jnp.float32)
        for i, k in enumerate([*FLAT, *range(NEAR, FACE), *UP, *DOWN]):
            rise = lattice[k][2] if k < NEAR else 0
            spread = jnp.where(lane // 2 == i, turn(tiles[k], 2 * i + (1, 0, 2)[rise]), spread)
        cols[x, pl.ds(4, 8), :] = spread
        return carry

    for part, group in enumerate(copies):
        for copy in group:
            copy.wait()
        lax.fori_loop(spans[part][0], sum(spans[part]), step, 0, unroll=True)
    table[...] = jnp.transpose(cols[...].reshape(128, 128))
    for half in range(2):
        halves[half, 0:16, :] = table[pl.ds(1 - half, 16, stride=2), :]
        at = 2 * CROSS + 10 * half
        halves[half, CROSS : CROSS + 10, :] = table[at : at + 10, :]
        halves[half, CROSS + 10 :, :] = jnp.zeros((32 - CROSS - 10, 128), jnp.float32)
    low, high = halves[0], halves[1]
    even = even_of("gz")
    za[...] = pick(even, high, low)
    zb[...] = pick(even, low, high)
    cen[...] = jnp.zeros_like(cen)
    for half in range(2):
        at = 2 * CROSS + 10 * half + half
        cen[8 - 8 * half : 13 - 8 * half, :] = table[pl.ds(at, 5, stride=2), :]


def face_kernel(za, cen, cells, za_out, ya, yb, xm, *, nx):
    za_out[...] = za[...]
    even = even_of("gy")
    for i in range(FACE):
        pair = []
        for side in SIDES:
            k, layer = (face_rows(1, side) + [(NEAR + j, 1) for j in range(6)])[i]
            y = layer - 1 if side > 0 else 8 - layer
            pair.append(cells[k, pl.ds(y, 8, stride=8), :])
        low, high = pair
        ya[i * 8 : i * 8 + 8, :] = pick(even, high, low)
        yb[i * 8 : i * 8 + 8, :] = pick(even, low, high)
    ya[FACE * 8 :, :] = cen[...]
    yb[FACE * 8 :, :] = cen[...]
    even = even_of("gx")
    for i in range(FACE):
        pair = []
        for side in SIDES:
            k, layer = (face_rows(0, side) + [(NEAR + j, 1) for j in range(6)])[i]
            x = layer - 1 if side > 0 else 8 - layer
            pair.append(cells[k, x * 8 : x * 8 + 8, :])
        low, high = pair
        if nx > 2:
            low, high = pick(even, high, low), pick(even, low, high)
        xm[0, i * 8 : i * 8 + 8, :] = low
        xm[1, i * 8 : i * 8 + 8, :] = high


def relay_kernel(mine, ga, gb, full, tail, packed):
    even = even_of("gy")
    a, b = ga[...], gb[...]
    tail[0:16, :] = full[...]
    woven = weave_y(mine[...], pick(even, a, b), pick(even, b, a))
    tail[16:, :] = woven
    packed[0:8, :] = fold(full[0:8, :], full[8:16, :])
    packed[8:, :] = fold(woven[:32], woven[32:])


def edge_kernel(ya, yb, cen, full, edges, *, nx):
    even = even_of("gy")
    at = slice(FACE * 8, FACE * 8 + 16)
    a, b = ya[at, :], yb[at, :]
    full[...] = weave_y(cen[...], pick(even, a, b), pick(even, b, a))
    even_x = even_of("gx")
    for i in range(NEAR + 6):
        for where, side_y in ((0, 1), (FACE, -1)):
            pair = []
            for side_x in SIDES:
                rows = edge_rows(side_x, side_y) + [(NEAR + j, 1, 1) for j in range(6)]
                k, layer_x, layer_y = rows[i]
                row = PLACE[1, side_y][k, layer_y] if k < NEAR else k
                x = layer_x - 1 if side_x > 0 else 8 - layer_x
                row = row * 8 + x
                a, b = ya[row : row + 1, :], yb[row : row + 1, :]
                pair.append(pick(even, a, b) if side_y > 0 else pick(even, b, a))
            one, two = pair
            if nx > 2:
                one, two = pick(even_x, two, one), pick(even_x, one, two)
            edges[0, where + i : where + i + 1, :] = one
            edges[1, where + i : where + i + 1, :] = two
    for slot in range(2):
        edges[slot, 2 * FACE :, :] = jnp.zeros((EDGES - 2 * FACE, 128), jnp.float32)


def factors(extra):
    damping = 0.5 * (1.0 - extra[3])
    beta = 1.0 / (1.0 + 0.5 * damping)
    return extra[:3], beta, damping * beta, extra[4] > 0.0


FIRST = {k: PLACE[2, 1][k, 1] for k in UP}
FIRST.update({k: 32 + PLACE[2, -1][k, 1] for k in DOWN})
SECOND = {k: 64 + i for i, k in enumerate(UP)}
SECOND.update({k: 72 + i for i, k in enumerate(DOWN)})


def shifted(value, ghost, k, column):
    lane = lanes_of(value.shape)
    if lattice[k][2] > 0:
        return jnp.where(lane == 127, turn(ghost, 127 - column), turn(value, -1))
    return jnp.where(lane == 0, turn(ghost, -column), turn(value, 1))


def row_b(ref, table, columns, x, skip):
    out = []
    for k in range(19):
        cx, cy, cz = lattice[k]
        value = ref[k * WIDE + x + cx, pl.ds(4 + cy, 8), :]
        if cz:
            value = shifted(value, table[x + cx - skip, pl.ds(4 + cy, 8), :], k, columns[k])
        out.append(value)
    return out


def first_row(m0, aux, m1, rho, table, x, skip, wanted=range(19)):
    extra = [aux[i * WIDE + x, pl.ds(4, 8), :] for i in range(6)]
    result, gradient = transpose_collision(row_b(m0, table, FIRST, x, skip), *factors(extra), rho[x, :, :])
    for k in wanted:
        m1[k * WIDE + x, pl.ds(4, 8), :] = result[k] * extra[5]
    if len(wanted) == 19:
        rho[x, :, :] = gradient


def caps(ghosts, center):
    b = []
    for k in range(19):
        cx, cy, cz = lattice[k]
        pair = []
        for half, side in enumerate(SIDES):
            if cz * side < 0:
                row = half * 8 + (DOWN if side > 0 else UP).index(k)
                pair.append(center[row : row + 1])
            else:
                row = half * 32 + PLACE[2, side][k, 2 if cz else 1]
                pair.append(ghosts[row : row + 1, :])
        b.append(turn(jnp.concatenate(pair, axis=0), -(TALL * cx + cy)))
    extra = [
        jnp.concatenate([ghosts[at + COEF + i : at + COEF + i + 1, :] for at in (0, 32)], axis=0) for i in range(6)
    ]
    result, _ = transpose_collision(b, *factors(extra))
    for half, side in enumerate(SIDES):
        for i, k in enumerate(UP if side > 0 else DOWN):
            row = 64 + half * 8 + i
            ghosts[row : row + 1, :] = (result[k] * extra[5])[half : half + 1]


def first_side(flat0, flat1, flat_aux, table, y, x0, skip):
    b = []
    for k in range(19):
        cx, cy, cz = lattice[k]
        start = (x0 + cx) * TALL + y + cy
        value = flat0[pl.ds(k * PLANE + start, 8, stride=TALL), :]
        if cz:
            value = shifted(value, table[pl.ds(start - skip * TALL, 8, stride=TALL), :], k, FIRST[k])
        b.append(value)
    start = x0 * TALL + y
    extra = [flat_aux[pl.ds(i * PLANE + start, 8, stride=TALL), :] for i in range(6)]
    result, _ = transpose_collision(b, *factors(extra))
    for k in range(19):
        if lattice[k][1] == (1 if y == 12 else -1):
            flat1[pl.ds(k * PLANE + start, 8, stride=TALL), :] = result[k] * extra[5]


def second_row(m1, aux, vel, dense, table, rho, over, x, skip):
    at = slice((x - 2) * 8, (x - 1) * 8)
    b = row_b(m1, table, SECOND, x, skip)
    extra = [vel[i, at, :] for i in range(3)] + [aux[i * WIDE + x, pl.ds(4, 8), :] for i in (3, 4)]
    _, gradient = transpose_collision(b, *factors(extra), dense[at, :])
    over[at, :] = rho[x, :, :] + gradient


def inner_kernel(cells, dense, st_hbm, ya, yb, tail, m0, aux, m1, rho, over, vel, dense_zero, partial, ghosts, table, st, sem):
    fetch = pltpu.make_async_copy(st_hbm.at[0], st, sem)
    fetch.start()
    even_y, even_z = even_of("gy"), even_of("gz")
    rho[...] = jnp.zeros_like(rho)

    def fill(x, carry):
        at = pl.ds(pl.multiple_of(x * 8, 8), 8)
        for k in range(19):
            m0[k * WIDE + x + 2, pl.ds(4, 8), :] = cells[k, at, :]
        for i in range(6):
            aux[i * WIDE + x + 2, pl.ds(4, 8), :] = cells[NEAR + i, at, :]
        rho[x + 2, :, :] = dense[at, :]
        return carry

    lax.fori_loop(0, 8, fill, 0, unroll=True)
    flat0, flat_aux = (ref.reshape(ref.shape[0] * TALL, 128) for ref in (m0, aux))
    a, b = ya[...], yb[...]
    for side, tiles in ((1, pick(even_y, a, b)), (-1, pick(even_y, b, a))):
        for i, (k, layer) in enumerate(face_rows(1, side)):
            y = 11 + layer if side > 0 else 4 - layer
            flat0[pl.ds(k * PLANE + 2 * TALL + y, 8, stride=TALL), :] = tiles[i * 8 : i * 8 + 8]
        for i in range(6):
            at = (NEAR + i) * 8
            y = 12 if side > 0 else 3
            flat_aux[pl.ds(i * PLANE + 2 * TALL + y, 8, stride=TALL), :] = tiles[at : at + 8]
    b, a = tail[16:48, :], tail[48:80, :]
    ghosts[0:32, :] = pick(even_z, a, b)
    ghosts[32:64, :] = pick(even_z, b, a)
    ghosts[64:128, :] = jnp.zeros((64, 128), jnp.float32)
    caps(ghosts, tail[0:16, :])
    table[0:128, :] = jnp.transpose(ghosts[...])
    table[128:, :] = jnp.zeros((64, 128), jnp.float32)
    table3 = table.reshape(WIDE, TALL, 128)

    def first(x, carry):
        first_row(m0, aux, m1, rho, table3, x, 2)
        return carry

    lax.fori_loop(3, 9, first, 0, unroll=True)
    fetch.wait()

    def states(x, carry):
        at = pl.ds(pl.multiple_of(x * 8, 8), 8)
        value, velocity, _, _ = flow([st[k, x] for k in range(19)], cells[NEAR + 3, at, :])
        dense_zero[at, :] = value
        for i in range(3):
            vel[i, at, :] = velocity[i]
        return carry

    lax.fori_loop(0, 8, states, 0, unroll=True)
    flat1 = m1.reshape(19 * PLANE, 128)
    for y in (3, 12):
        first_side(flat0, flat1, flat_aux, table, y, 3, 2)
    for x in range(4, 8):
        second_row(m1, aux, vel, dense_zero, table3, rho, over, x, 2)
    one = two = jnp.zeros((8, 128), jnp.float32)
    for x in range(4, 8):
        before, total = rho[x, :, :], over[x * 8 - 16 : x * 8 - 8, :]
        one, two = one + before * before, two + total * total
    partial[0, :, :] = one
    partial[1, :, :] = two


def outer_kernel(m0_in, aux_in, m1_in, rho_in, over_in, vel, dense, partial, tail, xm, far, edges, m0, aux, m1, rho, over, table, sums, init_hbm, ghosts, init, sems, *, nx):
    even_z = even_of("gz")
    flat0, flat1, flat_aux = (ref.reshape(ref.shape[0] * TALL, 128) for ref in (m0, m1, aux))
    even_x = even_of("gx")
    a, b = xm[0], xm[1]
    if nx > 2:
        even = even_of("gx")
        a, b = pick(even, a, b), pick(even, b, a)
    for side, tiles in zip(SIDES, (a, b)):
        for i, (k, layer) in enumerate(face_rows(0, side)):
            x = 9 + layer if side > 0 else 2 - layer
            m0[k * WIDE + x, pl.ds(4, 8), :] = tiles[i * 8 : i * 8 + 8]
        for i in range(6):
            at = (NEAR + i) * 8
            aux[i * WIDE + (10 if side > 0 else 1), pl.ds(4, 8), :] = tiles[at : at + 8]

    def along_x(ref, at):
        a, b = ref[0, at, :], ref[min(1, ref.shape[0] - 1), at, :]
        if nx == 2:
            return a, b
        return pick(even_x, a, b), pick(even_x, b, a)

    for where, side_y in ((0, 1), (FACE, -1)):
        for i in range(NEAR + 6):
            pair = along_x(edges, slice(where + i, where + i + 1))
            for side_x, line in zip(SIDES, pair):
                x, y = (10 if side_x > 0 else 1), (12 if side_y > 0 else 3)
                if i >= NEAR:
                    aux[(i - NEAR) * WIDE + x, y : y + 1, :] = line
                else:
                    k, layer_x, layer_y = edge_rows(side_x, side_y)[i]
                    x += side_x * (layer_x - 1)
                    y += side_y * (layer_y - 1)
                    m0[k * WIDE + x, y : y + 1, :] = line
    for tile, value in enumerate(weave_x(tail[16:, :], *map(unfold, along_x(far, slice(8, 40))))):
        b, a = value[0:32], value[32:64]
        ghosts[0:32, tile * 128 : tile * 128 + 128] = pick(even_z, a, b)
        ghosts[32:64, tile * 128 : tile * 128 + 128] = pick(even_z, b, a)
    center = jnp.concatenate(weave_x(tail[0:16, :], *map(unfold, along_x(far, slice(0, 8)))), axis=1)
    ghosts[64:128, :] = jnp.zeros((64, 256), jnp.float32)
    caps(ghosts, center)
    for tile in range(2):
        at = slice(tile * 128, tile * 128 + 128)
        table[at, :] = jnp.transpose(ghosts[:, at])
    table3 = table.reshape(TALL, TALL, 128)

    for x, inward in ((1, -1), (2, 0), (9, 0), (10, 1)):
        wanted = [k for k in range(19) if not inward or lattice[k][0] == inward]
        first_row(m0, aux, m1, rho, table3, x, 0, wanted)
    for y in (3, 12):
        for x0 in (1, 3):
            first_side(flat0, flat1, flat_aux, table, y, x0, 0)
    for x in (2, 3, 8, 9):
        second_row(m1, aux, vel, dense, table3, rho, over, x, 0)
    one, two = partial[0, :, :], partial[1, :, :]
    for x in (0, 1, 6, 7):
        before, total = rho[x + 2, :, :], over[x * 8 : x * 8 + 8, :]
        one, two = one + before * before, two + total * total
    one, two = jnp.sum(one, axis=0, keepdims=True), jnp.sum(two, axis=0, keepdims=True)
    devices = sums.shape[0]
    both_sums = jnp.where(lanes_of(one.shape) < 64, one + turn(one, 64), two + turn(two, 64))
    sums[...] = jnp.broadcast_to(both_sums[None], (devices, 1, 128))

    @pl.when(early())
    def _():
        second_all(m1, aux, vel, table3, init, init_hbm, sems)


def early():
    return lax.axis_index("gz") == 0


def second_all(m1, aux, vel, table, init, init_hbm, sems):
    copies = []
    for x in range(8):
        at = slice(x * 8, x * 8 + 8)
        b = row_b(m1, table, SECOND, x + 2, 0)
        extra = [vel[i, at, :] for i in range(3)] + [aux[i * WIDE + x + 2, pl.ds(4, 8), :] for i in (3, 4)]
        result, _ = transpose_collision(b, *factors(extra))
        for k in range(19):
            init[k, x] = result[k]
        copies.append(pltpu.make_async_copy(init.at[:, x], init_hbm.at[:, x], sems.at[x]))
        copies[-1].start()
    for copy in copies:
        copy.wait()


def final_kernel(m1, aux, vel, table, over, sums, init_in, init_hbm, descent, norms, init, sems, *, cell_count):
    @pl.when(jnp.logical_not(early()))
    def _():
        second_all(m1, aux, vel, table.reshape(TALL, TALL, 128), init, init_hbm, sems)

    total = jnp.sum(sums[...], axis=0)
    below = lanes_of(total.shape) < 64
    squares = [jnp.sum(jnp.where(below == first, total, 0.0), axis=1, keepdims=True) for first in (True, False)]
    norm = [jnp.sqrt(square / cell_count + 1e-06) for square in squares]
    descent[...] = over[...] / norm[1]
    norms[0] = jnp.sum(norm[0])
    norms[1] = jnp.sum(norm[1])


VMEM = pl.BlockSpec(memory_space=pltpu.VMEM)
SMEM = pl.BlockSpec(memory_space=pltpu.SMEM)
HBM = pl.BlockSpec(memory_space=pltpu.HBM)


def call(kernel, outs, scratch=(), ins=None, places=None, aliases=None, **names):
    def run(*arrays):
        return pl.pallas_call(
            functools.partial(kernel, **names),
            out_shape=[jax.ShapeDtypeStruct(shape, jnp.float32) for shape in outs],
            in_specs=ins or [VMEM] * len(arrays),
            out_specs=places or [VMEM] * len(outs),
            scratch_shapes=[pltpu.VMEM(v, jnp.float32) if isinstance(v, tuple) else v for v in scratch],
            input_output_aliases=aliases or {},
            compiler_params=pltpu.CompilerParams(vmem_limit_bytes=32 << 20),
            name=kernel.__name__,
        )(*arrays)

    return run


def in_hbm(array):
    return pltpu.with_memory_space_constraint(array, pltpu.HBM)


def swaps(axis):
    count = lax.axis_size(axis)
    ahead = [(i, (i + 1) % count if i % 2 == 0 else i - 1) for i in range(count)]
    behind = [(i, (i - 1) % count if i % 2 == 0 else (i + 1) % count) for i in range(count)]
    return ahead, behind


def both(one, two, axis):
    if axis in RINGS:
        count = lax.axis_size(axis)
        up = lax.ppermute(one, axis, [(i, (i + 1) % count) for i in range(count)])
        return lax.ppermute(two, axis, [((i + 1) % count, i) for i in range(count)]), up
    ahead, behind = swaps(axis)
    second = lax.ppermute(two, axis, behind)
    return lax.ppermute(one, axis, ahead), second


def two_sides(message):
    if lax.axis_size("gx") == 2:
        return lax.ppermute(message, "gx", [(0, 1), (1, 0)])
    return jnp.stack(both(message[0], message[1], "gx"))


def shards(final_adjoint, stored_states, porosity, solid_labels, boundary_mask):
    nx = lax.axis_size("gx")
    devices = nx * lax.axis_size("gy") * lax.axis_size("gz")
    cells = porosity.size
    layout = final_adjoint.shape
    block = layout[1:]
    zb, za, cen, values, dense = call(
        pack_kernel,
        [(32, 128), (32, 128), (16, 128), (FACE, 64, 128), (64, 128)],
        [
            layout,
            layout,
            block,
            pltpu.VMEM(block, jnp.int32),
            pltpu.VMEM(block, jnp.int32),
            (8, TALL, 128),
            (128, 128),
            (2, 32, 128),
            pltpu.SemaphoreType.DMA((4, 5)),
        ],
        [HBM] * 5,
    )(*(in_hbm(v) for v in (final_adjoint, stored_states, porosity, solid_labels, boundary_mask)))
    za, ya, yb, xm = call(
        face_kernel, [(32, 128), (YROWS, 128), (YROWS, 128), (2, XROWS, 128)], nx=nx
    )(za, cen, values)
    za, zb = both(za, zb, "gz")
    ya, yb = both(ya, yb, "gy")
    xm = two_sides(xm)
    mine = jnp.concatenate([zb, za], axis=0)
    ga, gb = both(mine, mine, "gy")
    full, edges = call(edge_kernel, [(16, 128), (2, EDGES, 128)], nx=nx)(ya, yb, cen)
    edges = two_sides(edges)
    tail, packed = call(relay_kernel, [(80, 128), (40, 128)])(mine, ga, gb, full)
    if nx == 2:
        far = lax.ppermute(packed, "gx", [(0, 1), (1, 0)])[None]
    else:
        far = jnp.stack(both(packed, packed, "gx"))
    tall, short = (19 * WIDE, TALL, 128), (6 * WIDE, TALL, 128)
    state = [tall, short, tall, (WIDE, 8, 128), (64, 128)]
    m0, aux, m1, rho, over, velocity, dense_zero, partial = call(
        inner_kernel,
        [*state, (3, 64, 128), (64, 128), (2, 8, 128)],
        [(128, 128), (PLANE, 128), layout, pltpu.SemaphoreType.DMA],
        [VMEM] * 2 + [HBM] + [VMEM] * 3,
    )(values, dense, in_hbm(stored_states), ya, yb, tail)
    m0, aux, m1, rho, over, table, sums, init = call(
        outer_kernel,
        [*state, (256, 128), (devices, 1, 128), layout],
        [(128, 256), layout, pltpu.SemaphoreType.DMA((8,))],
        places=[VMEM] * 7 + [HBM],
        aliases={i: i for i in range(5)},
        nx=nx,
    )(m0, aux, m1, rho, over, velocity, dense_zero, partial, tail, xm, far, edges)
    sums = lax.all_to_all(sums, AXES, 0, 0, tiled=True)
    init, descent, norms = call(
        final_kernel,
        [layout, (64, 128), (2,)],
        [layout, pltpu.SemaphoreType.DMA((8,))],
        [VMEM] * 6 + [HBM],
        [HBM, VMEM, SMEM],
        {6: 0},
        cell_count=cells * devices,
    )(m1, aux, velocity, table, over, sums, init)
    return init, descent.reshape(block), norms


def solution(mesh):
    in_specs = (
        P(None, "gx", "gy", "gz"),
        P(None, None, "gx", "gy", "gz"),
        P("gx", "gy", "gz"),
        P("gx", "gy", "gz"),
        P("gx", "gy", "gz"),
    )
    out_specs = (P(None, "gx", "gy", "gz"), P("gx", "gy", "gz"), P())
    return jax.shard_map(shards, mesh=mesh, in_specs=in_specs, out_specs=out_specs, check_vma=False)
```
